32 devices in a mesh: wide: 16 (over z, y, core), narrow: 2 (over x).
Axes of the slice: x: 2, y: 2, z: 4, core: 2. Of those that a mesh axis runs over, the one named last changes fastest.
Arguments:
- tokens: bfloat16 [32, 1024, 1024], P('wide', 'narrow'), may hold values from -6 to 6
- doc_ids: int32 [32, 1024], P('wide'), may hold values from 0 to 3, as said below
- w_qkv: bfloat16 [1024, 3072], replicated, may hold values from -0.1875 to 0.1875
- w_out: bfloat16 [1024, 1024], replicated, may hold values from -0.1875 to 0.1875
- w_up: bfloat16 [1024, 4096], replicated, may hold values from -0.1875 to 0.1875
- w_down: bfloat16 [4096, 1024], replicated, may hold values from -0.09375 to 0.09375
- norm_gains: float32 [4, 1024], replicated, may hold values from 0.5 to 1.5
- norm_biases: float32 [4, 1024], replicated, may hold values from -2 to 2
- cotangent: bfloat16 [32, 1024, 1024], P('wide', 'narrow'), may hold values from -6 to 6
Outputs:
- layer_out: bfloat16 [32, 1024, 1024], P('wide', 'narrow')
- grad_tokens: bfloat16 [32, 1024, 1024], P('wide', 'narrow')
- grad_qkv: float32 [1024, 3072], P('narrow')
- grad_out_proj: float32 [1024, 1024], P('narrow')
- grad_up: float32 [1024, 4096], P('narrow')
- grad_down: float32 [4096, 1024], P('narrow')
- grad_gains: float32 [4, 1024], P(None, 'narrow')
- grad_biases: float32 [4, 1024], P(None, 'narrow')
The draws below stay inside these ranges and needn't reach their ends.
Inputs may be any that keep to these rules, and one draw needn't show every extreme that they name: `doc_ids`: each pack holds either one document of all 1024 positions (number 0 throughout) or four documents of 256 positions numbered 0 to 3 in order; exactly half of the packs are of each kind.
All inputs are finite; a program needn't handle non-finite values.
Results may differ from the reference program's by a relative error of at most 0.015.
Values may be sent and summed in bfloat16 or wider, within the bound.
No kernel may reach another device: no remote copies, remote signals or barrier semaphores. Data moves between devices by JAX's collectives and lax.ppermute only.
A program may use at most 384 MiB of HBM per device.

```python
import math
import jax
import jax.numpy as jnp
from jax import lax

D = 1024
FF = 4096
HEADS = 16
HEAD_DIM = 64
PACK = 1024
PACKS = 32
N_NARROW = 2


def draw_doc_ids(key, part):
    order = jax.random.permutation(key, PACKS)
    single = order < PACKS // 2
    places = jnp.arange(PACK, dtype=jnp.int32)
    quarter = (places // (PACK // 4)).astype(jnp.int32)
    return jnp.where(single[:, None], jnp.zeros((PACKS, PACK), jnp.int32), quarter[None, :]).astype(jnp.int32)


def steps_of(own_key, dims, cuts, smallest, largest):
    factor_of = 1.0
    for axis_at, blocks in cuts:
        heights = jax.random.uniform(jax.random.fold_in(jax.random.fold_in(own_key, 6), axis_at), (blocks,), jnp.float32, smallest / len(cuts), largest / len(cuts))
        factor_of = factor_of * jnp.repeat(jnp.exp(heights), dims[axis_at] // blocks).reshape((-1,) + (1,) * (len(dims) - 1 - axis_at))
    return factor_of


def gaussian(key, dims, deviation, reach, cuts=(), kind=jnp.bfloat16):
    drawn = jax.random.normal(key, dims, jnp.float32) * deviation
    if len(cuts) > 0:
        drawn = steps_of(key, dims, cuts, -0.22, 0.18) * drawn
    return jnp.clip(drawn, min=-reach, max=reach).astype(kind)


def setup_inputs(seed: int = 0) -> dict:
    arg_keys = jax.random.split(jax.random.key(seed), 10)
    return {
        "tokens": gaussian(arg_keys[0], (PACKS, PACK, D), 1.0, 6.0, ((0, 16), (1, 2))),
        "doc_ids": draw_doc_ids(jax.random.fold_in(arg_keys[9], 71), 0),
        "w_qkv": gaussian(arg_keys[2], (D, 3 * D), D ** -0.5, 0.1875),
        "w_out": gaussian(arg_keys[3], (D, D), D ** -0.5, 0.1875),
        "w_up": gaussian(arg_keys[4], (D, FF), D ** -0.5, 0.1875),
        "w_down": gaussian(arg_keys[5], (FF, D), FF ** -0.5, 0.09375),
        "norm_gains": jnp.clip(1.0 + 0.1 * jax.random.normal(arg_keys[6], (4, D), jnp.float32), 0.5, 1.5),
        "norm_biases": gaussian(arg_keys[7], (4, D), 0.3, 2.0, (), jnp.float32),
        "cotangent": gaussian(arg_keys[8], (PACKS, PACK, D), 1.0, 6.0, ((0, 16), (1, 2))),
    }


EPS = 1e-05

@jax.custom_vjp
def low(v):
    return lax.optimization_barrier(v.astype(jnp.bfloat16)).astype(jnp.float32)

@jax.custom_vjp
def low_back(v):
    return v

def low_keep(v):
    return (low(v), None)

def low_pass(kept, grad):
    return (grad,)

def back_keep(v):
    return (v, None)

def back_low(kept, grad):
    return (low(grad),)
low.defvjp(low_keep, low_pass)
low_back.defvjp(back_keep, back_low)

def layer_norm(values, gain_row, bias_row):
    centre = values - lax.optimization_barrier(jnp.mean(values, axis=-1, keepdims=True))
    spread = lax.optimization_barrier(jnp.mean(centre * centre, axis=-1, keepdims=True))
    return centre * lax.rsqrt(spread + EPS) * gain_row + bias_row

def mirrored_positions(pack_len, groups):
    places = jnp.arange(pack_len, dtype=jnp.int32)
    block_len = pack_len // (2 * groups)
    owner_dev = places // (2 * block_len)
    within = places % (2 * block_len)
    return jnp.where(within < block_len, owner_dev * block_len + within, (2 * groups - 1 - owner_dev) * block_len + within - block_len).astype(jnp.int32)

def rotary_tables(places, head_size):
    halves = head_size // 2
    frequency = jnp.exp(-math.log(10000.0) * jnp.arange(halves, dtype=jnp.float32) * 2.0 / head_size)
    angles = places.astype(jnp.float32)[:, None] * frequency[None, :]
    cosine = jnp.cos(angles)
    sine_table = jnp.sin(angles)
    return (jnp.concatenate([cosine, cosine], -1), jnp.concatenate([sine_table, sine_table], -1))

def rotate_half(values):
    first_half, second_half = jnp.split(values, 2, axis=-1)
    return jnp.concatenate([-second_half, first_half], axis=-1)

def rotary(values, cosine, sine_table):
    return values * cosine[:, None, :] + rotate_half(values) * sine_table[:, None, :]

def matmul(left, right):
    return jnp.dot(left, right, precision=lax.Precision.HIGHEST, preferred_element_type=jnp.float32)

def pack_forward(inputs, doc_row, params):
    w_qkv, w_out, w_up, w_down, gains, biases = params
    places = mirrored_positions(PACK, N_NARROW)
    documents = jnp.take(doc_row, places)
    cosine, sine_table = rotary_tables(places, HEAD_DIM)
    scale = 1.0 / math.sqrt(HEAD_DIM)
    normed = low(layer_norm(inputs, gains[0], biases[0]))
    mixed = low_back(matmul(normed, w_qkv))
    queries = low(rotary(mixed[:, :D].reshape(PACK, HEADS, HEAD_DIM), cosine, sine_table))
    key_rows = low(rotary(mixed[:, D:2 * D].reshape(PACK, HEADS, HEAD_DIM), cosine, sine_table))
    values = low(mixed[:, 2 * D:].reshape(PACK, HEADS, HEAD_DIM))
    allowed = (places[:, None] >= places[None, :]) & (documents[:, None] == documents[None, :])

    def one_head(operands):
        head_query, head_key, head_value = operands
        scores = low_back(scale * matmul(head_query, head_key.T))
        scores = jnp.where(allowed, scores, -1e+30)
        weights = jax.nn.softmax(scores, axis=-1)
        return matmul(low(weights), head_value)
    head_outs = lax.map(jax.checkpoint(one_head), (jnp.transpose(queries, (1, 0, 2)), jnp.transpose(key_rows, (1, 0, 2)), jnp.transpose(values, (1, 0, 2))))
    attended = low(low_back(jnp.transpose(head_outs, (1, 0, 2)).reshape(PACK, D)))
    branch = low_back(matmul(attended, w_out))
    middle = inputs + layer_norm(branch, gains[1], biases[1])
    normed2 = low(layer_norm(middle, gains[2], biases[2]))
    hidden = low_back(matmul(normed2, w_up))
    active = low(jax.nn.gelu(hidden, approximate=True))
    branch2 = low_back(matmul(active, w_down))
    return middle + layer_norm(branch2, gains[3], biases[3])

def reference(tokens, doc_ids, w_qkv, w_out, w_up, w_down, norm_gains, norm_biases, cotangent):
    params = (w_qkv.astype(jnp.float32), w_out.astype(jnp.float32), w_up.astype(jnp.float32), w_down.astype(jnp.float32), norm_gains.astype(jnp.float32), norm_biases.astype(jnp.float32))

    def whole(inputs, weights):

        def step_pack(carry, item_parts):
            return (carry, jax.checkpoint(pack_forward)(item_parts[0], item_parts[1], weights))
        return lax.scan(step_pack, jnp.zeros((), jnp.float32), (inputs, doc_ids))[1]
    outputs, pull = jax.vjp(whole, tokens.astype(jnp.float32), params)
    grad_inputs, grad_params = pull(cotangent.astype(jnp.float32))
    return (outputs.astype(jnp.bfloat16), grad_inputs.astype(jnp.bfloat16), grad_params[0], grad_params[1], grad_params[2], grad_params[3], grad_params[4], grad_params[5])
```

```python
import functools
import math

import jax
import jax.numpy as jnp
from jax import lax
from jax.experimental import pallas as pl
from jax.experimental.pallas import tpu as pltpu
from jax.sharding import PartitionSpec as P

HEAD_DIM = 64
EPS = 1e-05
F32 = jnp.float32
BF16 = jnp.bfloat16
TILE = 256
GROUP = 256
VMEM_LIMIT = 60 * 1024 * 1024
NN = (((1,), (0,)), ((), ()))
NT = (((1,), (1,)), ((), ()))
TN = (((0,), (0,)), ((), ()))


def dot(left, right, dims=NN):
    return lax.dot_general(left, right, dims, preferred_element_type=F32)


def params(**extra):
    return pltpu.CompilerParams(vmem_limit_bytes=VMEM_LIMIT, **extra)


def whole(shape):
    return pl.BlockSpec(shape, lambda *_: (0,) * len(shape), pipeline_mode=pl.Buffered(1))


def norm_parts(rows):
    centre = rows - jnp.mean(rows, axis=-1, keepdims=True)
    rstd = lax.rsqrt(jnp.mean(centre * centre, axis=-1, keepdims=True) + EPS)
    return centre * rstd, rstd


def norm_back(unit, rstd, gain, grad):
    scaled = grad * gain
    first = jnp.mean(scaled, axis=-1, keepdims=True)
    second = jnp.mean(scaled * unit, axis=-1, keepdims=True)
    return rstd * (scaled - first - unit * second)


def token_sum(rows):
    return jnp.sum(rows, axis=0, keepdims=True)


def project_kernel(tok, w, gains, biases, cosine, sine, *refs):
    normed_out, mixed_out = refs[-2:]
    unit, _ = norm_parts(tok[...].astype(F32))
    normed = (unit * gains[0:1, :] + biases[0:1, :]).astype(BF16)
    normed_out[...] = normed
    width = tok.shape[1]
    lanes = lax.broadcasted_iota(jnp.int32, (TILE, 128), 1)
    first_half = lanes % HEAD_DIM < HEAD_DIM // 2
    scale = 1.0 / math.sqrt(HEAD_DIM)
    cos = cosine[...]
    sin = sine[...]
    for start in range(0, 3 * width, 256):
        part = dot(normed, w[:, start : start + 256])
        if start >= 2 * width:
            mixed_out[:, start : start + 256] = part.astype(BF16)
            continue
        for sub in range(0, 256, 128):
            u = part[:, sub : sub + 128]
            turned = jnp.where(first_half, pltpu.roll(u, 96, 1), pltpu.roll(u, 32, 1))
            out = u * cos + turned * sin
            out = out.astype(BF16)
            if start < width:
                out = out * jnp.asarray(scale, BF16)
            mixed_out[:, start + sub : start + sub + 128] = out


def project(tok, w_qkv, gains, biases, cosine, sine, first_block, earlier, pack_len):
    rows, width = tok.shape
    wide = w_qkv.shape[1]
    out_shape = (
        jax.ShapeDtypeStruct((pack_len, width), BF16),
        jax.ShapeDtypeStruct((pack_len, wide), BF16),
    )
    in_specs = [
        pl.BlockSpec((TILE, width), lambda i: (i, 0)),
        whole((width, wide)),
        whole(gains.shape),
        whole(biases.shape),
        pl.BlockSpec((TILE, 128), lambda i: (i + first_block, 0)),
        pl.BlockSpec((TILE, 128), lambda i: (i + first_block, 0)),
    ]
    args = [tok, w_qkv, gains, biases, cosine, sine]
    aliases = {}
    if earlier is not None:
        in_specs += [pl.BlockSpec(memory_space=pl.ANY)] * 2
        aliases = {6: 0, 7: 1}
        args += list(earlier)
    return pl.pallas_call(
        project_kernel,
        grid=(rows // TILE,),
        in_specs=in_specs,
        out_specs=(
            pl.BlockSpec((TILE, width), lambda i: (i + first_block, 0)),
            pl.BlockSpec((TILE, wide), lambda i: (i + first_block, 0)),
        ),
        out_shape=out_shape,
        input_output_aliases=aliases,
        compiler_params=params(),
        name="project",
    )(*args)


def diagonal_mask(scores):
    size = scores.shape[1]
    first = scores.shape[0] - size
    keys = lax.broadcasted_iota(jnp.int32, (size, size), 0)
    asks = lax.broadcasted_iota(jnp.int32, (size, size), 1)
    tail = jnp.where(keys <= asks, scores[first:], -1e30)
    if first == 0:
        return tail
    return jnp.concatenate([scores[:first], tail], axis=0)


def attend_kernel(info, q, k, v, out, stats, key_heads, q_t, v_t, out_t):
    heads = GROUP // HEAD_DIM
    blocks = q.shape[0] // TILE
    for i in range(blocks):
        rows = slice(i * TILE, (i + 1) * TILE)
        at = pl.multiple_of(info[i] * TILE, TILE)
        q_t[:, pl.ds(at, TILE)] = q[rows, :].T
        v_t[:, pl.ds(at, TILE)] = v[rows, :].T
        for h in range(heads):
            key_heads[h, pl.ds(at, TILE), :] = k[rows, h * HEAD_DIM : (h + 1) * HEAD_DIM]

    def one_head(h, first_key):
        head_rows = pl.ds(pl.multiple_of(h * HEAD_DIM, HEAD_DIM), HEAD_DIM)
        for block in range(blocks):
            cols = slice(block * TILE, (block + 1) * TILE)
            keys = slice(first_key(block), (block + 1) * TILE)
            scores = diagonal_mask(dot(key_heads[h, keys, :], q_t[head_rows, cols]))
            peak = jnp.max(scores, axis=0, keepdims=True)
            weights = jnp.exp(scores - peak)
            total = jnp.sum(weights, axis=0, keepdims=True)
            mixed = dot(v_t[head_rows, keys], weights.astype(BF16))
            out_t[head_rows, cols] = mixed * (1.0 / total)
            stats[0, pl.ds(h, 1), cols] = peak + jnp.log(total)

    many = info[blocks] != 0

    @pl.when(jnp.logical_not(many))
    def _():
        @pl.loop(0, heads)
        def _(h):
            one_head(h, lambda block: 0)

    @pl.when(many)
    def _():
        @pl.loop(0, heads)
        def _(h):
            one_head(h, lambda block: block * TILE)

    for i in range(blocks):
        at = pl.multiple_of(info[i] * TILE, TILE)
        out[i * TILE : (i + 1) * TILE, :] = out_t[:, pl.ds(at, TILE)].T.astype(BF16)


def attend(info, mixed):
    rows, wide = mixed.shape
    width = wide // 3
    groups = width // GROUP
    heads = GROUP // HEAD_DIM
    return pl.pallas_call(
        attend_kernel,
        grid_spec=pltpu.PrefetchScalarGridSpec(
            num_scalar_prefetch=1,
            grid=(groups,),
            in_specs=[
                pl.BlockSpec((rows, GROUP), lambda g, s: (0, g)),
                pl.BlockSpec((rows, GROUP), lambda g, s: (0, g + groups)),
                pl.BlockSpec((rows, GROUP), lambda g, s: (0, g + 2 * groups)),
            ],
            out_specs=(
                pl.BlockSpec((rows, GROUP), lambda g, s: (0, g)),
                pl.BlockSpec((1, heads, rows), lambda g, s: (g, 0, 0)),
            ),
            scratch_shapes=[
                pltpu.VMEM((heads, rows, HEAD_DIM), BF16),
                pltpu.VMEM((GROUP, rows), BF16),
                pltpu.VMEM((GROUP, rows), BF16),
                pltpu.VMEM((GROUP, rows), F32),
            ],
        ),
        out_shape=(
            jax.ShapeDtypeStruct((rows, width), BF16),
            jax.ShapeDtypeStruct((groups, heads, rows), F32),
        ),
        compiler_params=params(),
        name="attend",
    )(info, mixed, mixed, mixed)


def feed_kernel(tok, cot, att, w_out, w_up, w_down, gains, biases,
                layer_out, branch_out, normed2_out, active_out, back2_out, hidden_back_out, sums,
                slope):
    chunk = 1024
    residual = tok[...].astype(F32)
    branch = dot(att[...], w_out[...])
    branch_out[...] = branch
    unit1, _ = norm_parts(branch)
    middle = residual + unit1 * gains[1:2, :] + biases[1:2, :]
    unit2, _ = norm_parts(middle)
    normed2 = (unit2 * gains[2:3, :] + biases[2:3, :]).astype(BF16)
    normed2_out[...] = normed2
    ff = w_up.shape[1]
    root = math.sqrt(2.0 / math.pi)
    branch2 = jnp.zeros_like(branch)
    for start in range(0, ff, chunk):
        cols = slice(start, start + chunk)
        z = dot(normed2, w_up[:, cols])
        square = z * z
        bend = jnp.tanh(z * (root + (root * 0.044715) * square))
        half = 0.5 + 0.5 * bend
        active = (z * half).astype(BF16)
        active_out[:, cols] = active
        inner = (0.5 * root) + (1.5 * root * 0.044715) * square
        slope[:, cols] = half + z * (1.0 - bend * bend) * inner
        branch2 = branch2 + dot(active, w_down[cols, :])
    unit3, rstd3 = norm_parts(branch2)
    layer_out[...] = (middle + unit3 * gains[3:4, :] + biases[3:4, :]).astype(BF16)
    upstream = cot[...].astype(F32)
    back2 = norm_back(unit3, rstd3, gains[3:4, :], upstream).astype(BF16)
    back2_out[...] = back2

    @pl.when(pl.program_id(0) == 0)
    def _():
        sums[...] = jnp.zeros_like(sums)

    sums[0:1, :] += token_sum(upstream * unit3)
    sums[1:2, :] += token_sum(upstream)
    for start in range(0, ff, chunk):
        cols = slice(start, start + chunk)
        grad_active = dot(back2, w_down[cols, :], NT)
        hidden_back_out[:, cols] = (grad_active * slope[:, cols]).astype(BF16)


def feed(tok, cot, att, w_out, w_up, w_down, gains, biases):
    rows, width = tok.shape
    ff = w_up.shape[1]
    row_block = lambda size: pl.BlockSpec((TILE, size), lambda i: (i, 0))
    return pl.pallas_call(
        feed_kernel,
        grid=(rows // TILE,),
        in_specs=[
            row_block(width), row_block(width), row_block(width),
            whole(w_out.shape), whole(w_up.shape), whole(w_down.shape),
            whole(gains.shape), whole(biases.shape),
        ],
        out_specs=(
            row_block(width), row_block(width), row_block(width), row_block(ff),
            row_block(width), row_block(ff), pl.BlockSpec((8, width), lambda i: (0, 0)),
        ),
        out_shape=(
            jax.ShapeDtypeStruct((rows, width), BF16),
            jax.ShapeDtypeStruct((rows, width), F32),
            jax.ShapeDtypeStruct((rows, width), BF16),
            jax.ShapeDtypeStruct((rows, ff), BF16),
            jax.ShapeDtypeStruct((rows, width), BF16),
            jax.ShapeDtypeStruct((rows, ff), BF16),
            jax.ShapeDtypeStruct((8, width), F32),
        ),
        scratch_shapes=[pltpu.VMEM((TILE, ff), F32)],
        compiler_params=params(),
        name="feed",
    )(tok, cot, att, w_out, w_up, w_down, gains, biases)


def return_kernel(tok, cot, branch, hidden_back, w_out, w_up, gains, biases,
                  middle_back_out, branch_back_out, att_back_out, sums):
    unit1, rstd1 = norm_parts(branch[...])
    middle = tok[...].astype(F32) + unit1 * gains[1:2, :] + biases[1:2, :]
    unit2, rstd2 = norm_parts(middle)
    grad2 = dot(hidden_back[...], w_up[...], NT)
    middle_back = cot[...].astype(F32) + norm_back(unit2, rstd2, gains[2:3, :], grad2)
    middle_back_out[...] = middle_back
    branch_back = norm_back(unit1, rstd1, gains[1:2, :], middle_back).astype(BF16)
    branch_back_out[...] = branch_back
    att_back_out[...] = dot(branch_back, w_out[...], NT).astype(BF16)

    @pl.when(pl.program_id(0) == 0)
    def _():
        sums[...] = jnp.zeros_like(sums)

    sums[0:1, :] += token_sum(middle_back * unit1)
    sums[1:2, :] += token_sum(middle_back)
    sums[2:3, :] += token_sum(grad2 * unit2)
    sums[3:4, :] += token_sum(grad2)


def return_pass(tok, cot, branch, hidden_back, w_out, w_up, gains, biases):
    rows, width = tok.shape
    ff = w_up.shape[1]
    row_block = lambda size: pl.BlockSpec((TILE, size), lambda i: (i, 0))
    return pl.pallas_call(
        return_kernel,
        grid=(rows // TILE,),
        in_specs=[
            row_block(width), row_block(width), row_block(width), row_block(ff),
            whole(w_out.shape), whole(w_up.shape), whole(gains.shape), whole(biases.shape),
        ],
        out_specs=(
            row_block(width), row_block(width), row_block(width),
            pl.BlockSpec((8, width), lambda i: (0, 0)),
        ),
        out_shape=(
            jax.ShapeDtypeStruct((rows, width), F32),
            jax.ShapeDtypeStruct((rows, width), BF16),
            jax.ShapeDtypeStruct((rows, width), BF16),
            jax.ShapeDtypeStruct((8, width), F32),
        ),
        compiler_params=params(),
        name="return_pass",
    )(tok, cot, branch, hidden_back, w_out, w_up, gains, biases)


def attend_back_kernel(info, q, k, v, att, grad, stats, cos_t, sin_t, q_back, k_back, v_back,
                       q_heads, k_heads, v_heads, g_heads, q_t, k_t, g_t, inner, q_acc, k_acc, v_acc):
    heads = GROUP // HEAD_DIM
    half = HEAD_DIM // 2
    blocks = q.shape[0] // TILE
    rows_all = blocks * TILE
    for i in range(blocks):
        rows = slice(i * TILE, (i + 1) * TILE)
        at = pl.multiple_of(info[i] * TILE, TILE)
        spot = pl.ds(at, TILE)
        q_t[:, spot] = q[rows, :].T
        k_t[:, spot] = k[rows, :].T
        grad_t = grad[rows, :].T
        g_t[:, spot] = grad_t
        product = att[rows, :].T.astype(F32) * grad_t.astype(F32)
        for h in range(heads):
            lanes = slice(h * HEAD_DIM, (h + 1) * HEAD_DIM)
            q_heads[h, spot, :] = q[rows, lanes]
            k_heads[h, spot, :] = k[rows, lanes]
            v_heads[h, spot, :] = v[rows, lanes]
            g_heads[h, spot, :] = grad[rows, lanes]
            inner[pl.ds(h, 1), spot] = jnp.sum(product[lanes, :], axis=0, keepdims=True)

    def one_head(h, last_ask):
        head_rows = pl.ds(pl.multiple_of(h * HEAD_DIM, HEAD_DIM), HEAD_DIM)
        for block in range(blocks):
            keys = slice(block * TILE, (block + 1) * TILE)
            cols = slice(block * TILE, last_ask(block))
            scores = dot(k_heads[h, keys, :], q_t[head_rows, cols])
            low = scores[:, :TILE]
            keys_at = lax.broadcasted_iota(jnp.int32, (TILE, TILE), 0)
            asks_at = lax.broadcasted_iota(jnp.int32, (TILE, TILE), 1)
            low = jnp.where(keys_at <= asks_at, low, -1e30)
            if scores.shape[1] > TILE:
                scores = jnp.concatenate([low, scores[:, TILE:]], axis=1)
            else:
                scores = low
            weights = jnp.exp(scores - stats[0, pl.ds(h, 1), cols])
            weight_back = dot(v_heads[h, keys, :], g_t[head_rows, cols])
            score_back = (weights * (weight_back - inner[pl.ds(h, 1), cols])).astype(BF16)
            v_acc[h, keys, :] = dot(weights.astype(BF16), g_heads[h, cols, :])
            k_acc[h, keys, :] = dot(score_back, q_heads[h, cols, :])
            change = dot(k_t[head_rows, keys], score_back)
            if block == 0:
                q_acc[head_rows, cols] = change
            elif last_ask(0) < rows_all:
                q_acc[head_rows, cols] = change
            else:
                q_acc[head_rows, cols] += change

    many = info[blocks] != 0

    @pl.when(jnp.logical_not(many))
    def _():
        @pl.loop(0, heads)
        def _(h):
            one_head(h, lambda block: rows_all)

    @pl.when(many)
    def _():
        @pl.loop(0, heads)
        def _(h):
            one_head(h, lambda block: (block + 1) * TILE)

    scale = 1.0 / math.sqrt(HEAD_DIM)
    for i in range(blocks):
        rows = slice(i * TILE, (i + 1) * TILE)
        spot = pl.ds(pl.multiple_of(info[i] * TILE, TILE), TILE)
        cos = cos_t[:, rows]
        sin = sin_t[:, rows]

        def turn_back(parts, factor):
            turned = []
            for part in parts:
                first, second = part[:half], part[half:]
                turned.append(first * cos + second * sin)
                turned.append(second * cos - first * sin)
            return (jnp.concatenate(turned, axis=0) * factor).T.astype(BF16)

        q_back[rows, :] = turn_back(
            [q_acc[h * HEAD_DIM : (h + 1) * HEAD_DIM, spot] for h in range(heads)], scale
        )
        k_back[rows, :] = turn_back([k_acc[h, spot, :].T for h in range(heads)], 1.0)
        v_back[rows, :] = jnp.concatenate(
            [v_acc[h, spot, :] for h in range(heads)], axis=1
        ).astype(BF16)


def attend_back(info, mixed, att, grad, stats, cos_t, sin_t):
    rows, wide = mixed.shape
    width = wide // 3
    groups = width // GROUP
    heads = GROUP // HEAD_DIM
    spec = lambda shift: pl.BlockSpec((rows, GROUP), lambda g, s: (0, g + shift * groups))
    out = jax.ShapeDtypeStruct((rows, width), BF16)
    per_head = pltpu.VMEM((heads, rows, HEAD_DIM), BF16)
    turned = pltpu.VMEM((GROUP, rows), BF16)
    return pl.pallas_call(
        attend_back_kernel,
        grid_spec=pltpu.PrefetchScalarGridSpec(
            num_scalar_prefetch=1,
            grid=(groups,),
            in_specs=[
                spec(0), spec(1), spec(2), spec(0), spec(0),
                pl.BlockSpec((1, heads, rows), lambda g, s: (g, 0, 0)),
                pl.BlockSpec((HEAD_DIM // 2, rows), lambda g, s: (0, 0)),
                pl.BlockSpec((HEAD_DIM // 2, rows), lambda g, s: (0, 0)),
            ],
            out_specs=(spec(0), spec(0), spec(0)),
            scratch_shapes=[
                per_head, per_head, per_head, per_head,
                turned, turned, turned,
                pltpu.VMEM((8, rows), F32),
                pltpu.VMEM((GROUP, rows), F32),
                pltpu.VMEM((heads, rows, HEAD_DIM), F32),
                pltpu.VMEM((heads, rows, HEAD_DIM), F32),
            ],
        ),
        out_shape=(out, out, out),
        compiler_params=params(),
        name="attend_back",
    )(info, mixed, mixed, mixed, att, grad, stats, cos_t, sin_t)


def finish_kernel(tok, middle_back, q_back, k_back, v_back, w_qkv, gains, grad_out, sums):
    width = tok.shape[1]
    unit, rstd = norm_parts(tok[...].astype(F32))
    grad = (
        dot(q_back[...], w_qkv[:, :width], NT)
        + dot(k_back[...], w_qkv[:, width : 2 * width], NT)
        + dot(v_back[...], w_qkv[:, 2 * width :], NT)
    )
    back = middle_back[...] + norm_back(unit, rstd, gains[0:1, :], grad)
    grad_out[...] = back.astype(BF16)

    @pl.when(pl.program_id(0) == 0)
    def _():
        sums[...] = jnp.zeros_like(sums)

    sums[0:1, :] += token_sum(grad * unit)
    sums[1:2, :] += token_sum(grad)


def finish(tok, middle_back, q_back, k_back, v_back, w_qkv, gains):
    rows, width = tok.shape
    row_block = pl.BlockSpec((TILE, width), lambda i: (i, 0))
    return pl.pallas_call(
        finish_kernel,
        grid=(rows // TILE,),
        in_specs=[row_block] * 5 + [whole(w_qkv.shape), whole(gains.shape)],
        out_specs=(row_block, pl.BlockSpec((8, width), lambda i: (0, 0))),
        out_shape=(
            jax.ShapeDtypeStruct((rows, width), BF16),
            jax.ShapeDtypeStruct((8, width), F32),
        ),
        compiler_params=params(),
        name="finish",
    )(tok, middle_back, q_back, k_back, v_back, w_qkv, gains)


def weight_grad_kernel(picks, left, right, *refs):
    out = refs[-1]
    total = dot(left[...], right[...], TN)
    if len(refs) == 2:
        total = total + refs[0][...].astype(F32)
    out[...] = total.astype(BF16)


def weight_grad(picks, left, right, col_at, cols, addend=None, add_at=0):
    tokens = left.shape[0]
    count = picks.shape[0]
    in_specs = [
        pl.BlockSpec((tokens, TILE), lambda i, s: (0, s[i])),
        pl.BlockSpec((tokens, cols), lambda i, s: (0, col_at), pipeline_mode=pl.Buffered(1)),
    ]
    args = [picks, left, right]
    if addend is not None:
        in_specs.append(pl.BlockSpec((TILE, cols), lambda i, s: (i + add_at, 0)))
        args.append(addend)
    return pl.pallas_call(
        weight_grad_kernel,
        grid_spec=pltpu.PrefetchScalarGridSpec(
            num_scalar_prefetch=1,
            grid=(count,),
            in_specs=in_specs,
            out_specs=pl.BlockSpec((TILE, cols), lambda i, s: (i, 0)),
        ),
        out_shape=jax.ShapeDtypeStruct((count * TILE, cols), BF16),
        compiler_params=params(),
        name="weight_grad",
    )(*args)


def swap_wide(rows, bit):
    size = lax.axis_size("wide")
    return lax.ppermute(rows, "wide", [(i, i ^ bit) for i in range(size)])


def swap_narrow(rows):
    return lax.ppermute(rows, "narrow", [(0, 1), (1, 0)])


def add_up(parts, dtype=BF16):
    total = parts[0].astype(F32)
    for part in parts[1:]:
        total = total + part.astype(F32)
    return total.astype(dtype)


def half_of(parts, which):
    size = parts[0].shape[0] // 2
    return [lax.dynamic_slice_in_dim(part, which * size, size, 0) for part in parts]


def in_order(mine, theirs, which):
    return jnp.concatenate(
        [jnp.where(which == 0, mine, theirs), jnp.where(which == 0, theirs, mine)], axis=0
    )


def reduced_grad(left, right, col_at, cols, row_at, rows):
    n = lax.axis_index("narrow")
    w = lax.axis_index("wide")
    core = w % 2
    half_rows = left.shape[1] // 2
    per_core = rows // 2 // TILE
    block = jnp.arange(per_core, dtype=jnp.int32)

    def picks(x, c):
        return ((x * half_rows + row_at + c * (rows // 2)) // TILE + block).astype(jnp.int32)

    far = weight_grad(
        jnp.concatenate([picks(1 - n, 1 - core), picks(n, 1 - core)]), left, right, col_at, cols
    )
    from_core = swap_wide(far, 1)
    give = weight_grad(picks(1 - n, core), left, right, col_at, cols, from_core, 0)
    from_x = swap_narrow(give)
    parts = [weight_grad(picks(n, core), left, right, col_at, cols, from_core, per_core), from_x]
    bits = []
    bit = 2
    while bit < lax.axis_size("wide"):
        bits.append(bit)
        bit *= 2
    for bit in bits:
        mine = (w // bit) % 2
        got = swap_wide(add_up(half_of(parts, 1 - mine)), bit)
        parts = half_of(parts, mine) + [got]
    piece = add_up(parts)
    for bit in reversed(bits):
        piece = in_order(piece, swap_wide(piece, bit), (w // bit) % 2)
    return in_order(piece.astype(F32), swap_wide(piece, 1).astype(F32), core)


def local(tokens, doc_ids, w_qkv, w_out, w_up, w_down, norm_gains, norm_biases, cotangent):
    narrow_size = lax.axis_size("narrow")
    packs, tok_rows, width = tokens.shape
    assert narrow_size == 2 and packs == 2 and tok_rows == 2 * TILE
    pack_len = tok_rows * narrow_size
    ff = w_up.shape[1]
    n = lax.axis_index("narrow")
    pick = lambda array, index: lax.dynamic_index_in_dim(array, index, 0, keepdims=False)

    own_tok = pick(tokens, n)
    far_tok = swap_narrow(pick(tokens, 1 - n))
    own_cot = pick(cotangent, n)
    far_cot = swap_narrow(pick(cotangent, 1 - n))
    doc_row = pick(doc_ids, n)
    many = (doc_row[pack_len - 1] != 0).astype(jnp.int32)
    own_blocks = jnp.stack([n, 3 - n])
    far_blocks = jnp.stack([1 - n, 2 + n])
    block_at = jnp.concatenate([own_blocks, far_blocks]).astype(jnp.int32)
    info = jnp.concatenate([block_at, many[None]])

    halves = HEAD_DIM // 2
    frequency = jnp.exp(
        -math.log(10000.0) * jnp.arange(halves, dtype=F32) * 2.0 / HEAD_DIM
    )
    places = (block_at[:, None] * TILE + jnp.arange(TILE, dtype=jnp.int32)[None, :]).reshape(-1)
    angles_t = frequency[:, None] * places.astype(F32)[None, :]
    cos_t = jnp.cos(angles_t)
    sin_t = jnp.sin(angles_t)
    cos = cos_t.T
    sin = sin_t.T
    cosine = jnp.concatenate([cos] * 4, axis=1)
    sine = jnp.concatenate([-sin, sin, -sin, sin], axis=1)

    early = project(own_tok, w_qkv, norm_gains, norm_biases, cosine, sine, 0, None, pack_len)
    normed, mixed = project(
        far_tok, w_qkv, norm_gains, norm_biases, cosine, sine, 2, early, pack_len
    )
    tok = jnp.concatenate([own_tok, far_tok], axis=0)
    cot = jnp.concatenate([own_cot, far_cot], axis=0)
    att, stats = attend(info, mixed)
    out, branch, normed2, active, back2, hidden_back, sums3 = feed(
        tok, cot, att, w_out, w_up, w_down, norm_gains, norm_biases
    )
    far_out = swap_narrow(out[tok_rows:])
    grad_down = jnp.concatenate(
        [reduced_grad(active, back2, 0, width, at, ff // 4) for at in range(0, ff // 2, ff // 4)], axis=0
    )
    grad_up = jnp.concatenate(
        [reduced_grad(normed2, hidden_back, at, ff // 2, 0, width // 2) for at in range(2)], axis=1
    )
    middle_back, branch_back, att_back, sums12 = return_pass(
        tok, cot, branch, hidden_back, w_out, w_up, norm_gains, norm_biases
    )
    grad_out_proj = reduced_grad(att, branch_back, 0, width, 0, width // 2)
    q_back, k_back, v_back = attend_back(info, mixed, att, att_back, stats, cos_t, sin_t)
    grad_qkv = jnp.concatenate(
        [reduced_grad(normed, part, 0, width, 0, width // 2) for part in (q_back, k_back, v_back)],
        axis=1,
    )
    grad_tok, sums0 = finish(tok, middle_back, q_back, k_back, v_back, w_qkv, norm_gains)
    far_grad = swap_narrow(grad_tok[tok_rows:])

    norm_term = jnp.concatenate(
        [sums0[0:1], sums12[0:1], sums12[2:3], sums3[0:1],
         sums0[1:2], sums12[1:2], sums12[3:4], sums3[1:2]], axis=0
    )
    norm_term = norm_term + swap_narrow(norm_term)
    bit = 1
    while bit < lax.axis_size("wide"):
        norm_term = norm_term + swap_wide(norm_term, bit)
        bit *= 2
    norm_term = lax.dynamic_slice_in_dim(norm_term, n * (width // 2), width // 2, 1)

    def in_packs(own, far):
        return jnp.stack([jnp.where(n == 0, own, far), jnp.where(n == 0, far, own)])

    return (
        in_packs(out[:tok_rows], far_out),
        in_packs(grad_tok[:tok_rows], far_grad),
        grad_qkv,
        grad_out_proj,
        grad_up,
        grad_down,
        norm_term[:4],
        norm_term[4:],
    )


def solution(mesh):
    rows = P("wide", "narrow", None)
    return jax.shard_map(
        local,
        mesh=mesh,
        in_specs=(rows, P("wide", None), P(), P(), P(), P(), P(), P(), rows),
        out_specs=(
            rows, rows,
            P("narrow", None), P("narrow", None), P("narrow", None), P("narrow", None),
            P(None, "narrow"), P(None, "narrow"),
        ),
        check_vma=False,
    )
```

```python
import functools
import math

import jax
import jax.numpy as jnp
from jax import lax
from jax.experimental import pallas as pl
from jax.experimental.pallas import tpu as pltpu
from jax.sharding import PartitionSpec as P

HEAD_DIM = 64
EPS = 1e-05
F32 = jnp.float32
BF16 = jnp.bfloat16
TILE = 256
GROUP = 256
VMEM_LIMIT = 60 * 1024 * 1024
BYTES_PER_US = 900000
NN = (((1,), (0,)), ((), ()))
NT = (((1,), (1,)), ((), ()))
TN = (((0,), (0,)), ((), ()))


def dot(left, right, dims=NN):
    return lax.dot_general(left, right, dims, preferred_element_type=F32)


def call(kernel, grid, prefetch, inputs, outputs, deps, name, us, scratch=(), aliases=None):
    given = len(prefetch) + len(inputs)

    def body(*refs):
        kernel(*refs[:given], *refs[given + len(deps) :])

    in_specs = [spec for _, spec in inputs] + [pl.BlockSpec(memory_space=pl.ANY)] * len(deps)
    return pl.pallas_call(
        body,
        grid_spec=pltpu.PrefetchScalarGridSpec(
            num_scalar_prefetch=len(prefetch),
            grid=grid,
            in_specs=in_specs,
            out_specs=tuple(spec for _, spec in outputs),
            scratch_shapes=list(scratch),
        ),
        out_shape=tuple(shape for shape, _ in outputs),
        input_output_aliases=aliases or {},
        compiler_params=pltpu.CompilerParams(vmem_limit_bytes=VMEM_LIMIT),
        cost_estimate=pl.CostEstimate(
            flops=0, transcendentals=0, bytes_accessed=int(us * BYTES_PER_US)
        ),
        name=name,
    )(*prefetch, *[array for array, _ in inputs], *deps)


def shape(dims, dtype):
    return jax.ShapeDtypeStruct(dims, dtype)


def whole(dims):
    return pl.BlockSpec(dims, lambda *_: (0,) * len(dims), pipeline_mode=pl.Buffered(1))


def row_block(size):
    return pl.BlockSpec((TILE, size), lambda i, *_: (i, 0))


def own_rows(size):
    return pl.BlockSpec((1, TILE, size), lambda i, place, *_: (place[0], jnp.minimum(i, 1), 0))


def near_rows(size):
    return pl.BlockSpec((TILE, size), lambda i, *_: (jnp.minimum(i, 1), 0))


def far_rows(size):
    return pl.BlockSpec((TILE, size), lambda i, *_: (jnp.maximum(i - 2, 0), 0))


def pick_rows(own, far):
    return jnp.where(pl.program_id(0) < 2, own[0].astype(F32), far[...].astype(F32))


def put_rows(near, far, rows):
    @pl.when(pl.program_id(0) < 2)
    def _():
        near[...] = rows

    @pl.when(pl.program_id(0) >= 2)
    def _():
        far[...] = rows


def tie(array, *deps):
    return lax.optimization_barrier((array,) + deps)[0]


def norm_parts(rows):
    centre = rows - jnp.mean(rows, axis=-1, keepdims=True)
    rstd = lax.rsqrt(jnp.mean(centre * centre, axis=-1, keepdims=True) + EPS)
    return centre * rstd, rstd


def norm_back(unit, rstd, gain, grad):
    scaled = grad * gain
    first = jnp.mean(scaled, axis=-1, keepdims=True)
    second = jnp.mean(scaled * unit, axis=-1, keepdims=True)
    return rstd * (scaled - first - unit * second)


def token_sum(rows):
    return jnp.sum(rows, axis=0, keepdims=True)


def project_kernel(place, tok, w, gains, biases, cosine, sine, normed_out, mixed_out):
    rows = tok[0] if len(tok.shape) == 3 else tok[...]
    unit, _ = norm_parts(rows.astype(F32))
    normed = (unit * gains[0:1, :] + biases[0:1, :]).astype(BF16)
    normed_out[...] = normed
    width = normed.shape[1]
    lanes = lax.broadcasted_iota(jnp.int32, (TILE, 128), 1)
    first_half = lanes % HEAD_DIM < HEAD_DIM // 2
    scale = 1.0 / math.sqrt(HEAD_DIM)
    cos = cosine[...]
    sin = sine[...]
    for start in range(0, 3 * width, 256):
        part = dot(normed, w[:, start : start + 256])
        if start >= 2 * width:
            mixed_out[:, start : start + 256] = part.astype(BF16)
            continue
        for sub in range(0, 256, 128):
            u = part[:, sub : sub + 128]
            turned = jnp.where(first_half, pltpu.roll(u, 96, 1), pltpu.roll(u, 32, 1))
            out = u * cos + turned * sin
            out = out.astype(BF16)
            if start < width:
                out = out * jnp.asarray(scale, BF16)
            mixed_out[:, start + sub : start + sub + 128] = out


def project(place, tok, w_qkv, gains, biases, cosine, sine, first_block, earlier, pack_len):
    width, wide = w_qkv.shape
    steps = tok.shape[-2] // TILE
    at = lambda size: pl.BlockSpec((TILE, size), lambda i, *_: (i + first_block, 0))
    own = tok.ndim == 3
    return call(
        project_kernel,
        (steps,),
        [place],
        [
            (tok, own_rows(width) if own else row_block(width)),
            (w_qkv, whole(w_qkv.shape)),
            (gains, whole(gains.shape)),
            (biases, whole(biases.shape)),
            (cosine, at(128)),
            (sine, at(128)),
        ],
        [
            (shape((pack_len, width), BF16), at(width)),
            (shape((pack_len, wide), BF16), at(wide)),
        ],
        list(earlier),
        "project",
        8,
        aliases={7: 0, 8: 1} if earlier else None,
    )


def diagonal_mask(scores):
    size = scores.shape[1]
    first = scores.shape[0] - size
    keys = lax.broadcasted_iota(jnp.int32, (size, size), 0)
    asks = lax.broadcasted_iota(jnp.int32, (size, size), 1)
    tail = jnp.where(keys <= asks, scores[first:], -1e30)
    if first == 0:
        return tail
    return jnp.concatenate([scores[:first], tail], axis=0)


def attend_kernel(info, q, k, v, out, stats, key_heads, q_t, v_t, out_t):
    heads = GROUP // HEAD_DIM
    blocks = q.shape[0] // TILE
    for i in range(blocks):
        rows = slice(i * TILE, (i + 1) * TILE)
        at = pl.multiple_of(info[i] * TILE, TILE)
        q_t[:, pl.ds(at, TILE)] = q[rows, :].T
        v_t[:, pl.ds(at, TILE)] = v[rows, :].T
        for h in range(heads):
            key_heads[h, pl.ds(at, TILE), :] = k[rows, h * HEAD_DIM : (h + 1) * HEAD_DIM]

    def one_head(h, first_key):
        head_rows = pl.ds(pl.multiple_of(h * HEAD_DIM, HEAD_DIM), HEAD_DIM)
        for block in range(blocks):
            cols = slice(block * TILE, (block + 1) * TILE)
            keys = slice(first_key(block), (block + 1) * TILE)
            scores = diagonal_mask(dot(key_heads[h, keys, :], q_t[head_rows, cols]))
            peak = jnp.max(scores, axis=0, keepdims=True)
            weights = jnp.exp(scores - peak)
            total = jnp.sum(weights, axis=0, keepdims=True)
            mixed = dot(v_t[head_rows, keys], weights.astype(BF16))
            out_t[head_rows, cols] = mixed * (1.0 / total)
            stats[0, pl.ds(h, 1), cols] = peak + jnp.log(total)

    many = info[blocks] != 0

    @pl.when(jnp.logical_not(many))
    def _():
        @pl.loop(0, heads)
        def _(h):
            one_head(h, lambda block: 0)

    @pl.when(many)
    def _():
        @pl.loop(0, heads)
        def _(h):
            one_head(h, lambda block: block * TILE)

    for i in range(blocks):
        at = pl.multiple_of(info[i] * TILE, TILE)
        out[i * TILE : (i + 1) * TILE, :] = out_t[:, pl.ds(at, TILE)].T.astype(BF16)


def attend(info, mixed):
    rows, wide = mixed.shape
    width = wide // 3
    groups = width // GROUP
    heads = GROUP // HEAD_DIM
    part = lambda shift: pl.BlockSpec((rows, GROUP), lambda g, s: (0, g + shift * groups))
    return call(
        attend_kernel,
        (groups,),
        [info],
        [(mixed, part(0)), (mixed, part(1)), (mixed, part(2))],
        [
            (shape((rows, width), BF16), part(0)),
            (
                shape((groups, heads, rows), F32),
                pl.BlockSpec((1, heads, rows), lambda g, s: (g, 0, 0)),
            ),
        ],
        [],
        "attend",
        36,
        scratch=[
            pltpu.VMEM((heads, rows, HEAD_DIM), BF16),
            pltpu.VMEM((GROUP, rows), BF16),
            pltpu.VMEM((GROUP, rows), BF16),
            pltpu.VMEM((GROUP, rows), F32),
        ],
    )


def feed_kernel(place, own_tok, far_tok, own_cot, far_cot, att, w_out, w_up, w_down, gains, biases,
                near_out, far_out, branch_out, normed2_out, active_out, back2_out, hidden_back_out, sums,
                slope):
    chunk = 1024
    residual = pick_rows(own_tok, far_tok)
    branch = dot(att[...], w_out[...])
    branch_out[...] = branch
    unit1, _ = norm_parts(branch)
    middle = residual + unit1 * gains[1:2, :] + biases[1:2, :]
    unit2, _ = norm_parts(middle)
    normed2 = (unit2 * gains[2:3, :] + biases[2:3, :]).astype(BF16)
    normed2_out[...] = normed2
    ff = w_up.shape[1]
    root = math.sqrt(2.0 / math.pi)
    branch2 = jnp.zeros_like(branch)
    for start in range(0, ff, chunk):
        cols = slice(start, start + chunk)
        z = dot(normed2, w_up[:, cols])
        square = z * z
        bend = jnp.tanh(z * (root + (root * 0.044715) * square))
        half = 0.5 + 0.5 * bend
        active = (z * half).astype(BF16)
        active_out[:, cols] = active
        inner = (0.5 * root) + (1.5 * root * 0.044715) * square
        slope[:, cols] = half + z * (1.0 - bend * bend) * inner
        branch2 = branch2 + dot(active, w_down[cols, :])
    unit3, rstd3 = norm_parts(branch2)
    put_rows(near_out, far_out, (middle + unit3 * gains[3:4, :] + biases[3:4, :]).astype(BF16))
    upstream = pick_rows(own_cot, far_cot)
    back2 = norm_back(unit3, rstd3, gains[3:4, :], upstream).astype(BF16)
    back2_out[...] = back2

    @pl.when(pl.program_id(0) == 0)
    def _():
        sums[...] = jnp.zeros_like(sums)

    sums[0:1, :] += token_sum(upstream * unit3)
    sums[1:2, :] += token_sum(upstream)
    for start in range(0, ff, chunk):
        cols = slice(start, start + chunk)
        grad_active = dot(back2, w_down[cols, :], NT)
        hidden_back_out[:, cols] = (grad_active * slope[:, cols]).astype(BF16)


def feed(place, tokens, far_tok, cotangent, far_cot, att, w_out, w_up, w_down, gains, biases):
    rows, width = att.shape
    ff = w_up.shape[1]
    return call(
        feed_kernel,
        (rows // TILE,),
        [place],
        [
            (tokens, own_rows(width)), (far_tok, far_rows(width)),
            (cotangent, own_rows(width)), (far_cot, far_rows(width)),
            (att, row_block(width)),
            (w_out, whole(w_out.shape)), (w_up, whole(w_up.shape)), (w_down, whole(w_down.shape)),
            (gains, whole(gains.shape)), (biases, whole(biases.shape)),
        ],
        [
            (shape((rows // 2, width), BF16), near_rows(width)),
            (shape((rows // 2, width), BF16), far_rows(width)),
            (shape((rows, width), F32), row_block(width)),
            (shape((rows, width), BF16), row_block(width)),
            (shape((rows, ff), BF16), row_block(ff)),
            (shape((rows, width), BF16), row_block(width)),
            (shape((rows, ff), BF16), row_block(ff)),
            (shape((8, width), F32), whole((8, width))),
        ],
        [],
        "feed",
        49,
        scratch=[pltpu.VMEM((TILE, ff), F32)],
    )


def return_kernel(place, own_tok, far_tok, own_cot, far_cot, branch, hidden_back, w_out, w_up, gains, biases,
                  middle_back_out, branch_back_out, att_back_out, sums):
    unit1, rstd1 = norm_parts(branch[...])
    middle = pick_rows(own_tok, far_tok) + unit1 * gains[1:2, :] + biases[1:2, :]
    unit2, rstd2 = norm_parts(middle)
    grad2 = dot(hidden_back[...], w_up[...], NT)
    middle_back = pick_rows(own_cot, far_cot) + norm_back(unit2, rstd2, gains[2:3, :], grad2)
    middle_back_out[...] = middle_back
    branch_back = norm_back(unit1, rstd1, gains[1:2, :], middle_back).astype(BF16)
    branch_back_out[...] = branch_back
    att_back_out[...] = dot(branch_back, w_out[...], NT).astype(BF16)

    @pl.when(pl.program_id(0) == 0)
    def _():
        sums[...] = jnp.zeros_like(sums)

    sums[0:1, :] += token_sum(middle_back * unit1)
    sums[1:2, :] += token_sum(middle_back)
    sums[2:3, :] += token_sum(grad2 * unit2)
    sums[3:4, :] += token_sum(grad2)


def return_pass(place, tokens, far_tok, cotangent, far_cot, branch, hidden_back, w_out, w_up,
                gains, biases, deps):
    rows, width = branch.shape
    ff = w_up.shape[1]
    return call(
        return_kernel,
        (rows // TILE,),
        [place],
        [
            (tokens, own_rows(width)), (far_tok, far_rows(width)),
            (cotangent, own_rows(width)), (far_cot, far_rows(width)),
            (branch, row_block(width)), (hidden_back, row_block(ff)),
            (w_out, whole(w_out.shape)), (w_up, whole(w_up.shape)),
            (gains, whole(gains.shape)), (biases, whole(biases.shape)),
        ],
        [
            (shape((rows, width), F32), row_block(width)),
            (shape((rows, width), BF16), row_block(width)),
            (shape((rows, width), BF16), row_block(width)),
            (shape((8, width), F32), whole((8, width))),
        ],
        deps,
        "return_pass",
        24,
    )


def attend_back_kernel(info, q, k, v, att, grad, stats, cos_t, sin_t, back,
                       q_heads, k_heads, v_heads, g_heads, q_t, k_t, g_t, inner, q_acc, k_acc, v_acc):
    heads = GROUP // HEAD_DIM
    half = HEAD_DIM // 2
    blocks = q.shape[0] // TILE
    rows_all = blocks * TILE
    for i in range(blocks):
        rows = slice(i * TILE, (i + 1) * TILE)
        at = pl.multiple_of(info[i] * TILE, TILE)
        spot = pl.ds(at, TILE)
        q_t[:, spot] = q[rows, :].T
        k_t[:, spot] = k[rows, :].T
        grad_t = grad[rows, :].T
        g_t[:, spot] = grad_t
        product = att[rows, :].T.astype(F32) * grad_t.astype(F32)
        for h in range(heads):
            lanes = slice(h * HEAD_DIM, (h + 1) * HEAD_DIM)
            q_heads[h, spot, :] = q[rows, lanes]
            k_heads[h, spot, :] = k[rows, lanes]
            v_heads[h, spot, :] = v[rows, lanes]
            g_heads[h, spot, :] = grad[rows, lanes]
            inner[pl.ds(h, 1), spot] = jnp.sum(product[lanes, :], axis=0, keepdims=True)

    def one_head(h, last_ask):
        head_rows = pl.ds(pl.multiple_of(h * HEAD_DIM, HEAD_DIM), HEAD_DIM)
        for block in range(blocks):
            keys = slice(block * TILE, (block + 1) * TILE)
            cols = slice(block * TILE, last_ask(block))
            scores = dot(k_heads[h, keys, :], q_t[head_rows, cols])
            low = scores[:, :TILE]
            keys_at = lax.broadcasted_iota(jnp.int32, (TILE, TILE), 0)
            asks_at = lax.broadcasted_iota(jnp.int32, (TILE, TILE), 1)
            low = jnp.where(keys_at <= asks_at, low, -1e30)
            if scores.shape[1] > TILE:
                scores = jnp.concatenate([low, scores[:, TILE:]], axis=1)
            else:
                scores = low
            weights = jnp.exp(scores - stats[0, pl.ds(h, 1), cols])
            weight_back = dot(v_heads[h, keys, :], g_t[head_rows, cols])
            score_back = (weights * (weight_back - inner[pl.ds(h, 1), cols])).astype(BF16)
            v_acc[h, keys, :] = dot(weights.astype(BF16), g_heads[h, cols, :])
            k_acc[h, keys, :] = dot(score_back, q_heads[h, cols, :])
            change = dot(k_t[head_rows, keys], score_back)
            if block == 0:
                q_acc[head_rows, cols] = change
            elif last_ask(0) < rows_all:
                q_acc[head_rows, cols] = change
            else:
                q_acc[head_rows, cols] += change

    many = info[blocks] != 0

    @pl.when(jnp.logical_not(many))
    def _():
        @pl.loop(0, heads)
        def _(h):
            one_head(h, lambda block: rows_all)

    @pl.when(many)
    def _():
        @pl.loop(0, heads)
        def _(h):
            one_head(h, lambda block: (block + 1) * TILE)

    scale = 1.0 / math.sqrt(HEAD_DIM)
    for i in range(blocks):
        rows = slice(i * TILE, (i + 1) * TILE)
        spot = pl.ds(pl.multiple_of(info[i] * TILE, TILE), TILE)
        cos = cos_t[:, rows]
        sin = sin_t[:, rows]

        def turn_back(parts, factor):
            turned = []
            for part in parts:
                first, second = part[:half], part[half:]
                turned.append(first * cos + second * sin)
                turned.append(second * cos - first * sin)
            return (jnp.concatenate(turned, axis=0) * factor).T.astype(BF16)

        back[0, rows, :] = turn_back(
            [q_acc[h * HEAD_DIM : (h + 1) * HEAD_DIM, spot] for h in range(heads)], scale
        )
        back[1, rows, :] = turn_back([k_acc[h, spot, :].T for h in range(heads)], 1.0)
        back[2, rows, :] = jnp.concatenate(
            [v_acc[h, spot, :] for h in range(heads)], axis=1
        ).astype(BF16)


def attend_back(info, mixed, att, grad, stats, cos_t, sin_t, half, deps):
    rows, wide = mixed.shape
    width = wide // 3
    groups = width // GROUP
    heads = GROUP // HEAD_DIM
    first = half * (groups // 2)
    spec = lambda shift: pl.BlockSpec((rows, GROUP), lambda g, s: (0, g + first + shift * groups))
    per_head = pltpu.VMEM((heads, rows, HEAD_DIM), BF16)
    turned = pltpu.VMEM((GROUP, rows), BF16)
    angles = pl.BlockSpec((HEAD_DIM // 2, rows), lambda g, s: (0, 0))
    return call(
        attend_back_kernel,
        (groups // 2,),
        [info],
        [
            (mixed, spec(0)), (mixed, spec(1)), (mixed, spec(2)), (att, spec(0)), (grad, spec(0)),
            (stats, pl.BlockSpec((1, heads, rows), lambda g, s: (g + first, 0, 0))),
            (cos_t, angles), (sin_t, angles),
        ],
        [
            (
                shape((3, rows, width // 2), BF16),
                pl.BlockSpec((3, rows, GROUP), lambda g, s: (0, 0, g)),
            ),
        ],
        deps,
        "attend_back",
        22,
        scratch=[
            per_head, per_head, per_head, per_head,
            turned, turned, turned,
            pltpu.VMEM((8, rows), F32),
            pltpu.VMEM((GROUP, rows), F32),
            pltpu.VMEM((heads, rows, HEAD_DIM), F32),
            pltpu.VMEM((heads, rows, HEAD_DIM), F32),
        ],
    )[0]


def finish_kernel(place, own_tok, far_tok, middle_back, left_back, right_back, w_qkv, gains,
                  near_out, far_out, sums):
    half = left_back.shape[2]
    unit, rstd = norm_parts(pick_rows(own_tok, far_tok))
    grad = None
    for part in range(3):
        for side, back in enumerate((left_back, right_back)):
            start = (2 * part + side) * half
            term = dot(back[part], w_qkv[:, start : start + half], NT)
            grad = term if grad is None else grad + term
    back = middle_back[...] + norm_back(unit, rstd, gains[0:1, :], grad)
    put_rows(near_out, far_out, back.astype(BF16))

    @pl.when(pl.program_id(0) == 0)
    def _():
        sums[...] = jnp.zeros_like(sums)

    sums[0:1, :] += token_sum(grad * unit)
    sums[1:2, :] += token_sum(grad)


def finish(place, tokens, far_tok, middle_back, left_back, right_back, w_qkv, gains, deps):
    rows, width = middle_back.shape
    parts = pl.BlockSpec((3, TILE, width // 2), lambda i, *_: (0, i, 0))
    return call(
        finish_kernel,
        (rows // TILE,),
        [place],
        [
            (tokens, own_rows(width)), (far_tok, far_rows(width)),
            (middle_back, row_block(width)), (left_back, parts), (right_back, parts),
            (w_qkv, whole(w_qkv.shape)), (gains, whole(gains.shape)),
        ],
        [
            (shape((rows // 2, width), BF16), near_rows(width)),
            (shape((rows // 2, width), BF16), far_rows(width)),
            (shape((8, width), F32), whole((8, width))),
        ],
        deps,
        "finish",
        15,
    )


def in_packs_kernel(place, own, got, out):
    @pl.when(pl.program_id(0) < 2)
    def _():
        out[0] = own[...]

    @pl.when(pl.program_id(0) >= 2)
    def _():
        out[0] = got[...]


def in_packs(place, own, got, deps):
    rows, width = own.shape

    def at(i, place):
        mine = i < 2
        return (jnp.where(mine, place[0], 1 - place[0]), jnp.where(mine, i, i - 2), 0)

    return call(
        in_packs_kernel,
        (2 * rows // TILE,),
        [place],
        [(own, near_rows(width)), (got, far_rows(width))],
        [(shape((2, rows, width), BF16), pl.BlockSpec((1, TILE, width), at))],
        deps,
        "in_packs",
        3,
    )[0]


def weight_grad_kernel(addend_count, place, left, right, *refs):
    addends = refs[:addend_count]
    outs = refs[addend_count:]
    step = pl.program_id(0)
    share = pl.num_programs(0) // len(outs)
    rights = [right[...]] if len(right.shape) == 2 else [right[p] for p in range(right.shape[0])]
    start = 0
    for piece in rights:
        cols = slice(start, start + piece.shape[1])
        start = cols.stop
        total = dot(left[...], piece, TN)
        for addend in addends:
            total = total + addend[:, cols].astype(F32)
        total = total.astype(BF16)
        if len(outs) == 1:
            outs[0][:, cols] = total
            continue
        for number, out in enumerate(outs):

            @pl.when(step // share == number)
            def _(out=out, cols=cols, total=total):
                out[:, cols] = total


def swap_wide(rows, bit):
    size = lax.axis_size("wide")
    return lax.ppermute(rows, "wide", [(i, i ^ bit) for i in range(size)])


def swap_narrow(rows):
    return lax.ppermute(rows, "narrow", [(0, 1), (1, 0)])


def pair_sum(mine, theirs):
    return (mine.astype(F32) + theirs.astype(F32)).astype(BF16)


def choose(which, bit):
    return jnp.where(which == 1, bit, 1 - bit)


class Reduction:
    def __init__(self, place, left, right, count, cols, row_of, right_of, us):
        self.place, self.left, self.right = place, left, right
        self.count, self.cols, self.us = count, cols, us
        self.row_of, self.right_of = row_of, right_of
        self.state = [None] * count

    def blocks(self, steps, block_of, addends, outs, deps):
        tokens = self.left.shape[0]
        row = lambda i, place: (0, self.row_of(*block_of(i, place)))
        if self.right.ndim == 2:
            right = pl.BlockSpec(
                (tokens, self.cols), lambda i, place: (0, self.right_of(*block_of(i, place)))
            )
        else:
            right = pl.BlockSpec(
                (3, tokens, self.cols // 3),
                lambda i, place: (0, 0, self.right_of(*block_of(i, place))),
            )
        share = steps // outs
        out = shape((share * TILE, self.cols), BF16)
        out_at = lambda number: pl.BlockSpec(
            (TILE, self.cols), lambda i, place: (jnp.clip(i - number * share, 0, share - 1), 0)
        )
        add_at = lambda at: pl.BlockSpec((TILE, self.cols), lambda i, place: (at(i), 0))
        return call(
            functools.partial(weight_grad_kernel, len(addends)),
            (steps,),
            [self.place],
            [(self.left, pl.BlockSpec((tokens, TILE), row)), (self.right, right)]
            + [(array, add_at(at)) for array, at in addends],
            [(out, out_at(number)) for number in range(outs)],
            deps,
            "weight_grad",
            1.5 + self.us * steps,
        )

    def far(self, deps):
        count = self.count

        def block_of(i, place):
            n, c, b = place[0], place[1], place[2]
            return choose(i // (2 * count), n), 1 - c, choose(i % 2, b), (i // 2) % count

        sent = self.blocks(4 * count, block_of, [], 1, deps)[0]
        self.from_core = swap_wide(sent, 1)
        return sent

    def give(self, deps):
        def block_of(i, place):
            n, c, b = place[0], place[1], place[2]
            return 1 - n, c, choose(i % 2, b), i // 2

        sent = self.blocks(
            2 * self.count, block_of, [(self.from_core, lambda i: i)], self.count, deps
        )
        for k, part in enumerate(sent):
            self.state[k] = swap_narrow(part)
        return sent[0]

    def keep(self, k, deps):
        count = self.count

        def block_of(i, place):
            n, c, b = place[0], place[1], place[2]
            return n, c, choose(i, b), k

        addends = [(self.from_core, lambda i: 2 * (count + k) + i), (self.state[k], lambda i: i)]
        sent, kept = self.blocks(2, block_of, addends, 2, deps)
        self.state[k] = (kept, swap_wide(sent, 2), 4)
        return sent

    def step(self, k, dep):
        mine, got, bit = self.state[k]
        total = pair_sum(mine, tie(got, dep))
        if bit < lax.axis_size("wide"):
            self.state[k] = (total, swap_wide(total, bit), 2 * bit)
        else:
            self.state[k] = [total, swap_wide(total, 2), swap_wide(total, 1)]
        return total

    def spread(self, k, dep):
        whole_y = tie(self.state[k][1], dep)
        self.state[k][1] = whole_y
        self.state[k].append(swap_wide(whole_y, 1))
        return whole_y

    def done_steps(self, k):
        return isinstance(self.state[k], list)


def gather_kernel(place, *refs):
    out = refs[-1]
    for number, piece in enumerate(refs[:-1]):

        @pl.when(pl.program_id(0) == number)
        def _(piece=piece):
            out[...] = piece[...].astype(F32)


def gather(place, pieces, dims, block_at, deps):
    flat = [piece for group in pieces for piece in group]
    rows, cols = flat[0].shape

    def at(i, place):
        c = jnp.where(i % 4 < 2, place[1], 1 - place[1])
        b = jnp.where(i % 2 == 0, place[2], 1 - place[2])
        return block_at(c, b, i // 4)

    return call(
        gather_kernel,
        (len(flat),),
        [place],
        [(piece, pl.BlockSpec((rows, cols), lambda i, *_: (0, 0))) for piece in flat],
        [(shape(dims, F32), pl.BlockSpec((rows, cols), at))],
        deps,
        "gather",
        1 + 0.7 * len(flat),
    )[0]


def gather_mixed_kernel(place, *refs):
    out = refs[-1]
    quarter = refs[0].shape[1] // 3
    for core in range(2):

        @pl.when((pl.program_id(0) == place[1]) == (core == 0))
        def _(core=core):
            for side in range(2):
                for other in range(2):
                    piece = refs[4 * side + 2 * core + other]
                    b = place[2] if other == 0 else 1 - place[2]
                    for part in range(3):
                        at = pl.multiple_of((4 * part + 2 * side + b) * quarter, quarter)
                        values = piece[:, part * quarter : (part + 1) * quarter]
                        out[:, pl.ds(at, quarter)] = values.astype(F32)


def gather_mixed(place, pieces, dims, deps):
    flat = [piece for group in pieces for piece in group]
    return call(
        gather_mixed_kernel,
        (2,),
        [place],
        [(piece, whole(piece.shape)) for piece in flat],
        [(shape(dims, F32), pl.BlockSpec((TILE, dims[1]), lambda i, *_: (i, 0)))],
        deps,
        "gather_mixed",
        5,
    )[0]


def local(tokens, doc_ids, w_qkv, w_out, w_up, w_down, norm_gains, norm_biases, cotangent):
    narrow_size = lax.axis_size("narrow")
    packs, tok_rows, width = tokens.shape
    assert narrow_size == 2 and packs == 2 and tok_rows == 2 * TILE
    pack_len = tok_rows * narrow_size
    ff = w_up.shape[1]
    n = lax.axis_index("narrow")
    w = lax.axis_index("wide")
    place = jnp.stack([n, w % 2, (w // 2) % 2]).astype(jnp.int32)
    pick = lambda array, index: lax.dynamic_index_in_dim(array, index, 0, keepdims=False)

    far_tok = swap_narrow(pick(tokens, 1 - n))
    doc_row = pick(doc_ids, n)
    many = (doc_row[pack_len - 1] != 0).astype(jnp.int32)
    block_at = jnp.stack([n, 3 - n, 1 - n, 2 + n]).astype(jnp.int32)
    info = jnp.concatenate([block_at, many[None]])

    halves = HEAD_DIM // 2
    frequency = jnp.exp(
        -math.log(10000.0) * jnp.arange(halves, dtype=F32) * 2.0 / HEAD_DIM
    )
    places = (block_at[:, None] * TILE + jnp.arange(TILE, dtype=jnp.int32)[None, :]).reshape(-1)
    angles_t = frequency[:, None] * places.astype(F32)[None, :]
    cos_t = jnp.cos(angles_t)
    sin_t = jnp.sin(angles_t)
    cos = cos_t.T
    sin = sin_t.T
    cosine = jnp.concatenate([cos] * 4, axis=1)
    sine = jnp.concatenate([-sin, sin, -sin, sin], axis=1)

    early = project(
        place, tokens, w_qkv, norm_gains, norm_biases, cosine, sine, 0, (), pack_len
    )
    far_cot = swap_narrow(tie(pick(cotangent, 1 - n), early[0]))
    normed, mixed = project(
        place, far_tok, w_qkv, norm_gains, norm_biases, cosine, sine, 2, early, pack_len
    )
    att, stats = attend(info, mixed)
    near_out, far_out, branch, normed2, active, back2, hidden_back, sums3 = feed(
        place, tokens, far_tok, cotangent, far_cot, att, w_out, w_up, w_down,
        norm_gains, norm_biases,
    )
    got_out = swap_narrow(far_out)

    reduce = functools.partial(Reduction, place)
    down = reduce(active, back2, 2, 1024, lambda x, c, b, k: 8 * x + 4 * c + 2 * b + k,
                  lambda x, c, b, k: 0, 0.8)
    up = reduce(normed2, hidden_back, 2, 1024, lambda x, c, b, k: 2 * x + c,
                lambda x, c, b, k: 2 * b + k, 0.8)
    last = down.far([])
    last = up.far([last])
    last = down.give([last])
    last = up.give([last])
    middle_back, branch_back, att_back, sums12 = return_pass(
        place, tokens, far_tok, cotangent, far_cot, branch, hidden_back, w_out, w_up,
        norm_gains, norm_biases, [last],
    )
    proj = reduce(att, branch_back, 1, 512, lambda x, c, b, k: 2 * x + c, lambda x, c, b, k: b, 0.5)
    a = proj.far([])
    b = down.keep(0, [a])
    left_back = attend_back(info, mixed, att, att_back, stats, cos_t, sin_t, 0, [b])
    qkv = [reduce(normed, left_back, 1, 768, lambda x, c, b, k: 2 * x + c, lambda x, c, b, k: b, 0.7)]
    a = qkv[0].far([])
    b = down.keep(1, [a])
    d = proj.give([b])
    e = down.step(0, d)
    right_back = attend_back(info, mixed, att, att_back, stats, cos_t, sin_t, 1, [d, e])
    qkv.append(
        reduce(normed, right_back, 1, 768, lambda x, c, b, k: 2 * x + c, lambda x, c, b, k: b, 0.7)
    )
    a = qkv[1].far([])
    b = qkv[0].give([a])
    d = up.keep(0, [b])
    e = down.step(1, d)
    f = down.step(0, e)
    near_grad, far_grad, sums0 = finish(
        place, tokens, far_tok, middle_back, left_back, right_back, w_qkv, norm_gains, [d, f]
    )
    a = qkv[1].give([near_grad])
    got_grad = swap_narrow(tie(far_grad, a))
    norm_term = jnp.concatenate(
        [sums0[0:1], sums12[0:1], sums12[2:3], sums3[0:1],
         sums0[1:2], sums12[1:2], sums12[3:4], sums3[1:2]], axis=0
    )
    norm_term = norm_term + swap_narrow(norm_term)
    a = up.keep(1, [a])
    out = in_packs(place, near_out, got_out, [a])
    last = proj.keep(0, [a])
    bit = 1
    chunks = [(down, 0), (down, 1), (up, 0), (up, 1), (proj, 0)]
    mixed_chunks = [(qkv[0], 0), (qkv[1], 0)]
    waiting = list(mixed_chunks)
    while chunks:
        later = []
        for red, k in chunks:
            if red.done_steps(k):
                last = red.spread(k, last)
            else:
                last = red.step(k, last)
                later.append((red, k))
        chunks = later
        if bit < lax.axis_size("wide"):
            norm_term = norm_term + swap_wide(norm_term, bit)
            bit *= 2
        if waiting:
            red, k = waiting.pop(0)
            last = red.keep(k, [last])
            chunks.append((red, k))
    while bit < lax.axis_size("wide"):
        norm_term = norm_term + swap_wide(norm_term, bit)
        bit *= 2
    grad_down = gather(
        place, down.state, (ff // 2, width), lambda c, b, k: (4 * c + 2 * b + k, 0), []
    )
    grad_up = gather(place, up.state, (width // 2, ff), lambda c, b, k: (c, 2 * b + k), [])
    grad_out_proj = gather(place, proj.state, (width // 2, width), lambda c, b, k: (c, b), [])
    grad_qkv = gather_mixed(
        place, [qkv[0].state[0], qkv[1].state[0]], (width // 2, 3 * width), []
    )
    grad_tok = in_packs(place, near_grad, got_grad, [])
    norm_term = lax.dynamic_slice_in_dim(norm_term, n * (width // 2), width // 2, 1)
    return (
        out,
        grad_tok,
        grad_qkv,
        grad_out_proj,
        grad_up,
        grad_down,
        norm_term[:4],
        norm_term[4:],
    )


def solution(mesh):
    rows = P("wide", "narrow", None)
    return jax.shard_map(
        local,
        mesh=mesh,
        in_specs=(rows, P("wide", None), P(), P(), P(), P(), P(), P(), rows),
        out_specs=(
            rows, rows,
            P("narrow", None), P("narrow", None), P("narrow", None), P("narrow", None),
            P(None, "narrow"), P(None, "narrow"),
        ),
        check_vma=False,
    )
```

```python
import functools
import math

import jax
import jax.numpy as jnp
from jax import lax
from jax.experimental import pallas as pl
from jax.experimental.pallas import tpu as pltpu
from jax.sharding import PartitionSpec as P

HEAD_DIM = 64
EPS = 1e-05
F32 = jnp.float32
BF16 = jnp.bfloat16
TILE = 256
GROUP = 256
VMEM_LIMIT = 60 * 1024 * 1024
FLOPS_PER_US = 1000000000
NN = (((1,), (0,)), ((), ()))
NT = (((1,), (1,)), ((), ()))
TN = (((0,), (0,)), ((), ()))


def dot(left, right, dims=NN):
    return lax.dot_general(left, right, dims, preferred_element_type=F32)


def call(kernel, grid, prefetch, inputs, outputs, deps, name, us, scratch=(), aliases=None):
    given = len(prefetch) + len(inputs)

    def body(*refs):
        kernel(*refs[:given], *refs[given + len(deps) :])

    in_specs = [spec for _, spec in inputs] + [pl.BlockSpec(memory_space=pl.ANY)] * len(deps)
    return pl.pallas_call(
        body,
        grid_spec=pltpu.PrefetchScalarGridSpec(
            num_scalar_prefetch=len(prefetch),
            grid=grid,
            in_specs=in_specs,
            out_specs=tuple(spec for _, spec in outputs),
            scratch_shapes=list(scratch),
        ),
        out_shape=tuple(shape for shape, _ in outputs),
        input_output_aliases=aliases or {},
        compiler_params=pltpu.CompilerParams(vmem_limit_bytes=VMEM_LIMIT),
        cost_estimate=pl.CostEstimate(
            flops=int(us * FLOPS_PER_US), transcendentals=0, bytes_accessed=1
        ),
        name=name,
    )(*prefetch, *[array for array, _ in inputs], *deps)


def shape(dims, dtype):
    return jax.ShapeDtypeStruct(dims, dtype)


def whole(dims):
    return pl.BlockSpec(dims, lambda *_: (0,) * len(dims), pipeline_mode=pl.Buffered(1))


def row_block(size):
    return pl.BlockSpec((TILE, size), lambda i, *_: (i, 0))


def own_rows(size):
    return pl.BlockSpec((1, TILE, size), lambda i, place, *_: (place[0], jnp.minimum(i, 1), 0))


def far_rows(size):
    return pl.BlockSpec((TILE, size), lambda i, *_: (jnp.maximum(i - 2, 0), 0))


def pick_rows(own, far):
    return jnp.where(pl.program_id(0) < 2, own[0].astype(F32), far[...].astype(F32))


def put_rows(near, far, rows):
    @pl.when(pl.program_id(0) < 2)
    def _():
        near[0] = rows

    @pl.when(pl.program_id(0) >= 2)
    def _():
        far[...] = rows


def tie(array, *deps):
    return lax.optimization_barrier((array,) + deps)[0]


def norm_parts(rows):
    centre = rows - jnp.mean(rows, axis=-1, keepdims=True)
    rstd = lax.rsqrt(jnp.mean(centre * centre, axis=-1, keepdims=True) + EPS)
    return centre * rstd, rstd


def norm_back(unit, rstd, gain, grad):
    scaled = grad * gain
    first = jnp.mean(scaled, axis=-1, keepdims=True)
    second = jnp.mean(scaled * unit, axis=-1, keepdims=True)
    return rstd * (scaled - first - unit * second)


def token_sum(rows):
    return jnp.sum(rows, axis=0, keepdims=True)


def project_kernel(place, tok, w, gains, biases, cosine, sine, normed_out, mixed_out):
    rows = tok[0] if len(tok.shape) == 3 else tok[...]
    unit, _ = norm_parts(rows.astype(F32))
    normed = (unit * gains[0:1, :] + biases[0:1, :]).astype(BF16)
    normed_out[...] = normed
    width = normed.shape[1]
    lanes = lax.broadcasted_iota(jnp.int32, (TILE, 128), 1)
    first_half = lanes % HEAD_DIM < HEAD_DIM // 2
    scale = 1.0 / math.sqrt(HEAD_DIM)
    cos = cosine[...]
    sin = sine[...]
    for start in range(0, 3 * width, 256):
        part = dot(normed, w[:, start : start + 256])
        if start >= 2 * width:
            mixed_out[:, start : start + 256] = part.astype(BF16)
            continue
        for sub in range(0, 256, 128):
            u = part[:, sub : sub + 128]
            turned = jnp.where(first_half, pltpu.roll(u, 96, 1), pltpu.roll(u, 32, 1))
            out = u * cos + turned * sin
            out = out.astype(BF16)
            if start < width:
                out = out * jnp.asarray(scale, BF16)
            mixed_out[:, start + sub : start + sub + 128] = out


def project(place, tok, w_qkv, gains, biases, cosine, sine, first_block, earlier, pack_len):
    width, wide = w_qkv.shape
    steps = tok.shape[-2] // TILE
    at = lambda size: pl.BlockSpec((TILE, size), lambda i, *_: (i + first_block, 0))
    own = tok.ndim == 3
    return call(
        project_kernel,
        (steps,),
        [place],
        [
            (tok, own_rows(width) if own else row_block(width)),
            (w_qkv, whole(w_qkv.shape)),
            (gains, whole(gains.shape)),
            (biases, whole(biases.shape)),
            (cosine, at(128)),
            (sine, at(128)),
        ],
        [
            (shape((pack_len, width), BF16), at(width)),
            (shape((pack_len, wide), BF16), at(wide)),
        ],
        list(earlier),
        "project",
        8,
        aliases={7: 0, 8: 1} if earlier else None,
    )


def diagonal_mask(scores):
    size = scores.shape[1]
    first = scores.shape[0] - size
    keys = lax.broadcasted_iota(jnp.int32, (size, size), 0)
    asks = lax.broadcasted_iota(jnp.int32, (size, size), 1)
    tail = jnp.where(keys <= asks, scores[first:], -1e30)
    if first == 0:
        return tail
    return jnp.concatenate([scores[:first], tail], axis=0)


def attend_kernel(info, q, k, v, out, stats, key_heads, q_t, v_t, out_t):
    heads = GROUP // HEAD_DIM
    blocks = q.shape[0] // TILE
    for i in range(blocks):
        rows = slice(i * TILE, (i + 1) * TILE)
        at = pl.multiple_of(info[i] * TILE, TILE)
        q_t[:, pl.ds(at, TILE)] = q[rows, :].T
        v_t[:, pl.ds(at, TILE)] = v[rows, :].T
        for h in range(heads):
            key_heads[h, pl.ds(at, TILE), :] = k[rows, h * HEAD_DIM : (h + 1) * HEAD_DIM]

    def one_head(h, first_key):
        head_rows = pl.ds(pl.multiple_of(h * HEAD_DIM, HEAD_DIM), HEAD_DIM)
        for block in range(blocks):
            cols = slice(block * TILE, (block + 1) * TILE)
            keys = slice(first_key(block), (block + 1) * TILE)
            scores = diagonal_mask(dot(key_heads[h, keys, :], q_t[head_rows, cols]))
            peak = jnp.max(scores, axis=0, keepdims=True)
            weights = jnp.exp(scores - peak)
            total = jnp.sum(weights, axis=0, keepdims=True)
            mixed = dot(v_t[head_rows, keys], weights.astype(BF16))
            out_t[head_rows, cols] = mixed * (1.0 / total)
            stats[0, pl.ds(h, 1), cols] = peak + jnp.log(total)

    many = info[blocks] != 0

    @pl.when(jnp.logical_not(many))
    def _():
        @pl.loop(0, heads)
        def _(h):
            one_head(h, lambda block: 0)

    @pl.when(many)
    def _():
        @pl.loop(0, heads)
        def _(h):
            one_head(h, lambda block: block * TILE)

    for i in range(blocks):
        at = pl.multiple_of(info[i] * TILE, TILE)
        out[i * TILE : (i + 1) * TILE, :] = out_t[:, pl.ds(at, TILE)].T.astype(BF16)


def attend(info, mixed):
    rows, wide = mixed.shape
    width = wide // 3
    groups = width // GROUP
    heads = GROUP // HEAD_DIM
    part = lambda shift: pl.BlockSpec((rows, GROUP), lambda g, s: (0, g + shift * groups))
    return call(
        attend_kernel,
        (groups,),
        [info],
        [(mixed, part(0)), (mixed, part(1)), (mixed, part(2))],
        [
            (shape((rows, width), BF16), part(0)),
            (
                shape((groups, heads, rows), F32),
                pl.BlockSpec((1, heads, rows), lambda g, s: (g, 0, 0)),
            ),
        ],
        [],
        "attend",
        36,
        scratch=[
            pltpu.VMEM((heads, rows, HEAD_DIM), BF16),
            pltpu.VMEM((GROUP, rows), BF16),
            pltpu.VMEM((GROUP, rows), BF16),
            pltpu.VMEM((GROUP, rows), F32),
        ],
    )


def feed_kernel(place, own_tok, far_tok, own_cot, far_cot, att, w_out, w_up, w_down, gains, biases,
                near_out, far_out, branch_out, normed2_out, active_out, back2_out, hidden_back_out, sums,
                slope):
    chunk = 1024
    residual = pick_rows(own_tok, far_tok)
    branch = dot(att[...], w_out[...])
    branch_out[...] = branch
    unit1, _ = norm_parts(branch)
    middle = residual + unit1 * gains[1:2, :] + biases[1:2, :]
    unit2, _ = norm_parts(middle)
    normed2 = (unit2 * gains[2:3, :] + biases[2:3, :]).astype(BF16)
    normed2_out[...] = normed2
    ff = w_up.shape[1]
    root = math.sqrt(2.0 / math.pi)
    branch2 = jnp.zeros_like(branch)
    for start in range(0, ff, chunk):
        cols = slice(start, start + chunk)
        z = dot(normed2, w_up[:, cols])
        square = z * z
        bend = jnp.tanh(z * (root + (root * 0.044715) * square))
        half = 0.5 + 0.5 * bend
        active = (z * half).astype(BF16)
        active_out[:, cols] = active
        inner = (0.5 * root) + (1.5 * root * 0.044715) * square
        slope[:, cols] = half + z * (1.0 - bend * bend) * inner
        branch2 = branch2 + dot(active, w_down[cols, :])
    unit3, rstd3 = norm_parts(branch2)
    put_rows(near_out, far_out, (middle + unit3 * gains[3:4, :] + biases[3:4, :]).astype(BF16))
    upstream = pick_rows(own_cot, far_cot)
    back2 = norm_back(unit3, rstd3, gains[3:4, :], upstream).astype(BF16)
    back2_out[...] = back2

    @pl.when(pl.program_id(0) == 0)
    def _():
        sums[...] = jnp.zeros_like(sums)

    sums[0:1, :] += token_sum(upstream * unit3)
    sums[1:2, :] += token_sum(upstream)
    for start in range(0, ff, chunk):
        cols = slice(start, start + chunk)
        grad_active = dot(back2, w_down[cols, :], NT)
        hidden_back_out[:, cols] = (grad_active * slope[:, cols]).astype(BF16)


def feed(place, tokens, far_tok, cotangent, far_cot, att, w_out, w_up, w_down, gains, biases):
    rows, width = att.shape
    ff = w_up.shape[1]
    return call(
        feed_kernel,
        (rows // TILE,),
        [place],
        [
            (tokens, own_rows(width)), (far_tok, far_rows(width)),
            (cotangent, own_rows(width)), (far_cot, far_rows(width)),
            (att, row_block(width)),
            (w_out, whole(w_out.shape)), (w_up, whole(w_up.shape)), (w_down, whole(w_down.shape)),
            (gains, whole(gains.shape)), (biases, whole(biases.shape)),
        ],
        [
            (shape((2, rows // 2, width), BF16), own_rows(width)),
            (shape((rows // 2, width), BF16), far_rows(width)),
            (shape((rows, width), F32), row_block(width)),
            (shape((rows, width), BF16), row_block(width)),
            (shape((rows, ff), BF16), row_block(ff)),
            (shape((rows, width), BF16), row_block(width)),
            (shape((rows, ff), BF16), row_block(ff)),
            (shape((8, width), F32), whole((8, width))),
        ],
        [],
        "feed",
        49,
        scratch=[pltpu.VMEM((TILE, ff), F32)],
    )


def return_kernel(place, own_tok, far_tok, own_cot, far_cot, branch, hidden_back, w_out, w_up, gains, biases,
                  middle_back_out, branch_back_out, att_back_out, sums):
    unit1, rstd1 = norm_parts(branch[...])
    middle = pick_rows(own_tok, far_tok) + unit1 * gains[1:2, :] + biases[1:2, :]
    unit2, rstd2 = norm_parts(middle)
    grad2 = dot(hidden_back[...], w_up[...], NT)
    middle_back = pick_rows(own_cot, far_cot) + norm_back(unit2, rstd2, gains[2:3, :], grad2)
    middle_back_out[...] = middle_back
    branch_back = norm_back(unit1, rstd1, gains[1:2, :], middle_back).astype(BF16)
    branch_back_out[...] = branch_back
    att_back_out[...] = dot(branch_back, w_out[...], NT).astype(BF16)

    @pl.when(pl.program_id(0) == 0)
    def _():
        sums[...] = jnp.zeros_like(sums)

    sums[0:1, :] += token_sum(middle_back * unit1)
    sums[1:2, :] += token_sum(middle_back)
    sums[2:3, :] += token_sum(grad2 * unit2)
    sums[3:4, :] += token_sum(grad2)


def return_pass(place, tokens, far_tok, cotangent, far_cot, branch, hidden_back, w_out, w_up,
                gains, biases, deps):
    rows, width = branch.shape
    ff = w_up.shape[1]
    return call(
        return_kernel,
        (rows // TILE,),
        [place],
        [
            (tokens, own_rows(width)), (far_tok, far_rows(width)),
            (cotangent, own_rows(width)), (far_cot, far_rows(width)),
            (branch, row_block(width)), (hidden_back, row_block(ff)),
            (w_out, whole(w_out.shape)), (w_up, whole(w_up.shape)),
            (gains, whole(gains.shape)), (biases, whole(biases.shape)),
        ],
        [
            (shape((rows, width), F32), row_block(width)),
            (shape((rows, width), BF16), row_block(width)),
            (shape((rows, width), BF16), row_block(width)),
            (shape((8, width), F32), whole((8, width))),
        ],
        deps,
        "return_pass",
        24,
    )


def attend_back_kernel(info, q, k, v, att, grad, stats, cos_t, sin_t, back,
                       q_heads, k_heads, v_heads, g_heads, q_t, k_t, g_t, inner, q_acc, k_acc, v_acc):
    heads = GROUP // HEAD_DIM
    half = HEAD_DIM // 2
    blocks = q.shape[0] // TILE
    rows_all = blocks * TILE
    for i in range(blocks):
        rows = slice(i * TILE, (i + 1) * TILE)
        at = pl.multiple_of(info[i] * TILE, TILE)
        spot = pl.ds(at, TILE)
        q_t[:, spot] = q[rows, :].T
        k_t[:, spot] = k[rows, :].T
        grad_t = grad[rows, :].T
        g_t[:, spot] = grad_t
        product = att[rows, :].T.astype(F32) * grad_t.astype(F32)
        for h in range(heads):
            lanes = slice(h * HEAD_DIM, (h + 1) * HEAD_DIM)
            q_heads[h, spot, :] = q[rows, lanes]
            k_heads[h, spot, :] = k[rows, lanes]
            v_heads[h, spot, :] = v[rows, lanes]
            g_heads[h, spot, :] = grad[rows, lanes]
            inner[pl.ds(h, 1), spot] = jnp.sum(product[lanes, :], axis=0, keepdims=True)

    def one_head(h, last_ask):
        head_rows = pl.ds(pl.multiple_of(h * HEAD_DIM, HEAD_DIM), HEAD_DIM)
        for block in range(blocks):
            keys = slice(block * TILE, (block + 1) * TILE)
            cols = slice(block * TILE, last_ask(block))
            scores = dot(k_heads[h, keys, :], q_t[head_rows, cols])
            low = scores[:, :TILE]
            keys_at = lax.broadcasted_iota(jnp.int32, (TILE, TILE), 0)
            asks_at = lax.broadcasted_iota(jnp.int32, (TILE, TILE), 1)
            low = jnp.where(keys_at <= asks_at, low, -1e30)
            if scores.shape[1] > TILE:
                scores = jnp.concatenate([low, scores[:, TILE:]], axis=1)
            else:
                scores = low
            weights = jnp.exp(scores - stats[0, pl.ds(h, 1), cols])
            weight_back = dot(v_heads[h, keys, :], g_t[head_rows, cols])
            score_back = (weights * (weight_back - inner[pl.ds(h, 1), cols])).astype(BF16)
            v_acc[h, keys, :] = dot(weights.astype(BF16), g_heads[h, cols, :])
            k_acc[h, keys, :] = dot(score_back, q_heads[h, cols, :])
            change = dot(k_t[head_rows, keys], score_back)
            if block == 0:
                q_acc[head_rows, cols] = change
            elif last_ask(0) < rows_all:
                q_acc[head_rows, cols] = change
            else:
                q_acc[head_rows, cols] += change

    many = info[blocks] != 0

    @pl.when(jnp.logical_not(many))
    def _():
        @pl.loop(0, heads)
        def _(h):
            one_head(h, lambda block: rows_all)

    @pl.when(many)
    def _():
        @pl.loop(0, heads)
        def _(h):
            one_head(h, lambda block: (block + 1) * TILE)

    scale = 1.0 / math.sqrt(HEAD_DIM)
    for i in range(blocks):
        rows = slice(i * TILE, (i + 1) * TILE)
        spot = pl.ds(pl.multiple_of(info[i] * TILE, TILE), TILE)
        cos = cos_t[:, rows]
        sin = sin_t[:, rows]

        def turn_back(parts, factor):
            turned = []
            for part in parts:
                first, second = part[:half], part[half:]
                turned.append(first * cos + second * sin)
                turned.append(second * cos - first * sin)
            return (jnp.concatenate(turned, axis=0) * factor).T.astype(BF16)

        back[0, rows, :] = turn_back(
            [q_acc[h * HEAD_DIM : (h + 1) * HEAD_DIM, spot] for h in range(heads)], scale
        )
        back[1, rows, :] = turn_back([k_acc[h, spot, :].T for h in range(heads)], 1.0)
        back[2, rows, :] = jnp.concatenate(
            [v_acc[h, spot, :] for h in range(heads)], axis=1
        ).astype(BF16)


def attend_back(info, mixed, att, grad, stats, cos_t, sin_t, half, deps):
    rows, wide = mixed.shape
    width = wide // 3
    groups = width // GROUP
    heads = GROUP // HEAD_DIM
    first = half * (groups // 2)
    spec = lambda shift: pl.BlockSpec((rows, GROUP), lambda g, s: (0, g + first + shift * groups))
    per_head = pltpu.VMEM((heads, rows, HEAD_DIM), BF16)
    turned = pltpu.VMEM((GROUP, rows), BF16)
    angles = pl.BlockSpec((HEAD_DIM // 2, rows), lambda g, s: (0, 0))
    return call(
        attend_back_kernel,
        (groups // 2,),
        [info],
        [
            (mixed, spec(0)), (mixed, spec(1)), (mixed, spec(2)), (att, spec(0)), (grad, spec(0)),
            (stats, pl.BlockSpec((1, heads, rows), lambda g, s: (g + first, 0, 0))),
            (cos_t, angles), (sin_t, angles),
        ],
        [
            (
                shape((3, rows, width // 2), BF16),
                pl.BlockSpec((3, rows, GROUP), lambda g, s: (0, 0, g)),
            ),
        ],
        deps,
        "attend_back",
        22,
        scratch=[
            per_head, per_head, per_head, per_head,
            turned, turned, turned,
            pltpu.VMEM((8, rows), F32),
            pltpu.VMEM((GROUP, rows), F32),
            pltpu.VMEM((heads, rows, HEAD_DIM), F32),
            pltpu.VMEM((heads, rows, HEAD_DIM), F32),
        ],
    )[0]


def finish_kernel(place, own_tok, far_tok, middle_back, left_back, right_back, w_qkv, gains,
                  near_out, far_out, sums):
    half = left_back.shape[2]
    unit, rstd = norm_parts(pick_rows(own_tok, far_tok))
    grad = None
    for part in range(3):
        for side, back in enumerate((left_back, right_back)):
            start = (2 * part + side) * half
            term = dot(back[part], w_qkv[:, start : start + half], NT)
            grad = term if grad is None else grad + term
    back = middle_back[...] + norm_back(unit, rstd, gains[0:1, :], grad)
    put_rows(near_out, far_out, back.astype(BF16))

    @pl.when(pl.program_id(0) == 0)
    def _():
        sums[...] = jnp.zeros_like(sums)

    sums[0:1, :] += token_sum(grad * unit)
    sums[1:2, :] += token_sum(grad)


def finish(place, tokens, far_tok, middle_back, left_back, right_back, w_qkv, gains, deps):
    rows, width = middle_back.shape
    parts = pl.BlockSpec((3, TILE, width // 2), lambda i, *_: (0, i, 0))
    return call(
        finish_kernel,
        (rows // TILE,),
        [place],
        [
            (tokens, own_rows(width)), (far_tok, far_rows(width)),
            (middle_back, row_block(width)), (left_back, parts), (right_back, parts),
            (w_qkv, whole(w_qkv.shape)), (gains, whole(gains.shape)),
        ],
        [
            (shape((2, rows // 2, width), BF16), own_rows(width)),
            (shape((rows // 2, width), BF16), far_rows(width)),
            (shape((8, width), F32), whole((8, width))),
        ],
        deps,
        "finish",
        15,
    )


def weight_grad_kernel(source_count, place, *refs):
    out = refs[-1]
    addends = refs[2 * source_count : -1]
    start = 0
    for number in range(source_count):
        left, right = refs[2 * number], refs[2 * number + 1]
        rights = [right] if len(right.shape) == 2 else [right.at[p] for p in range(3)]
        for piece in rights:
            cols = slice(start, start + piece.shape[1])
            start = cols.stop
            total = dot(left[...], piece[...], TN)
            for addend in addends:
                total = total + addend[:, cols].astype(F32)
            out[:, cols] = total.astype(BF16)


def swap_wide(rows, bit):
    size = lax.axis_size("wide")
    return lax.ppermute(rows, "wide", [(i, i ^ bit) for i in range(size)])


def swap_narrow(rows):
    return lax.ppermute(rows, "narrow", [(0, 1), (1, 0)])


def swap_crossed(rows, first):
    pairs = []
    for i in range(lax.axis_size("wide")):
        for n in range(2):
            along_x = (i % 2 == 0) == first
            peer = (i, 1 - n) if along_x else (i ^ 2, n)
            pairs.append((2 * i + n, 2 * peer[0] + peer[1]))
    return lax.ppermute(rows, ("wide", "narrow"), pairs)


def swap_two(rows, even_bit, odd_bit):
    size = lax.axis_size("wide")
    return lax.ppermute(
        rows, "wide", [(i, i ^ (even_bit if i % 2 == 0 else odd_bit)) for i in range(size)]
    )


def pair_sum(mine, theirs):
    return (mine.astype(F32) + theirs.astype(F32)).astype(BF16)


def choose(which, bit):
    return jnp.where(which == 1, bit, 1 - bit)


class Reduction:
    def __init__(self, place, sources, rows, cols, halves, us):
        self.place, self.sources = place, sources
        self.rows, self.cols, self.halves, self.us = rows, cols, halves, us
        self.bits = []
        bit = 4
        while bit < lax.axis_size("wide"):
            self.bits.append(bit)
            bit *= 2

    def blocks(self, steps, core_of, pair_of, addends, deps):
        tokens = self.sources[0][0].shape[0]

        def at(place_of):
            def index(i, h, place):
                core = core_of(place)
                first, second = pair_of(i, place)
                x = jnp.where(core == 0, first, second)
                b = jnp.where(core == 0, second, first)
                return place_of(x, core, b, h)

            return index

        inputs = []
        for left, left_of, right, right_of, width in self.sources:
            inputs.append((left, pl.BlockSpec((tokens, self.rows), at(left_of))))
            dims = (tokens, width) if right.ndim == 2 else (3, tokens, width)
            inputs.append((right, pl.BlockSpec(dims, at(right_of))))
        block = (self.rows, self.cols // self.halves)
        for array, row in addends:
            inputs.append((array, pl.BlockSpec(block, lambda i, h, place, row=row: (row(i), h))))
        return call(
            functools.partial(weight_grad_kernel, len(self.sources)),
            (steps, self.halves),
            [self.place],
            inputs,
            [
                (
                    shape((steps * self.rows, self.cols), BF16),
                    pl.BlockSpec(block, lambda i, h, place: (i, h)),
                )
            ],
            deps,
            "weight_grad",
            0.5 + 0.3 * self.us * steps,
        )[0]

    def far(self, deps):
        pair_of = lambda i, place: (choose(i // 2, place[4]), choose(i % 2, place[3]))
        sent = self.blocks(4, lambda place: 1 - place[1], pair_of, [], deps)
        self.core = swap_wide(sent, 1)
        return sent

    def first(self, deps):
        pair_of = lambda i, place: (1 - place[3], choose(i, place[4]))
        sent = self.blocks(2, lambda place: place[1], pair_of, [(self.core, lambda i: i)], deps)
        self.near = swap_crossed(sent, True)
        return sent

    def second(self, deps):
        pair_of = lambda i, place: (place[3], 1 - place[4])
        addends = [(self.core, lambda i: 2), (self.near, lambda i: 0)]
        sent = self.blocks(1, lambda place: place[1], pair_of, addends, deps)
        self.side = swap_crossed(sent, False)
        return sent

    def keep(self, deps):
        pair_of = lambda i, place: (place[3], place[4])
        addends = [(self.core, lambda i: 3), (self.near, lambda i: 1), (self.side, lambda i: 0)]
        self.total = self.blocks(1, lambda place: place[1], pair_of, addends, deps)
        self.hop = 0
        self.send()
        return self.total

    def send(self):
        self.got = swap_two(self.total, self.bits[self.hop], self.bits[-1 - self.hop])
        self.hop += 1

    def step(self, dep):
        self.total = pair_sum(self.total, tie(self.got, dep))
        if self.hop < len(self.bits):
            self.send()
        else:
            self.from_y = swap_wide(self.total, 2)
            self.from_core = swap_wide(self.total, 1)
        return self.total

    def spread(self, dep):
        self.from_y = tie(self.from_y, dep)
        self.from_both = swap_wide(self.from_y, 1)
        return self.from_y

    def pieces(self):
        return [self.total, self.from_y, self.from_core, self.from_both]


def gather_kernel(place, *refs):
    out = refs[-1]
    for number, piece in enumerate(refs[:4]):

        @pl.when(pl.program_id(0) == number)
        def _(piece=piece):
            out[...] = piece[...].astype(F32)


def piece_owner(number, place):
    c = jnp.where(number < 2, place[1], 1 - place[1])
    b = jnp.where(number % 2 == 0, place[2], 1 - place[2])
    return c, b


def gather(place, pieces, dims, cols, first, parts, block_at, deps):
    rows = pieces[0].shape[0]

    def part_of(number):
        def index(i, h, place):
            turn = jnp.where(i == number, h, jnp.where(i < number, 0, parts - 1))
            return (0, first + turn)

        return pl.BlockSpec((rows, cols), index)

    return call(
        gather_kernel,
        (4, parts),
        [place],
        [(piece, part_of(number)) for number, piece in enumerate(pieces)],
        [
            (
                shape(dims, F32),
                pl.BlockSpec(
                    (rows, cols), lambda i, h, place: block_at(*piece_owner(i, place), h)
                ),
            )
        ],
        deps,
        "gather",
        6,
    )[0]


def gather_mixed_kernel(place, *refs):
    out = refs[-1]
    quarter = refs[0].shape[1]
    mine = pl.program_id(0) == place[1]
    for core in range(2):

        @pl.when(mine == (core == 0))
        def _(core=core):
            for other in range(2):
                b = place[2] if other == 0 else 1 - place[2]
                at = pl.multiple_of(b * quarter, quarter)
                out[:, pl.ds(at, quarter)] = refs[2 * core + other][...].astype(F32)


def gather_mixed(place, pieces, dims, half, earlier, deps):
    piece = pl.BlockSpec((TILE, TILE), lambda i, p, place: (0, p))
    return call(
        gather_mixed_kernel,
        (2, 3),
        [place],
        [(array, piece) for array in pieces],
        [
            (
                shape(dims, F32),
                pl.BlockSpec((TILE, 2 * TILE), lambda i, p, place: (i, 2 * p + half)),
            )
        ],
        earlier + deps,
        "gather_mixed",
        4,
        aliases={5: 0} if earlier else None,
    )[0]


def local(tokens, doc_ids, w_qkv, w_out, w_up, w_down, norm_gains, norm_biases, cotangent):
    narrow_size = lax.axis_size("narrow")
    packs, tok_rows, width = tokens.shape
    assert narrow_size == 2 and packs == 2 and tok_rows == 2 * TILE
    pack_len = tok_rows * narrow_size
    ff = w_up.shape[1]
    n = lax.axis_index("narrow")
    w = lax.axis_index("wide")
    core = w % 2
    side = (w // 2) % 2
    place = jnp.stack(
        [n, core, side, jnp.where(core == 0, n, side), jnp.where(core == 0, side, n)]
    ).astype(jnp.int32)
    pick = lambda array, index: lax.dynamic_index_in_dim(array, index, 0, keepdims=False)

    far_tok = swap_narrow(pick(tokens, 1 - n))
    doc_row = pick(doc_ids, n)
    many = (doc_row[pack_len - 1] != 0).astype(jnp.int32)
    block_at = jnp.stack([n, 3 - n, 1 - n, 2 + n]).astype(jnp.int32)
    info = jnp.concatenate([block_at, many[None]])

    halves = HEAD_DIM // 2
    frequency = jnp.exp(
        -math.log(10000.0) * jnp.arange(halves, dtype=F32) * 2.0 / HEAD_DIM
    )
    places = (block_at[:, None] * TILE + jnp.arange(TILE, dtype=jnp.int32)[None, :]).reshape(-1)
    angles_t = frequency[:, None] * places.astype(F32)[None, :]
    cos_t = jnp.cos(angles_t)
    sin_t = jnp.sin(angles_t)
    cos = cos_t.T
    sin = sin_t.T
    cosine = jnp.concatenate([cos] * 4, axis=1)
    sine = jnp.concatenate([-sin, sin, -sin, sin], axis=1)

    early = project(
        place, tokens, w_qkv, norm_gains, norm_biases, cosine, sine, 0, (), pack_len
    )
    far_cot = swap_narrow(tie(pick(cotangent, 1 - n), early[0]))
    normed, mixed = project(
        place, far_tok, w_qkv, norm_gains, norm_biases, cosine, sine, 2, early, pack_len
    )
    att, stats = attend(info, mixed)
    near_out, far_out, branch, normed2, active, back2, hidden_back, sums3 = feed(
        place, tokens, far_tok, cotangent, far_cot, att, w_out, w_up, w_down,
        norm_gains, norm_biases,
    )
    got_out = swap_narrow(far_out)

    half_wide = width // 2
    down = Reduction(
        place,
        [(active, lambda x, c, b, h: (0, 4 * x + 2 * c + b),
          back2, lambda x, c, b, h: (0, h), half_wide)],
        2 * TILE, width, 2, 1.5,
    )
    up = Reduction(
        place,
        [(normed2, lambda x, c, b, h: (0, x),
          hidden_back, lambda x, c, b, h: (0, 2 * (2 * c + b) + h), half_wide)],
        2 * TILE, width, 2, 1.5,
    )
    last = down.far([])
    last = up.far([last])
    last = down.first([last])
    last = up.first([last])
    middle_back, branch_back, att_back, sums12 = return_pass(
        place, tokens, far_tok, cotangent, far_cot, branch, hidden_back, w_out, w_up,
        norm_gains, norm_biases, [last, got_out],
    )
    last = down.second([middle_back])
    left_back = attend_back(info, mixed, att, att_back, stats, cos_t, sin_t, 0, [last])
    by_rows = lambda x, c, b, h: (0, 2 * x + c)
    by_parts = lambda x, c, b, h: (0, 0, b)
    left = Reduction(
        place,
        [(normed, by_rows, left_back, by_parts, TILE),
         (att, by_rows, branch_back, lambda x, c, b, h: (0, b), half_wide)],
        TILE, 5 * TILE, 1, 1.2,
    )
    last = left.far([])
    last = down.keep([last])
    last = up.second([last])
    right_back = attend_back(info, mixed, att, att_back, stats, cos_t, sin_t, 1, [last])
    right = Reduction(
        place, [(normed, by_rows, right_back, by_parts, TILE)], TILE, 3 * TILE, 1, 0.8
    )
    last = right.far([])
    last = left.first([last])
    last = up.keep([last])
    a = down.step(last)
    near_grad, far_grad, sums0 = finish(
        place, tokens, far_tok, middle_back, left_back, right_back, w_qkv, norm_gains, [last, a]
    )
    last = right.first([near_grad])
    norm_term = jnp.concatenate(
        [sums0[0:1], sums12[0:1], sums12[2:3], sums3[0:1],
         sums0[1:2], sums12[1:2], sums12[3:4], sums3[1:2]], axis=0
    )
    norm_got = swap_narrow(tie(norm_term, last))
    hops = [2 ** bit for bit in range(lax.axis_size("wide").bit_length() - 1)]

    def norm_step(last):
        nonlocal norm_term, norm_got
        norm_term = norm_term + tie(norm_got, last)
        if hops:
            norm_got = swap_wide(norm_term, hops.pop(0))
        return norm_term

    late = left.second([last])
    out = lax.dynamic_update_slice(near_out, tie(got_out, late)[None], (1 - n, 0, 0))
    last = down.step(late)
    last = up.step(last)
    last = norm_step(last)
    last = right.second([last])
    last = left.keep([last])
    got_grad = swap_narrow(tie(far_grad, last))
    last = norm_step(last)
    last = right.keep([last])
    extra = len(left.bits) - 2
    for _ in range(extra):
        last = down.step(last)
        last = up.step(last)
    last = down.spread(last)
    last = norm_step(last)
    last = left.step(last)
    last = up.step(last)
    last = right.step(last)
    last = norm_step(last)
    for _ in range(extra):
        last = left.step(last)
        last = right.step(last)
    grad_down = gather(
        place, down.pieces(), (ff // 2, width), half_wide, 0, 2,
        lambda c, b, h: (2 * c + b, h), [last],
    )
    last = left.step(grad_down)
    last = right.step(last)
    while hops:
        last = norm_step(last)
    last = up.spread(last)
    last = norm_step(last)
    grad_tok = lax.dynamic_update_slice(near_grad, tie(got_grad, last)[None], (1 - n, 0, 0))
    grad_up = gather(
        place, up.pieces(), (half_wide, ff), half_wide, 0, 2,
        lambda c, b, h: (0, 2 * (2 * c + b) + h), [last],
    )
    last = left.spread(grad_up)
    last = right.spread(last)
    grad_out_proj = gather(
        place, left.pieces(), (half_wide, width), TILE, 3, 2,
        lambda c, b, h: (c, 2 * b + h), [last],
    )
    grad_qkv = gather_mixed(
        place, left.pieces(), (half_wide, 3 * width), 0, [], [grad_out_proj]
    )
    grad_qkv = gather_mixed(
        place, right.pieces(), (half_wide, 3 * width), 1, [grad_qkv], []
    )
    norm_term = lax.dynamic_slice_in_dim(norm_term, n * half_wide, half_wide, 1)
    return (
        out,
        grad_tok,
        grad_qkv,
        grad_out_proj,
        grad_up,
        grad_down,
        norm_term[:4],
        norm_term[4:],
    )


def solution(mesh):
    rows = P("wide", "narrow", None)
    return jax.shard_map(
        local,
        mesh=mesh,
        in_specs=(rows, P("wide", None), P(), P(), P(), P(), P(), P(), rows),
        out_specs=(
            rows, rows,
            P("narrow", None), P("narrow", None), P("narrow", None), P("narrow", None),
            P(None, "narrow"), P(None, "narrow"),
        ),
        check_vma=False,
    )
```

```python
import functools
import math

import jax
import jax.numpy as jnp
from jax import lax
from jax.experimental import pallas as pl
from jax.experimental.pallas import tpu as pltpu
from jax.sharding import PartitionSpec as P

HEAD_DIM = 64
EPS = 1e-05
F32 = jnp.float32
BF16 = jnp.bfloat16
TILE = 256
GROUP = 256
VMEM_LIMIT = 60 * 1024 * 1024
FLOPS_PER_US = 1000000000
NN = (((1,), (0,)), ((), ()))
NT = (((1,), (1,)), ((), ()))
TN = (((0,), (0,)), ((), ()))


def dot(left, right, dims=NN):
    return lax.dot_general(left, right, dims, preferred_element_type=F32)


def call(kernel, grid, prefetch, inputs, outputs, deps, name, us, scratch=(), aliases=None):
    given = len(prefetch) + len(inputs)

    def body(*refs):
        kernel(*refs[:given], *refs[given + len(deps) :])

    in_specs = [spec for _, spec in inputs] + [pl.BlockSpec(memory_space=pl.ANY)] * len(deps)
    return pl.pallas_call(
        body,
        grid_spec=pltpu.PrefetchScalarGridSpec(
            num_scalar_prefetch=len(prefetch),
            grid=grid,
            in_specs=in_specs,
            out_specs=tuple(spec for _, spec in outputs),
            scratch_shapes=list(scratch),
        ),
        out_shape=tuple(shape for shape, _ in outputs),
        input_output_aliases=aliases or {},
        compiler_params=pltpu.CompilerParams(vmem_limit_bytes=VMEM_LIMIT),
        cost_estimate=pl.CostEstimate(
            flops=int(us * FLOPS_PER_US), transcendentals=0, bytes_accessed=1
        ),
        name=name,
    )(*prefetch, *[array for array, _ in inputs], *deps)


def shape(dims, dtype):
    return jax.ShapeDtypeStruct(dims, dtype)


def whole(dims):
    return pl.BlockSpec(dims, lambda *_: (0,) * len(dims), pipeline_mode=pl.Buffered(1))


def row_block(size):
    return pl.BlockSpec((TILE, size), lambda i, *_: (i, 0))


def own_rows(size):
    return pl.BlockSpec((1, TILE, size), lambda i, place, *_: (place[0], jnp.minimum(i, 1), 0))


def far_rows(size):
    return pl.BlockSpec((TILE, size), lambda i, *_: (jnp.maximum(i - 2, 0), 0))


def pick_rows(own, far):
    return jnp.where(pl.program_id(0) < 2, own[0].astype(F32), far[...].astype(F32))


def put_rows(near, far, rows):
    @pl.when(pl.program_id(0) < 2)
    def _():
        near[0] = rows

    @pl.when(pl.program_id(0) >= 2)
    def _():
        far[...] = rows


class Stream:
    def __init__(self, sems, parts):
        self.copies = [
            pltpu.make_async_copy(source.at[:, cols], target.at[:, cols], sems.at[number])
            for number, (source, target, cols) in enumerate(parts)
        ]
        self.taken = 0

        @pl.when(pl.program_id(0) == 0)
        def _():
            for copy in self.copies:
                copy.start()

    def take(self, count):
        parts = self.copies[self.taken : self.taken + count]
        self.taken += count

        @pl.when(pl.program_id(0) == 0)
        def _():
            for copy in parts:
                copy.wait()


ANY = pl.BlockSpec(memory_space=pl.ANY)


def tie(array, *deps):
    return lax.optimization_barrier((array,) + deps)[0]


def norm_parts(rows):
    centre = rows - jnp.mean(rows, axis=-1, keepdims=True)
    rstd = lax.rsqrt(jnp.mean(centre * centre, axis=-1, keepdims=True) + EPS)
    return centre * rstd, rstd


def norm_back(unit, rstd, gain, grad):
    scaled = grad * gain
    first = jnp.mean(scaled, axis=-1, keepdims=True)
    second = jnp.mean(scaled * unit, axis=-1, keepdims=True)
    return rstd * (scaled - first - unit * second)


def token_sum(rows):
    return jnp.sum(rows, axis=0, keepdims=True)


def project_kernel(place, tok, w_far, gains, biases, cosine, sine, normed_out, mixed_out, w, sems):
    stream = Stream(sems, [(w_far, w, slice(at, at + 512)) for at in range(0, w.shape[1], 512)])
    rows = tok[0] if len(tok.shape) == 3 else tok[...]
    unit, _ = norm_parts(rows.astype(F32))
    normed = (unit * gains[0:1, :] + biases[0:1, :]).astype(BF16)
    normed_out[...] = normed
    width = normed.shape[1]
    lanes = lax.broadcasted_iota(jnp.int32, (TILE, 128), 1)
    first_half = lanes % HEAD_DIM < HEAD_DIM // 2
    scale = 1.0 / math.sqrt(HEAD_DIM)
    cos = cosine[...]
    sin = sine[...]
    for start in range(0, 3 * width, 256):
        if start in (0, 512, 1536):
            stream.take({0: 1, 512: 2, 1536: 3}[start])
        part = dot(normed, w[:, start : start + 256])
        if start >= 2 * width:
            mixed_out[:, start : start + 256] = part.astype(BF16)
            continue
        for sub in range(0, 256, 128):
            u = part[:, sub : sub + 128]
            turned = jnp.where(first_half, pltpu.roll(u, 96, 1), pltpu.roll(u, 32, 1))
            out = u * cos + turned * sin
            out = out.astype(BF16)
            if start < width:
                out = out * jnp.asarray(scale, BF16)
            mixed_out[:, start + sub : start + sub + 128] = out


def project(place, tok, w_qkv, gains, biases, cosine, sine, first_block, earlier, pack_len):
    width, wide = w_qkv.shape
    steps = tok.shape[-2] // TILE
    at = lambda size: pl.BlockSpec((TILE, size), lambda i, *_: (i + first_block, 0))
    own = tok.ndim == 3
    return call(
        project_kernel,
        (steps,),
        [place],
        [
            (tok, own_rows(width) if own else row_block(width)),
            (w_qkv, ANY),
            (gains, whole(gains.shape)),
            (biases, whole(biases.shape)),
            (cosine, at(128)),
            (sine, at(128)),
        ],
        [
            (shape((pack_len, width), BF16), at(width)),
            (shape((pack_len, wide), BF16), at(wide)),
        ],
        list(earlier),
        "project",
        8,
        scratch=[pltpu.VMEM(w_qkv.shape, BF16), pltpu.SemaphoreType.DMA((6,))],
        aliases={7: 0, 8: 1} if earlier else None,
    )


def diagonal_mask(scores):
    size = scores.shape[1]
    first = scores.shape[0] - size
    keys = lax.broadcasted_iota(jnp.int32, (size, size), 0)
    asks = lax.broadcasted_iota(jnp.int32, (size, size), 1)
    tail = jnp.where(keys <= asks, scores[first:], -1e30)
    if first == 0:
        return tail
    return jnp.concatenate([scores[:first], tail], axis=0)


def attend_kernel(info, q, k, v, out, stats, key_heads, q_t, v_t, out_t):
    heads = GROUP // HEAD_DIM
    blocks = q.shape[0] // TILE
    for i in range(blocks):
        rows = slice(i * TILE, (i + 1) * TILE)
        at = pl.multiple_of(info[i] * TILE, TILE)
        q_t[:, pl.ds(at, TILE)] = q[rows, :].T
        v_t[:, pl.ds(at, TILE)] = v[rows, :].T
        for h in range(heads):
            key_heads[h, pl.ds(at, TILE), :] = k[rows, h * HEAD_DIM : (h + 1) * HEAD_DIM]

    def one_head(h, first_key):
        head_rows = pl.ds(pl.multiple_of(h * HEAD_DIM, HEAD_DIM), HEAD_DIM)
        for block in range(blocks):
            cols = slice(block * TILE, (block + 1) * TILE)
            keys = slice(first_key(block), (block + 1) * TILE)
            scores = diagonal_mask(dot(key_heads[h, keys, :], q_t[head_rows, cols]))
            peak = jnp.max(scores, axis=0, keepdims=True)
            weights = jnp.exp(scores - peak)
            total = jnp.sum(weights, axis=0, keepdims=True)
            mixed = dot(v_t[head_rows, keys], weights.astype(BF16))
            out_t[head_rows, cols] = mixed * (1.0 / total)
            stats[0, pl.ds(h, 1), cols] = peak + jnp.log(total)

    many = info[blocks] != 0

    @pl.when(jnp.logical_not(many))
    def _():
        @pl.loop(0, heads)
        def _(h):
            one_head(h, lambda block: 0)

    @pl.when(many)
    def _():
        @pl.loop(0, heads)
        def _(h):
            one_head(h, lambda block: block * TILE)

    for i in range(blocks):
        at = pl.multiple_of(info[i] * TILE, TILE)
        out[i * TILE : (i + 1) * TILE, :] = out_t[:, pl.ds(at, TILE)].T.astype(BF16)


def attend(info, mixed):
    rows, wide = mixed.shape
    width = wide // 3
    groups = width // GROUP
    heads = GROUP // HEAD_DIM
    part = lambda shift: pl.BlockSpec((rows, GROUP), lambda g, s: (0, g + shift * groups))
    return call(
        attend_kernel,
        (groups,),
        [info],
        [(mixed, part(0)), (mixed, part(1)), (mixed, part(2))],
        [
            (shape((rows, width), BF16), part(0)),
            (
                shape((groups, heads, rows), F32),
                pl.BlockSpec((1, heads, rows), lambda g, s: (g, 0, 0)),
            ),
        ],
        [],
        "attend",
        36,
        scratch=[
            pltpu.VMEM((heads, rows, HEAD_DIM), BF16),
            pltpu.VMEM((GROUP, rows), BF16),
            pltpu.VMEM((GROUP, rows), BF16),
            pltpu.VMEM((GROUP, rows), F32),
        ],
    )


def feed_kernel(place, own_tok, far_tok, own_cot, far_cot, att, out_far, up_far, down_far,
                gains, biases, near_out, far_out, branch_out, normed2_out, active_out, back2_out, hidden_back_out, sums,
                slope, w_out, w_up, w_down, sems):
    chunk = 1024
    parts = [(out_far, w_out, slice(0, w_out.shape[1]))]
    for start in range(0, w_up.shape[1], chunk):
        parts.append((up_far, w_up, slice(start, start + chunk)))
        parts.append((down_far.at[start : start + chunk], w_down.at[start : start + chunk],
                      slice(0, w_down.shape[1])))
    stream = Stream(sems, parts)
    stream.take(1)
    residual = pick_rows(own_tok, far_tok)
    branch = dot(att[...], w_out[...])
    branch_out[...] = branch
    unit1, _ = norm_parts(branch)
    middle = residual + unit1 * gains[1:2, :] + biases[1:2, :]
    unit2, _ = norm_parts(middle)
    normed2 = (unit2 * gains[2:3, :] + biases[2:3, :]).astype(BF16)
    normed2_out[...] = normed2
    ff = w_up.shape[1]
    root = math.sqrt(2.0 / math.pi)
    branch2 = jnp.zeros_like(branch)
    for start in range(0, ff, chunk):
        cols = slice(start, start + chunk)
        if start <= 2 * chunk:
            stream.take(2 if start < 2 * chunk else 4)
        z = dot(normed2, w_up[:, cols])
        square = z * z
        bend = jnp.tanh(z * (root + (root * 0.044715) * square))
        half = 0.5 + 0.5 * bend
        active = (z * half).astype(BF16)
        active_out[:, cols] = active
        inner = (0.5 * root) + (1.5 * root * 0.044715) * square
        slope[:, cols] = half + z * (1.0 - bend * bend) * inner
        branch2 = branch2 + dot(active, w_down[cols, :])
    unit3, rstd3 = norm_parts(branch2)
    put_rows(near_out, far_out, (middle + unit3 * gains[3:4, :] + biases[3:4, :]).astype(BF16))
    upstream = pick_rows(own_cot, far_cot)
    back2 = norm_back(unit3, rstd3, gains[3:4, :], upstream).astype(BF16)
    back2_out[...] = back2

    @pl.when(pl.program_id(0) == 0)
    def _():
        sums[...] = jnp.zeros_like(sums)

    sums[0:1, :] += token_sum(upstream * unit3)
    sums[1:2, :] += token_sum(upstream)
    for start in range(0, ff, chunk):
        cols = slice(start, start + chunk)
        grad_active = dot(back2, w_down[cols, :], NT)
        hidden_back_out[:, cols] = (grad_active * slope[:, cols]).astype(BF16)


def feed(place, tokens, far_tok, cotangent, far_cot, att, w_out, w_up, w_down, gains, biases):
    rows, width = att.shape
    ff = w_up.shape[1]
    return call(
        feed_kernel,
        (rows // TILE,),
        [place],
        [
            (tokens, own_rows(width)), (far_tok, far_rows(width)),
            (cotangent, own_rows(width)), (far_cot, far_rows(width)),
            (att, row_block(width)), (w_out, ANY), (w_up, ANY), (w_down, ANY),
            (gains, whole(gains.shape)), (biases, whole(biases.shape)),
        ],
        [
            (shape((2, rows // 2, width), BF16), own_rows(width)),
            (shape((rows // 2, width), BF16), far_rows(width)),
            (shape((rows, width), F32), row_block(width)),
            (shape((rows, width), BF16), row_block(width)),
            (shape((rows, ff), BF16), row_block(ff)),
            (shape((rows, width), BF16), row_block(width)),
            (shape((rows, ff), BF16), row_block(ff)),
            (shape((8, width), F32), whole((8, width))),
        ],
        [],
        "feed",
        49,
        scratch=[
            pltpu.VMEM((TILE, ff), F32),
            pltpu.VMEM(w_out.shape, BF16), pltpu.VMEM(w_up.shape, BF16), pltpu.VMEM(w_down.shape, BF16),
            pltpu.SemaphoreType.DMA((9,)),
        ],
    )


def return_kernel(place, own_tok, far_tok, own_cot, far_cot, branch, hidden_back, out_far, up_far,
                  gains, biases, middle_back_out, branch_back_out, att_back_out, sums,
                  w_out, w_up, sems):
    chunk = 1024
    starts = range(0, w_up.shape[1], chunk)
    stream = Stream(
        sems,
        [(up_far, w_up, slice(start, start + chunk)) for start in starts]
        + [(out_far, w_out, slice(0, w_out.shape[1]))],
    )
    unit1, rstd1 = norm_parts(branch[...])
    middle = pick_rows(own_tok, far_tok) + unit1 * gains[1:2, :] + biases[1:2, :]
    unit2, rstd2 = norm_parts(middle)
    grad2 = None
    for start in starts:
        if start <= 2 * chunk:
            stream.take(1 if start < 2 * chunk else 3)
        cols = slice(start, start + chunk)
        term = dot(hidden_back[:, cols], w_up[:, cols], NT)
        grad2 = term if grad2 is None else grad2 + term
    middle_back = pick_rows(own_cot, far_cot) + norm_back(unit2, rstd2, gains[2:3, :], grad2)
    middle_back_out[...] = middle_back
    branch_back = norm_back(unit1, rstd1, gains[1:2, :], middle_back).astype(BF16)
    branch_back_out[...] = branch_back
    att_back_out[...] = dot(branch_back, w_out[...], NT).astype(BF16)

    @pl.when(pl.program_id(0) == 0)
    def _():
        sums[...] = jnp.zeros_like(sums)

    sums[0:1, :] += token_sum(middle_back * unit1)
    sums[1:2, :] += token_sum(middle_back)
    sums[2:3, :] += token_sum(grad2 * unit2)
    sums[3:4, :] += token_sum(grad2)


def return_pass(place, tokens, far_tok, cotangent, far_cot, branch, hidden_back, w_out, w_up,
                gains, biases, deps):
    rows, width = branch.shape
    ff = w_up.shape[1]
    return call(
        return_kernel,
        (rows // TILE,),
        [place],
        [
            (tokens, own_rows(width)), (far_tok, far_rows(width)),
            (cotangent, own_rows(width)), (far_cot, far_rows(width)),
            (branch, row_block(width)), (hidden_back, row_block(ff)),
            (w_out, ANY), (w_up, ANY),
            (gains, whole(gains.shape)), (biases, whole(biases.shape)),
        ],
        [
            (shape((rows, width), F32), row_block(width)),
            (shape((rows, width), BF16), row_block(width)),
            (shape((rows, width), BF16), row_block(width)),
            (shape((8, width), F32), whole((8, width))),
        ],
        deps,
        "return_pass",
        24,
        scratch=[
            pltpu.VMEM(w_out.shape, BF16), pltpu.VMEM(w_up.shape, BF16), pltpu.SemaphoreType.DMA((5,)),
        ],
    )


def attend_back_kernel(info, q, k, v, att, grad, stats, cos_t, sin_t, back,
                       q_heads, k_heads, v_heads, g_heads, q_t, k_t, g_t, inner, q_acc, k_acc, v_acc):
    heads = GROUP // HEAD_DIM
    half = HEAD_DIM // 2
    blocks = q.shape[0] // TILE
    rows_all = blocks * TILE
    for i in range(blocks):
        rows = slice(i * TILE, (i + 1) * TILE)
        at = pl.multiple_of(info[i] * TILE, TILE)
        spot = pl.ds(at, TILE)
        q_t[:, spot] = q[rows, :].T
        k_t[:, spot] = k[rows, :].T
        grad_t = grad[rows, :].T
        g_t[:, spot] = grad_t
        product = att[rows, :].T.astype(F32) * grad_t.astype(F32)
        for h in range(heads):
            lanes = slice(h * HEAD_DIM, (h + 1) * HEAD_DIM)
            q_heads[h, spot, :] = q[rows, lanes]
            k_heads[h, spot, :] = k[rows, lanes]
            v_heads[h, spot, :] = v[rows, lanes]
            g_heads[h, spot, :] = grad[rows, lanes]
            inner[pl.ds(h, 1), spot] = jnp.sum(product[lanes, :], axis=0, keepdims=True)

    def one_head(h, last_ask):
        head_rows = pl.ds(pl.multiple_of(h * HEAD_DIM, HEAD_DIM), HEAD_DIM)
        for block in range(blocks):
            keys = slice(block * TILE, (block + 1) * TILE)
            cols = slice(block * TILE, last_ask(block))
            scores = dot(k_heads[h, keys, :], q_t[head_rows, cols])
            low = scores[:, :TILE]
            keys_at = lax.broadcasted_iota(jnp.int32, (TILE, TILE), 0)
            asks_at = lax.broadcasted_iota(jnp.int32, (TILE, TILE), 1)
            low = jnp.where(keys_at <= asks_at, low, -1e30)
            if scores.shape[1] > TILE:
                scores = jnp.concatenate([low, scores[:, TILE:]], axis=1)
            else:
                scores = low
            weights = jnp.exp(scores - stats[0, pl.ds(h, 1), cols])
            weight_back = dot(v_heads[h, keys, :], g_t[head_rows, cols])
            score_back = (weights * (weight_back - inner[pl.ds(h, 1), cols])).astype(BF16)
            v_acc[h, keys, :] = dot(weights.astype(BF16), g_heads[h, cols, :])
            k_acc[h, keys, :] = dot(score_back, q_heads[h, cols, :])
            change = dot(k_t[head_rows, keys], score_back)
            if block == 0:
                q_acc[head_rows, cols] = change
            elif last_ask(0) < rows_all:
                q_acc[head_rows, cols] = change
            else:
                q_acc[head_rows, cols] += change

    many = info[blocks] != 0

    @pl.when(jnp.logical_not(many))
    def _():
        @pl.loop(0, heads)
        def _(h):
            one_head(h, lambda block: rows_all)

    @pl.when(many)
    def _():
        @pl.loop(0, heads)
        def _(h):
            one_head(h, lambda block: (block + 1) * TILE)

    scale = 1.0 / math.sqrt(HEAD_DIM)
    for i in range(blocks):
        rows = slice(i * TILE, (i + 1) * TILE)
        spot = pl.ds(pl.multiple_of(info[i] * TILE, TILE), TILE)
        cos = cos_t[:, rows]
        sin = sin_t[:, rows]

        def turn_back(parts, factor):
            turned = []
            for part in parts:
                first, second = part[:half], part[half:]
                turned.append(first * cos + second * sin)
                turned.append(second * cos - first * sin)
            return (jnp.concatenate(turned, axis=0) * factor).T.astype(BF16)

        back[0, rows, :] = turn_back(
            [q_acc[h * HEAD_DIM : (h + 1) * HEAD_DIM, spot] for h in range(heads)], scale
        )
        back[1, rows, :] = turn_back([k_acc[h, spot, :].T for h in range(heads)], 1.0)
        back[2, rows, :] = jnp.concatenate(
            [v_acc[h, spot, :] for h in range(heads)], axis=1
        ).astype(BF16)


def attend_back(info, mixed, att, grad, stats, cos_t, sin_t, group, earlier, deps):
    rows, wide = mixed.shape
    width = wide // 3
    groups = width // GROUP
    heads = GROUP // HEAD_DIM
    spec = lambda shift: pl.BlockSpec((rows, GROUP), lambda i, s: (0, group + shift * groups))
    per_head = pltpu.VMEM((heads, rows, HEAD_DIM), BF16)
    turned = pltpu.VMEM((GROUP, rows), BF16)
    angles = pl.BlockSpec((HEAD_DIM // 2, rows), lambda i, s: (0, 0))
    return call(
        attend_back_kernel,
        (1,),
        [info],
        [
            (mixed, spec(0)), (mixed, spec(1)), (mixed, spec(2)), (att, spec(0)), (grad, spec(0)),
            (stats, pl.BlockSpec((1, heads, rows), lambda i, s: (group, 0, 0))),
            (cos_t, angles), (sin_t, angles),
        ],
        [
            (
                shape((3, rows, 2 * GROUP), BF16),
                pl.BlockSpec((3, rows, GROUP), lambda i, s: (0, 0, group % 2)),
            ),
        ],
        earlier + deps,
        "attend_back",
        12,
        scratch=[
            per_head, per_head, per_head, per_head,
            turned, turned, turned,
            pltpu.VMEM((8, rows), F32),
            pltpu.VMEM((GROUP, rows), F32),
            pltpu.VMEM((heads, rows, HEAD_DIM), F32),
            pltpu.VMEM((heads, rows, HEAD_DIM), F32),
        ],
        aliases={9: 0} if earlier else None,
    )[0]


def finish_kernel(place, own_tok, far_tok, middle_back, left_back, right_back, w_far, gains,
                  near_out, far_out, sums, w_qkv, sems):
    half = left_back.shape[2]
    stream = Stream(
        sems, [(w_far, w_qkv, slice(at, at + half)) for at in range(0, w_qkv.shape[1], half)]
    )
    unit, rstd = norm_parts(pick_rows(own_tok, far_tok))
    grad = None
    for part in range(3):
        for side, back in enumerate((left_back, right_back)):
            start = (2 * part + side) * half
            if start in (0, half, 3 * half):
                stream.take({0: 1, half: 2, 3 * half: 3}[start])
            term = dot(back[part], w_qkv[:, start : start + half], NT)
            grad = term if grad is None else grad + term
    back = middle_back[...] + norm_back(unit, rstd, gains[0:1, :], grad)
    put_rows(near_out, far_out, back.astype(BF16))

    @pl.when(pl.program_id(0) == 0)
    def _():
        sums[...] = jnp.zeros_like(sums)

    sums[0:1, :] += token_sum(grad * unit)
    sums[1:2, :] += token_sum(grad)


def finish(place, tokens, far_tok, middle_back, left_back, right_back, w_qkv, gains, deps):
    rows, width = middle_back.shape
    parts = pl.BlockSpec((3, TILE, width // 2), lambda i, *_: (0, i, 0))
    return call(
        finish_kernel,
        (rows // TILE,),
        [place],
        [
            (tokens, own_rows(width)), (far_tok, far_rows(width)),
            (middle_back, row_block(width)), (left_back, parts), (right_back, parts),
            (w_qkv, ANY), (gains, whole(gains.shape)),
        ],
        [
            (shape((2, rows // 2, width), BF16), own_rows(width)),
            (shape((rows // 2, width), BF16), far_rows(width)),
            (shape((8, width), F32), whole((8, width))),
        ],
        deps,
        "finish",
        8,
        scratch=[pltpu.VMEM(w_qkv.shape, BF16), pltpu.SemaphoreType.DMA((6,))],
    )


def weight_grad_kernel(source_count, out_count, place, *refs):
    outs = refs[-out_count:]
    addends = refs[2 * source_count : -out_count]
    share = pl.num_programs(0) // out_count
    start = 0
    for number in range(source_count):
        left, right = refs[2 * number], refs[2 * number + 1]
        rights = [right] if len(right.shape) == 2 else [right.at[p] for p in range(3)]
        for piece in rights:
            cols = slice(start, start + piece.shape[1])
            start = cols.stop
            total = dot(left[...], piece[...], TN)
            for addend in addends:
                total = total + addend[:, cols].astype(F32)
            total = total.astype(BF16)
            if out_count == 1:
                outs[0][:, cols] = total
                continue
            for turn, out in enumerate(outs):

                @pl.when(pl.program_id(0) // share == turn)
                def _(out=out, cols=cols, total=total):
                    out[:, cols] = total


def swap_wide(rows, bit):
    size = lax.axis_size("wide")
    return lax.ppermute(rows, "wide", [(i, i ^ bit) for i in range(size)])


def swap_narrow(rows):
    return lax.ppermute(rows, "narrow", [(0, 1), (1, 0)])


def swap_crossed(rows, first):
    pairs = []
    for i in range(lax.axis_size("wide")):
        for n in range(2):
            along_x = (i % 2 == 0) == first
            peer = (i, 1 - n) if along_x else (i ^ 2, n)
            pairs.append((2 * i + n, 2 * peer[0] + peer[1]))
    return lax.ppermute(rows, ("wide", "narrow"), pairs)


def swap_two(rows, even_bit, odd_bit):
    size = lax.axis_size("wide")
    return lax.ppermute(
        rows, "wide", [(i, i ^ (even_bit if i % 2 == 0 else odd_bit)) for i in range(size)]
    )


def pair_sum(mine, theirs):
    return (mine.astype(F32) + theirs.astype(F32)).astype(BF16)


def choose(which, bit):
    return jnp.where(which == 1, bit, 1 - bit)


class Reduction:
    def __init__(self, place, sources, rows, cols, halves, us):
        self.place, self.sources = place, sources
        self.rows, self.cols, self.halves, self.us = rows, cols, halves, us
        self.bits = []
        bit = 4
        while bit < lax.axis_size("wide"):
            self.bits.append(bit)
            bit *= 2

    def blocks(self, steps, core_of, pair_of, addends, deps, outs=1):
        tokens = self.sources[0][0].shape[0]

        def at(place_of):
            def index(i, h, place):
                core = core_of(place)
                first, second = pair_of(i, place)
                x = jnp.where(core == 0, first, second)
                b = jnp.where(core == 0, second, first)
                return place_of(x, core, b, h)

            return index

        inputs = []
        for left, left_of, right, right_of, width in self.sources:
            inputs.append((left, pl.BlockSpec((tokens, self.rows), at(left_of))))
            dims = (tokens, width) if right.ndim == 2 else (3, tokens, width)
            inputs.append((right, pl.BlockSpec(dims, at(right_of))))
        block = (self.rows, self.cols // self.halves)
        share = steps // outs
        for array, row in addends:
            inputs.append((array, pl.BlockSpec(block, lambda i, h, place, row=row: (row(i), h))))
        return call(
            functools.partial(weight_grad_kernel, len(self.sources), outs),
            (steps, self.halves),
            [self.place],
            inputs,
            [
                (
                    shape((share * self.rows, self.cols), BF16),
                    pl.BlockSpec(
                        block, lambda i, h, place, at=turn * share: (jnp.clip(i - at, 0, share - 1), h)
                    ),
                )
                for turn in range(outs)
            ],
            deps,
            "weight_grad",
            0.5 + 0.3 * self.us * steps,
        )

    def far(self, deps):
        pair_of = lambda i, place: (choose(i // 2, place[4]), choose(i % 2, place[3]))
        sent = self.blocks(4, lambda place: 1 - place[1], pair_of, [], deps, outs=2)
        self.core = [swap_wide(part, 1) for part in sent]
        return sent[0]

    def first(self, deps):
        pair_of = lambda i, place: (1 - place[3], choose(i, place[4]))
        sent = self.blocks(
            2, lambda place: place[1], pair_of, [(self.core[0], lambda i: i)], deps + self.core[1:]
        )[0]
        self.near = swap_crossed(sent, True)
        return sent

    def second(self, deps):
        pair_of = lambda i, place: (place[3], 1 - place[4])
        addends = [(self.core[1], lambda i: 0), (self.near, lambda i: 0)]
        sent = self.blocks(1, lambda place: place[1], pair_of, addends, deps)[0]
        self.side = swap_crossed(sent, False)
        return sent

    def keep(self, deps):
        pair_of = lambda i, place: (place[3], place[4])
        addends = [(self.core[1], lambda i: 1), (self.near, lambda i: 1), (self.side, lambda i: 0)]
        self.total = self.blocks(1, lambda place: place[1], pair_of, addends, deps)[0]
        self.hop = 0
        self.send()
        return self.total

    def send(self):
        self.got = swap_two(self.total, self.bits[self.hop], self.bits[-1 - self.hop])
        self.hop += 1

    def step(self, dep):
        self.total = pair_sum(self.total, tie(self.got, dep))
        if self.hop < len(self.bits):
            self.send()
        else:
            self.from_core = swap_wide(self.total, 1)
        return self.total

    def open(self, dep):
        self.from_y = swap_wide(tie(self.total, dep), 2)

    def spread(self, dep):
        self.from_y = tie(self.from_y, dep)
        self.from_both = swap_wide(self.from_y, 1)
        return self.from_y

    def pieces(self):
        return [self.total, self.from_y, self.from_core, self.from_both]


def gather_kernel(place, *refs):
    out = refs[-1]
    for number, piece in enumerate(refs[:4]):

        @pl.when(pl.program_id(0) == number)
        def _(piece=piece):
            out[...] = piece[...].astype(F32)


def piece_owner(number, place):
    c = jnp.where(number < 2, place[1], 1 - place[1])
    b = jnp.where(number % 2 == 0, place[2], 1 - place[2])
    return c, b


def gather(place, pieces, dims, cols, first, parts, block_at, deps):
    rows = pieces[0].shape[0]

    def part_of(number):
        def index(i, h, place):
            turn = jnp.where(i == number, h, jnp.where(i < number, 0, parts - 1))
            return (0, first + turn)

        return pl.BlockSpec((rows, cols), index)

    return call(
        gather_kernel,
        (4, parts),
        [place],
        [(piece, part_of(number)) for number, piece in enumerate(pieces)],
        [
            (
                shape(dims, F32),
                pl.BlockSpec(
                    (rows, cols), lambda i, h, place: block_at(*piece_owner(i, place), h)
                ),
            )
        ],
        deps,
        "gather",
        6,
    )[0]


def gather_mixed_kernel(place, *refs):
    out = refs[-1]
    quarter = refs[0].shape[1]
    mine = pl.program_id(0) == place[1]
    for core in range(2):

        @pl.when(mine == (core == 0))
        def _(core=core):
            for other in range(2):
                b = place[2] if other == 0 else 1 - place[2]
                at = pl.multiple_of(b * quarter, quarter)
                out[:, pl.ds(at, quarter)] = refs[2 * core + other][...].astype(F32)


def gather_mixed(place, pieces, dims, half, earlier, deps):
    piece = pl.BlockSpec((TILE, TILE), lambda i, p, place: (0, p))
    return call(
        gather_mixed_kernel,
        (2, 3),
        [place],
        [(array, piece) for array in pieces],
        [
            (
                shape(dims, F32),
                pl.BlockSpec((TILE, 2 * TILE), lambda i, p, place: (i, 2 * p + half)),
            )
        ],
        earlier + deps,
        "gather_mixed",
        4,
        aliases={5: 0} if earlier else None,
    )[0]


def local(tokens, doc_ids, w_qkv, w_out, w_up, w_down, norm_gains, norm_biases, cotangent):
    narrow_size = lax.axis_size("narrow")
    packs, tok_rows, width = tokens.shape
    assert narrow_size == 2 and packs == 2 and tok_rows == 2 * TILE
    pack_len = tok_rows * narrow_size
    ff = w_up.shape[1]
    n = lax.axis_index("narrow")
    w = lax.axis_index("wide")
    core = w % 2
    side = (w // 2) % 2
    place = jnp.stack(
        [n, core, side, jnp.where(core == 0, n, side), jnp.where(core == 0, side, n)]
    ).astype(jnp.int32)
    pick = lambda array, index: lax.dynamic_index_in_dim(array, index, 0, keepdims=False)

    far_tok = swap_narrow(pick(tokens, 1 - n))
    doc_row = pick(doc_ids, n)
    many = (doc_row[pack_len - 1] != 0).astype(jnp.int32)
    block_at = jnp.stack([n, 3 - n, 1 - n, 2 + n]).astype(jnp.int32)
    info = jnp.concatenate([block_at, many[None]])

    halves = HEAD_DIM // 2
    frequency = jnp.exp(
        -math.log(10000.0) * jnp.arange(halves, dtype=F32) * 2.0 / HEAD_DIM
    )
    places = (block_at[:, None] * TILE + jnp.arange(TILE, dtype=jnp.int32)[None, :]).reshape(-1)
    angles_t = frequency[:, None] * places.astype(F32)[None, :]
    cos_t = jnp.cos(angles_t)
    sin_t = jnp.sin(angles_t)
    cos = cos_t.T
    sin = sin_t.T
    cosine = jnp.concatenate([cos] * 4, axis=1)
    sine = jnp.concatenate([-sin, sin, -sin, sin], axis=1)

    early = project(
        place, tokens, w_qkv, norm_gains, norm_biases, cosine, sine, 0, (), pack_len
    )
    far_cot = swap_narrow(tie(pick(cotangent, 1 - n), early[0]))
    normed, mixed = project(
        place, far_tok, w_qkv, norm_gains, norm_biases, cosine, sine, 2, early, pack_len
    )
    att, stats = attend(info, mixed)
    near_out, far_out, branch, normed2, active, back2, hidden_back, sums3 = feed(
        place, tokens, far_tok, cotangent, far_cot, att, w_out, w_up, w_down,
        norm_gains, norm_biases,
    )
    half_wide = width // 2
    down = Reduction(
        place,
        [(active, lambda x, c, b, h: (0, 4 * x + 2 * c + b),
          back2, lambda x, c, b, h: (0, 0), width)],
        2 * TILE, width, 1, 1.5,
    )
    up = Reduction(
        place,
        [(normed2, lambda x, c, b, h: (0, x),
          hidden_back, lambda x, c, b, h: (0, 2 * c + b), width)],
        2 * TILE, width, 1, 1.5,
    )
    last = down.far([])
    last = up.far([last])
    last = down.first([last])
    last = up.first([last])
    middle_back, branch_back, att_back, sums12 = return_pass(
        place, tokens, far_tok, cotangent, far_cot, branch, hidden_back, w_out, w_up,
        norm_gains, norm_biases, [last],
    )

    def back(group, earlier, deps):
        return attend_back(
            info, mixed, att, att_back, stats, cos_t, sin_t, group, earlier, deps
        )

    last = down.second([middle_back])
    left_back = back(0, [], [last])
    last = up.second([left_back])
    left_back = back(1, [left_back], [last])
    by_rows = lambda x, c, b, h: (0, 2 * x + c)
    by_parts = lambda x, c, b, h: (0, 0, b)
    left = Reduction(
        place,
        [(normed, by_rows, left_back, by_parts, TILE),
         (att, by_rows, branch_back, lambda x, c, b, h: (0, b), half_wide)],
        TILE, 5 * TILE, 1, 1.2,
    )
    last = down.keep([left_back])
    last = up.keep([last])
    got_out = swap_narrow(tie(far_out, last))
    last = left.far([last])
    right_back = back(2, [], [last])
    last = down.step(right_back)
    last = left.first([last])
    right_back = back(3, [right_back], [last])
    right = Reduction(
        place, [(normed, by_rows, right_back, by_parts, TILE)], TILE, 3 * TILE, 1, 0.8
    )
    last = right.far([])
    last = up.step(last)
    last = left.second([last])
    last = right.first([last, got_out])
    extra = len(down.bits) - 2
    for _ in range(extra):
        last = down.step(last)
    last = down.step(last)
    near_grad, far_grad, sums0 = finish(
        place, tokens, far_tok, middle_back, left_back, right_back, w_qkv, norm_gains,
        [last, down.from_core],
    )
    last = right.second([near_grad])
    last = left.keep([last])
    norm_term = jnp.concatenate(
        [sums0[0:1], sums12[0:1], sums12[2:3], sums3[0:1],
         sums0[1:2], sums12[1:2], sums12[3:4], sums3[1:2]], axis=0
    )
    hops = [2 ** bit for bit in range(lax.axis_size("wide").bit_length() - 1)]

    def norm_step(last):
        nonlocal norm_term, norm_got
        norm_term = norm_term + tie(norm_got, last)
        if hops:
            norm_got = swap_wide(norm_term, hops.pop(0))
        return norm_term

    last = right.keep([last])
    down.open(last)
    for _ in range(extra):
        last = up.step(last)
    last = up.step(last)
    norm_got = swap_narrow(tie(norm_term, last))
    for _ in range(extra):
        last = left.step(last)
        last = right.step(last)
    last = left.step(last)
    up.open(last)
    last = norm_step(last)
    last = down.spread(last)
    last = right.step(last)
    got_grad = swap_narrow(tie(far_grad, last))
    grad_down = gather(
        place, down.pieces(), (ff // 2, width), half_wide, 0, 2,
        lambda c, b, h: (2 * c + b, h), [last],
    )
    last = norm_step(grad_down)
    out = lax.dynamic_update_slice(near_out, tie(got_out, last)[None], (1 - n, 0, 0))
    last = left.step(last)
    last = up.spread(last)
    left.open(last)
    last = norm_step(last)
    last = right.step(last)
    right.open(last)
    grad_up = gather(
        place, up.pieces(), (half_wide, ff), half_wide, 0, 2,
        lambda c, b, h: (0, 2 * (2 * c + b) + h), [last],
    )
    last = grad_up
    while hops:
        last = norm_step(last)
    last = norm_step(last)
    grad_tok = lax.dynamic_update_slice(near_grad, tie(got_grad, last)[None], (1 - n, 0, 0))
    last = left.spread(last)
    last = right.spread(last)
    grad_out_proj = gather(
        place, left.pieces(), (half_wide, width), TILE, 3, 2,
        lambda c, b, h: (c, 2 * b + h), [last],
    )
    grad_qkv = gather_mixed(
        place, left.pieces(), (half_wide, 3 * width), 0, [], [grad_out_proj]
    )
    grad_qkv = gather_mixed(
        place, right.pieces(), (half_wide, 3 * width), 1, [grad_qkv], []
    )
    norm_term = lax.dynamic_slice_in_dim(norm_term, n * half_wide, half_wide, 1)
    return (
        out,
        grad_tok,
        grad_qkv,
        grad_out_proj,
        grad_up,
        grad_down,
        norm_term[:4],
        norm_term[4:],
    )


def solution(mesh):
    rows = P("wide", "narrow", None)
    return jax.shard_map(
        local,
        mesh=mesh,
        in_specs=(rows, P("wide", None), P(), P(), P(), P(), P(), P(), rows),
        out_specs=(
            rows, rows,
            P("narrow", None), P("narrow", None), P("narrow", None), P("narrow", None),
            P(None, "narrow"), P(None, "narrow"),
        ),
        check_vma=False,
    )
```

```python
import functools
import math

import jax
import jax.numpy as jnp
from jax import lax
from jax.experimental import pallas as pl
from jax.experimental.pallas import tpu as pltpu
from jax.sharding import PartitionSpec as P

HEAD_DIM = 64
EPS = 1e-05
F32 = jnp.float32
BF16 = jnp.bfloat16
TILE = 256
GROUP = 256
FLOPS_PER_US = 1000000000
NN = (((1,), (0,)), ((), ()))
NT = (((1,), (1,)), ((), ()))
TN = (((0,), (0,)), ((), ()))


def dot(left, right, dims=NN):
    return lax.dot_general(left, right, dims, preferred_element_type=F32)


def call(kernel, grid, prefetch, inputs, outputs, deps, name, vmem, us, scratch=(), aliases=None):
    given = len(prefetch) + len(inputs)

    def body(*refs):
        kernel(*refs[:given], *refs[given + len(deps) :])

    in_specs = [spec for _, spec in inputs] + [pl.BlockSpec(memory_space=pl.ANY)] * len(deps)
    return pl.pallas_call(
        body,
        grid_spec=pltpu.PrefetchScalarGridSpec(
            num_scalar_prefetch=len(prefetch),
            grid=grid,
            in_specs=in_specs,
            out_specs=tuple(spec for _, spec in outputs),
            scratch_shapes=list(scratch),
        ),
        out_shape=tuple(shape for shape, _ in outputs),
        input_output_aliases=aliases or {},
        compiler_params=pltpu.CompilerParams(vmem_limit_bytes=vmem * 1024 * 1024),
        cost_estimate=pl.CostEstimate(
            flops=int(us * FLOPS_PER_US), transcendentals=0, bytes_accessed=1
        ),
        name=name,
    )(*prefetch, *[array for array, _ in inputs], *deps)


def shape(dims, dtype):
    return jax.ShapeDtypeStruct(dims, dtype)


def far_away(array):
    return pltpu.with_memory_space_constraint(array, pltpu.HBM)


def whole(dims):
    return pl.BlockSpec(dims, lambda *_: (0,) * len(dims), pipeline_mode=pl.Buffered(1))


def row_block(size):
    return pl.BlockSpec((TILE, size), lambda i, *_: (i, 0))


def own_rows(size):
    return pl.BlockSpec((1, TILE, size), lambda i, place, *_: (place[0], jnp.minimum(i, 1), 0))


def far_rows(size):
    return pl.BlockSpec((TILE, size), lambda i, *_: (jnp.maximum(i - 2, 0), 0))


def pick_rows(own, far):
    return jnp.where(pl.program_id(0) < 2, own[0].astype(F32), far[...].astype(F32))


def put_rows(near, far, rows):
    @pl.when(pl.program_id(0) < 2)
    def _():
        near[0] = rows

    @pl.when(pl.program_id(0) >= 2)
    def _():
        far[...] = rows


def tie(array, *deps):
    return lax.optimization_barrier((array,) + deps)[0]


def norm_parts(rows):
    centre = rows - jnp.mean(rows, axis=-1, keepdims=True)
    rstd = lax.rsqrt(jnp.mean(centre * centre, axis=-1, keepdims=True) + EPS)
    return centre * rstd, rstd


def norm_back(unit, rstd, gain, grad):
    scaled = grad * gain
    first = jnp.mean(scaled, axis=-1, keepdims=True)
    second = jnp.mean(scaled * unit, axis=-1, keepdims=True)
    return rstd * (scaled - first - unit * second)


def token_sum(rows):
    return jnp.sum(rows, axis=0, keepdims=True)


def project_kernel(place, tok, w, gains, biases, cosine, sine, normed_out, mixed_out):
    rows = tok[0] if len(tok.shape) == 3 else tok[...]
    unit, _ = norm_parts(rows.astype(F32))
    normed = (unit * gains[0:1, :] + biases[0:1, :]).astype(BF16)
    normed_out[...] = normed
    width = normed.shape[1]
    lanes = lax.broadcasted_iota(jnp.int32, (TILE, 128), 1)
    first_half = lanes % HEAD_DIM < HEAD_DIM // 2
    scale = 1.0 / math.sqrt(HEAD_DIM)
    cos = cosine[...]
    sin = sine[...]
    for start in range(0, 3 * width, 256):
        part = dot(normed, w[:, start : start + 256])
        if start >= 2 * width:
            mixed_out[:, start : start + 256] = part.astype(BF16)
            continue
        for sub in range(0, 256, 128):
            u = part[:, sub : sub + 128]
            turned = jnp.where(first_half, pltpu.roll(u, 96, 1), pltpu.roll(u, 32, 1))
            out = u * cos + turned * sin
            out = out.astype(BF16)
            if start < width:
                out = out * jnp.asarray(scale, BF16)
            mixed_out[:, start + sub : start + sub + 128] = out


def project(place, tok, w_qkv, gains, biases, cosine, sine, first_block, earlier, pack_len):
    width, wide = w_qkv.shape
    steps = tok.shape[-2] // TILE
    at = lambda size: pl.BlockSpec((TILE, size), lambda i, *_: (i + first_block, 0))
    own = tok.ndim == 3
    return call(
        project_kernel,
        (steps,),
        [place],
        [
            (tok, own_rows(width) if own else row_block(width)),
            (far_away(w_qkv), whole(w_qkv.shape)),
            (gains, whole(gains.shape)),
            (biases, whole(biases.shape)),
            (cosine, at(128)),
            (sine, at(128)),
        ],
        [
            (pltpu.HBM((pack_len, width), BF16), at(width)),
            (pltpu.HBM((pack_len, wide), BF16), at(wide)),
        ],
        [far_away(array) for array in earlier],
        "project",
        24,
        8,
        aliases={7: 0, 8: 1} if earlier else None,
    )


def diagonal_mask(scores):
    size = scores.shape[1]
    first = scores.shape[0] - size
    keys = lax.broadcasted_iota(jnp.int32, (size, size), 0)
    asks = lax.broadcasted_iota(jnp.int32, (size, size), 1)
    tail = jnp.where(keys <= asks, scores[first:], -1e30)
    if first == 0:
        return tail
    return jnp.concatenate([scores[:first], tail], axis=0)


def attend_kernel(info, q, k, v, out, stats, key_heads, q_t, v_t, out_t):
    heads = GROUP // HEAD_DIM
    blocks = q.shape[0] // TILE
    for i in range(blocks):
        rows = slice(i * TILE, (i + 1) * TILE)
        at = pl.multiple_of(info[i] * TILE, TILE)
        q_t[:, pl.ds(at, TILE)] = q[rows, :].T
        v_t[:, pl.ds(at, TILE)] = v[rows, :].T
        for h in range(heads):
            key_heads[h, pl.ds(at, TILE), :] = k[rows, h * HEAD_DIM : (h + 1) * HEAD_DIM]

    def one_head(h, first_key):
        head_rows = pl.ds(pl.multiple_of(h * HEAD_DIM, HEAD_DIM), HEAD_DIM)
        for block in range(blocks):
            cols = slice(block * TILE, (block + 1) * TILE)
            keys = slice(first_key(block), (block + 1) * TILE)
            scores = diagonal_mask(dot(key_heads[h, keys, :], q_t[head_rows, cols]))
            peak = jnp.max(scores, axis=0, keepdims=True)
            weights = jnp.exp(scores - peak)
            total = jnp.sum(weights, axis=0, keepdims=True)
            mixed = dot(v_t[head_rows, keys], weights.astype(BF16))
            out_t[head_rows, cols] = mixed * (1.0 / total)
            stats[0, pl.ds(h, 1), cols] = peak + jnp.log(total)

    many = info[blocks] != 0

    @pl.when(jnp.logical_not(many))
    def _():
        @pl.loop(0, heads)
        def _(h):
            one_head(h, lambda block: 0)

    @pl.when(many)
    def _():
        @pl.loop(0, heads)
        def _(h):
            one_head(h, lambda block: block * TILE)

    for i in range(blocks):
        at = pl.multiple_of(info[i] * TILE, TILE)
        out[i * TILE : (i + 1) * TILE, :] = out_t[:, pl.ds(at, TILE)].T.astype(BF16)


def attend(info, mixed):
    rows, wide = mixed.shape
    width = wide // 3
    groups = width // GROUP
    heads = GROUP // HEAD_DIM
    part = lambda shift: pl.BlockSpec((rows, GROUP), lambda g, s: (0, g + shift * groups))
    return call(
        attend_kernel,
        (groups,),
        [info],
        [(far_away(mixed), part(0)), (far_away(mixed), part(1)), (far_away(mixed), part(2))],
        [
            (pltpu.HBM((rows, width), BF16), part(0)),
            (
                shape((groups, heads, rows), F32),
                pl.BlockSpec((1, heads, rows), lambda g, s: (g, 0, 0)),
            ),
        ],
        [],
        "attend",
        24,
        36,
        scratch=[
            pltpu.VMEM((heads, rows, HEAD_DIM), BF16),
            pltpu.VMEM((GROUP, rows), BF16),
            pltpu.VMEM((GROUP, rows), BF16),
            pltpu.VMEM((GROUP, rows), F32),
        ],
    )


def feed_kernel(place, own_tok, far_tok, own_cot, far_cot, att, w_out, w_up, w_down, gains, biases,
                near_out, far_out, branch_out, normed2_out, active_out, back2_out, hidden_back_out, sums,
                slope):
    chunk = 1024
    residual = pick_rows(own_tok, far_tok)
    branch = dot(att[...], w_out[...])
    branch_out[...] = branch
    unit1, _ = norm_parts(branch)
    middle = residual + unit1 * gains[1:2, :] + biases[1:2, :]
    unit2, _ = norm_parts(middle)
    normed2 = (unit2 * gains[2:3, :] + biases[2:3, :]).astype(BF16)
    normed2_out[...] = normed2
    ff = w_up.shape[1]
    root = math.sqrt(2.0 / math.pi)
    branch2 = jnp.zeros_like(branch)
    for start in range(0, ff, chunk):
        cols = slice(start, start + chunk)
        z = dot(normed2, w_up[:, cols])
        square = z * z
        bend = jnp.tanh(z * (root + (root * 0.044715) * square))
        half = 0.5 + 0.5 * bend
        active = (z * half).astype(BF16)
        active_out[:, cols] = active
        inner = (0.5 * root) + (1.5 * root * 0.044715) * square
        slope[:, cols] = half + z * (1.0 - bend * bend) * inner
        branch2 = branch2 + dot(active, w_down[cols, :])
    unit3, rstd3 = norm_parts(branch2)
    put_rows(near_out, far_out, (middle + unit3 * gains[3:4, :] + biases[3:4, :]).astype(BF16))
    upstream = pick_rows(own_cot, far_cot)
    back2 = norm_back(unit3, rstd3, gains[3:4, :], upstream).astype(BF16)
    back2_out[...] = back2

    @pl.when(pl.program_id(0) == 0)
    def _():
        sums[...] = jnp.zeros_like(sums)

    sums[0:1, :] += token_sum(upstream * unit3)
    sums[1:2, :] += token_sum(upstream)
    for start in range(0, ff, chunk):
        cols = slice(start, start + chunk)
        grad_active = dot(back2, w_down[cols, :], NT)
        hidden_back_out[:, cols] = (grad_active * slope[:, cols]).astype(BF16)


def feed(place, tokens, far_tok, cotangent, far_cot, att, w_out, w_up, w_down, gains, biases):
    rows, width = att.shape
    ff = w_up.shape[1]
    return call(
        feed_kernel,
        (rows // TILE,),
        [place],
        [
            (far_away(tokens), own_rows(width)), (far_tok, far_rows(width)),
            (far_away(cotangent), own_rows(width)), (far_cot, far_rows(width)),
            (far_away(att), row_block(width)),
            (w_out, whole(w_out.shape)), (w_up, whole(w_up.shape)), (w_down, whole(w_down.shape)),
            (gains, whole(gains.shape)), (biases, whole(biases.shape)),
        ],
        [
            (pltpu.HBM((2, rows // 2, width), BF16), own_rows(width)),
            (shape((rows // 2, width), BF16), far_rows(width)),
            (pltpu.HBM((rows, width), F32), row_block(width)),
            (shape((rows, width), BF16), row_block(width)),
            (pltpu.HBM((rows, ff), BF16), row_block(ff)),
            (shape((rows, width), BF16), row_block(width)),
            (pltpu.HBM((rows, ff), BF16), row_block(ff)),
            (shape((8, width), F32), whole((8, width))),
        ],
        [],
        "feed",
        52,
        49,
        scratch=[pltpu.VMEM((TILE, ff), F32)],
    )


def return_kernel(place, own_tok, far_tok, own_cot, far_cot, branch, hidden_back, w_out, w_up, gains, biases,
                  middle_back_out, branch_back_out, att_back_out, sums):
    unit1, rstd1 = norm_parts(branch[...])
    middle = pick_rows(own_tok, far_tok) + unit1 * gains[1:2, :] + biases[1:2, :]
    unit2, rstd2 = norm_parts(middle)
    grad2 = dot(hidden_back[...], w_up[...], NT)
    middle_back = pick_rows(own_cot, far_cot) + norm_back(unit2, rstd2, gains[2:3, :], grad2)
    middle_back_out[...] = middle_back
    branch_back = norm_back(unit1, rstd1, gains[1:2, :], middle_back).astype(BF16)
    branch_back_out[...] = branch_back
    att_back_out[...] = dot(branch_back, w_out[...], NT).astype(BF16)

    @pl.when(pl.program_id(0) == 0)
    def _():
        sums[...] = jnp.zeros_like(sums)

    sums[0:1, :] += token_sum(middle_back * unit1)
    sums[1:2, :] += token_sum(middle_back)
    sums[2:3, :] += token_sum(grad2 * unit2)
    sums[3:4, :] += token_sum(grad2)


def return_pass(place, tokens, far_tok, cotangent, far_cot, branch, hidden_back, w_out, w_up,
                gains, biases, deps):
    rows, width = branch.shape
    ff = w_up.shape[1]
    return call(
        return_kernel,
        (rows // TILE,),
        [place],
        [
            (far_away(tokens), own_rows(width)), (far_tok, far_rows(width)),
            (far_away(cotangent), own_rows(width)), (far_cot, far_rows(width)),
            (far_away(branch), row_block(width)), (far_away(hidden_back), row_block(ff)),
            (far_away(w_out), whole(w_out.shape)), (far_away(w_up), whole(w_up.shape)),
            (gains, whole(gains.shape)), (biases, whole(biases.shape)),
        ],
        [
            (pltpu.HBM((rows, width), F32), row_block(width)),
            (shape((rows, width), BF16), row_block(width)),
            (shape((rows, width), BF16), row_block(width)),
            (shape((8, width), F32), whole((8, width))),
        ],
        deps,
        "return_pass",
        32,
        24,
    )


def attend_back_kernel(info, q, k, v, att, grad, stats, cos_t, sin_t, back,
                       q_heads, k_heads, v_heads, g_heads, q_t, k_t, g_t, inner, q_acc, k_acc, v_acc):
    heads = GROUP // HEAD_DIM
    half = HEAD_DIM // 2
    blocks = q.shape[0] // TILE
    rows_all = blocks * TILE
    for i in range(blocks):
        rows = slice(i * TILE, (i + 1) * TILE)
        at = pl.multiple_of(info[i] * TILE, TILE)
        spot = pl.ds(at, TILE)
        q_t[:, spot] = q[rows, :].T
        k_t[:, spot] = k[rows, :].T
        grad_t = grad[rows, :].T
        g_t[:, spot] = grad_t
        product = att[rows, :].T.astype(F32) * grad_t.astype(F32)
        for h in range(heads):
            lanes = slice(h * HEAD_DIM, (h + 1) * HEAD_DIM)
            q_heads[h, spot, :] = q[rows, lanes]
            k_heads[h, spot, :] = k[rows, lanes]
            v_heads[h, spot, :] = v[rows, lanes]
            g_heads[h, spot, :] = grad[rows, lanes]
            inner[pl.ds(h, 1), spot] = jnp.sum(product[lanes, :], axis=0, keepdims=True)

    def one_head(h, last_ask):
        head_rows = pl.ds(pl.multiple_of(h * HEAD_DIM, HEAD_DIM), HEAD_DIM)
        for block in range(blocks):
            keys = slice(block * TILE, (block + 1) * TILE)
            cols = slice(block * TILE, last_ask(block))
            scores = dot(k_heads[h, keys, :], q_t[head_rows, cols])
            low = scores[:, :TILE]
            keys_at = lax.broadcasted_iota(jnp.int32, (TILE, TILE), 0)
            asks_at = lax.broadcasted_iota(jnp.int32, (TILE, TILE), 1)
            low = jnp.where(keys_at <= asks_at, low, -1e30)
            if scores.shape[1] > TILE:
                scores = jnp.concatenate([low, scores[:, TILE:]], axis=1)
            else:
                scores = low
            weights = jnp.exp(scores - stats[0, pl.ds(h, 1), cols])
            weight_back = dot(v_heads[h, keys, :], g_t[head_rows, cols])
            score_back = (weights * (weight_back - inner[pl.ds(h, 1), cols])).astype(BF16)
            v_acc[h, keys, :] = dot(weights.astype(BF16), g_heads[h, cols, :])
            k_acc[h, keys, :] = dot(score_back, q_heads[h, cols, :])
            change = dot(k_t[head_rows, keys], score_back)
            if block == 0:
                q_acc[head_rows, cols] = change
            elif last_ask(0) < rows_all:
                q_acc[head_rows, cols] = change
            else:
                q_acc[head_rows, cols] += change

    many = info[blocks] != 0

    @pl.when(jnp.logical_not(many))
    def _():
        @pl.loop(0, heads)
        def _(h):
            one_head(h, lambda block: rows_all)

    @pl.when(many)
    def _():
        @pl.loop(0, heads)
        def _(h):
            one_head(h, lambda block: (block + 1) * TILE)

    scale = 1.0 / math.sqrt(HEAD_DIM)
    for i in range(blocks):
        rows = slice(i * TILE, (i + 1) * TILE)
        spot = pl.ds(pl.multiple_of(info[i] * TILE, TILE), TILE)
        cos = cos_t[:, rows]
        sin = sin_t[:, rows]

        def turn_back(parts, factor):
            turned = []
            for part in parts:
                first, second = part[:half], part[half:]
                turned.append(first * cos + second * sin)
                turned.append(second * cos - first * sin)
            return (jnp.concatenate(turned, axis=0) * factor).T.astype(BF16)

        back[0, rows, :] = turn_back(
            [q_acc[h * HEAD_DIM : (h + 1) * HEAD_DIM, spot] for h in range(heads)], scale
        )
        back[1, rows, :] = turn_back([k_acc[h, spot, :].T for h in range(heads)], 1.0)
        back[2, rows, :] = jnp.concatenate(
            [v_acc[h, spot, :] for h in range(heads)], axis=1
        ).astype(BF16)


def attend_back(info, mixed, att, grad, stats, cos_t, sin_t, half, deps):
    rows, wide = mixed.shape
    width = wide // 3
    groups = width // GROUP
    heads = GROUP // HEAD_DIM
    first = half * (groups // 2)
    spec = lambda shift: pl.BlockSpec((rows, GROUP), lambda i, s: (0, i + first + shift * groups))
    per_head = pltpu.VMEM((heads, rows, HEAD_DIM), BF16)
    turned = pltpu.VMEM((GROUP, rows), BF16)
    angles = pl.BlockSpec((HEAD_DIM // 2, rows), lambda i, s: (0, 0))
    return call(
        attend_back_kernel,
        (groups // 2,),
        [info],
        [
            (far_away(mixed), spec(0)), (far_away(mixed), spec(1)), (far_away(mixed), spec(2)),
            (far_away(att), spec(0)), (far_away(grad), spec(0)),
            (stats, pl.BlockSpec((1, heads, rows), lambda i, s: (i + first, 0, 0))),
            (cos_t, angles), (sin_t, angles),
        ],
        [
            (
                pltpu.HBM((3, rows, 2 * GROUP), BF16),
                pl.BlockSpec((3, rows, GROUP), lambda i, s: (0, 0, i)),
            ),
        ],
        deps,
        "attend_back",
        32,
        24,
        scratch=[
            per_head, per_head, per_head, per_head,
            turned, turned, turned,
            pltpu.VMEM((8, rows), F32),
            pltpu.VMEM((GROUP, rows), F32),
            pltpu.VMEM((heads, rows, HEAD_DIM), F32),
            pltpu.VMEM((heads, rows, HEAD_DIM), F32),
        ],
    )[0]


def finish_kernel(place, own_tok, far_tok, middle_back, left_back, right_back, w_qkv, gains,
                  near_out, far_out, sums):
    half = left_back.shape[2]
    unit, rstd = norm_parts(pick_rows(own_tok, far_tok))
    grad = None
    for part in range(3):
        for side, back in enumerate((left_back, right_back)):
            start = (2 * part + side) * half
            term = dot(back[part], w_qkv[:, start : start + half], NT)
            grad = term if grad is None else grad + term
    back = middle_back[...] + norm_back(unit, rstd, gains[0:1, :], grad)
    put_rows(near_out, far_out, back.astype(BF16))

    @pl.when(pl.program_id(0) == 0)
    def _():
        sums[...] = jnp.zeros_like(sums)

    sums[0:1, :] += token_sum(grad * unit)
    sums[1:2, :] += token_sum(grad)


def finish(place, tokens, far_tok, middle_back, left_back, right_back, w_qkv, gains, deps):
    rows, width = middle_back.shape
    parts = pl.BlockSpec((3, TILE, width // 2), lambda i, *_: (0, i, 0))
    return call(
        finish_kernel,
        (rows // TILE,),
        [place],
        [
            (far_away(tokens), own_rows(width)), (far_tok, far_rows(width)),
            (far_away(middle_back), row_block(width)), (far_away(left_back), parts), (far_away(right_back), parts),
            (far_away(w_qkv), whole(w_qkv.shape)), (gains, whole(gains.shape)),
        ],
        [
            (pltpu.HBM((2, rows // 2, width), BF16), own_rows(width)),
            (shape((rows // 2, width), BF16), far_rows(width)),
            (shape((8, width), F32), whole((8, width))),
        ],
        deps,
        "finish",
        24,
        15,
    )


def weight_grad_kernel(source_count, out_count, place, *refs):
    outs = refs[-out_count:]
    addends = refs[2 * source_count : -out_count]
    share = pl.num_programs(0) // out_count
    start = 0
    for number in range(source_count):
        left, right = refs[2 * number], refs[2 * number + 1]
        rights = [right] if len(right.shape) == 2 else [right.at[p] for p in range(3)]
        turned = left[...].T
        for piece in rights:
            cols = slice(start, start + piece.shape[1])
            start = cols.stop
            total = dot(turned, piece[...])
            for addend in addends:
                total = total + addend[:, cols].astype(F32)
            total = total.astype(BF16)
            if out_count == 1:
                outs[0][:, cols] = total
                continue
            for turn, out in enumerate(outs):

                @pl.when(pl.program_id(0) // share == turn)
                def _(out=out, cols=cols, total=total):
                    out[:, cols] = total


def swap_wide(rows, bit):
    size = lax.axis_size("wide")
    return lax.ppermute(rows, "wide", [(i, i ^ bit) for i in range(size)])


def swap_narrow(rows):
    return lax.ppermute(rows, "narrow", [(0, 1), (1, 0)])


def swap_crossed(rows, first):
    pairs = []
    for i in range(lax.axis_size("wide")):
        for n in range(2):
            along_x = (i % 2 == 0) == first
            peer = (i, 1 - n) if along_x else (i ^ 2, n)
            pairs.append((2 * i + n, 2 * peer[0] + peer[1]))
    return lax.ppermute(rows, ("wide", "narrow"), pairs)


def swap_two(rows, even_bit, odd_bit):
    size = lax.axis_size("wide")
    return lax.ppermute(
        rows, "wide", [(i, i ^ (even_bit if i % 2 == 0 else odd_bit)) for i in range(size)]
    )


def pair_sum(mine, theirs):
    return (mine.astype(F32) + theirs.astype(F32)).astype(BF16)


def choose(which, bit):
    return jnp.where(which == 1, bit, 1 - bit)


class Reduction:
    def __init__(self, place, sources, rows, cols, halves, us):
        self.place, self.sources = place, sources
        self.rows, self.cols, self.halves, self.us = rows, cols, halves, us
        self.bits = []
        bit = 4
        while bit < lax.axis_size("wide"):
            self.bits.append(bit)
            bit *= 2

    def blocks(self, steps, core_of, pair_of, addends, deps, outs=1):
        tokens = self.sources[0][0].shape[0]

        def at(place_of):
            def index(i, h, place):
                core = core_of(place)
                first, second = pair_of(i, place)
                x = jnp.where(core == 0, first, second)
                b = jnp.where(core == 0, second, first)
                return place_of(x, core, b, h)

            return index

        inputs = []
        for left, left_of, right, right_of, width in self.sources:
            inputs.append((left, pl.BlockSpec((tokens, self.rows), at(left_of))))
            dims = (tokens, width) if right.ndim == 2 else (3, tokens, width)
            inputs.append((right, pl.BlockSpec(dims, at(right_of))))
        block = (self.rows, self.cols // self.halves)
        share = steps // outs
        for array, row in addends:
            inputs.append((array, pl.BlockSpec(block, lambda i, h, place, row=row: (row(i), h))))
        return call(
            functools.partial(weight_grad_kernel, len(self.sources), outs),
            (steps, self.halves),
            [self.place],
            inputs,
            [
                (
                    shape((share * self.rows, self.cols), BF16),
                    pl.BlockSpec(
                        block, lambda i, h, place, at=turn * share: (jnp.clip(i - at, 0, share - 1), h)
                    ),
                )
                for turn in range(outs)
            ],
            deps,
            "weight_grad",
            24,
            0.5 + 0.3 * self.us * steps,
        )

    def far(self, deps):
        pair_of = lambda i, place: (choose(i // 2, place[4]), choose(i % 2, place[3]))
        sent = self.blocks(4, lambda place: 1 - place[1], pair_of, [], deps, outs=2)
        self.core = [swap_wide(part, 1) for part in sent]
        return sent[0]

    def first(self, deps):
        pair_of = lambda i, place: (1 - place[3], choose(i, place[4]))
        sent = self.blocks(
            2, lambda place: place[1], pair_of, [(self.core[0], lambda i: i)], deps + self.core[1:]
        )[0]
        self.near = swap_crossed(sent, True)
        return sent

    def second(self, deps):
        pair_of = lambda i, place: (place[3], 1 - place[4])
        addends = [(self.core[1], lambda i: 0), (self.near, lambda i: 0)]
        sent = self.blocks(1, lambda place: place[1], pair_of, addends, deps)[0]
        self.side = swap_crossed(sent, False)
        return sent

    def keep(self, deps):
        pair_of = lambda i, place: (place[3], place[4])
        addends = [(self.core[1], lambda i: 1), (self.near, lambda i: 1), (self.side, lambda i: 0)]
        self.total = self.blocks(1, lambda place: place[1], pair_of, addends, deps)[0]
        self.hop = 0
        self.send()
        return self.total

    def send(self):
        self.got = swap_two(self.total, self.bits[self.hop], self.bits[-1 - self.hop])
        self.hop += 1

    def step(self, dep):
        self.total = pair_sum(self.total, tie(self.got, dep))
        if self.hop < len(self.bits):
            self.send()
        else:
            self.from_core = swap_wide(self.total, 1)
        return self.total

    def open(self, dep):
        self.from_y = swap_wide(tie(self.total, dep), 2)

    def spread(self, dep):
        self.from_y = tie(self.from_y, dep)
        self.from_both = swap_wide(self.from_y, 1)
        return self.from_y

    def pieces(self):
        return [self.total, self.from_y, self.from_core, self.from_both]


def gather_kernel(place, *refs):
    out = refs[-1]
    for number, piece in enumerate(refs[:4]):

        @pl.when(pl.program_id(0) == number)
        def _(piece=piece):
            out[...] = piece[...].astype(F32)


def piece_owner(number, place):
    c = jnp.where(number < 2, place[1], 1 - place[1])
    b = jnp.where(number % 2 == 0, place[2], 1 - place[2])
    return c, b


def gather(place, pieces, dims, cols, first, parts, block_at, deps):
    rows = pieces[0].shape[0]

    def part_of(number):
        def index(i, h, place):
            turn = jnp.where(i == number, h, jnp.where(i < number, 0, parts - 1))
            return (0, first + turn)

        return pl.BlockSpec((rows, cols), index)

    return call(
        gather_kernel,
        (4, parts),
        [place],
        [(piece, part_of(number)) for number, piece in enumerate(pieces)],
        [
            (
                shape(dims, F32),
                pl.BlockSpec(
                    (rows, cols), lambda i, h, place: block_at(*piece_owner(i, place), h)
                ),
            )
        ],
        deps,
        "gather",
        20,
        6,
    )[0]


def gather_mixed_kernel(place, *refs):
    out = refs[-1]
    quarter = refs[0].shape[1]
    mine = pl.program_id(0) == place[1]
    for core in range(2):

        @pl.when(mine == (core == 0))
        def _(core=core):
            for other in range(2):
                b = place[2] if other == 0 else 1 - place[2]
                at = pl.multiple_of(b * quarter, quarter)
                out[:, pl.ds(at, quarter)] = refs[2 * core + other][...].astype(F32)


def gather_mixed(place, pieces, dims, half, earlier, deps):
    piece = pl.BlockSpec((TILE, TILE), lambda i, p, place: (0, p))
    return call(
        gather_mixed_kernel,
        (2, 3),
        [place],
        [(array, piece) for array in pieces],
        [
            (
                shape(dims, F32),
                pl.BlockSpec((TILE, 2 * TILE), lambda i, p, place: (i, 2 * p + half)),
            )
        ],
        earlier + deps,
        "gather_mixed",
        16,
        4,
        aliases={5: 0} if earlier else None,
    )[0]


def local(tokens, doc_ids, w_qkv, w_out, w_up, w_down, norm_gains, norm_biases, cotangent):
    narrow_size = lax.axis_size("narrow")
    packs, tok_rows, width = tokens.shape
    assert narrow_size == 2 and packs == 2 and tok_rows == 2 * TILE
    pack_len = tok_rows * narrow_size
    ff = w_up.shape[1]
    n = lax.axis_index("narrow")
    w = lax.axis_index("wide")
    core = w % 2
    side = (w // 2) % 2
    place = jnp.stack(
        [n, core, side, jnp.where(core == 0, n, side), jnp.where(core == 0, side, n)]
    ).astype(jnp.int32)
    pick = lambda array, index: lax.dynamic_index_in_dim(array, index, 0, keepdims=False)

    far_tok = swap_narrow(pick(tokens, 1 - n))
    doc_row = pick(doc_ids, n)
    many = (doc_row[pack_len - 1] != 0).astype(jnp.int32)
    block_at = jnp.stack([n, 3 - n, 1 - n, 2 + n]).astype(jnp.int32)
    info = jnp.concatenate([block_at, many[None]])

    halves = HEAD_DIM // 2
    frequency = jnp.exp(
        -math.log(10000.0) * jnp.arange(halves, dtype=F32) * 2.0 / HEAD_DIM
    )
    places = (block_at[:, None] * TILE + jnp.arange(TILE, dtype=jnp.int32)[None, :]).reshape(-1)
    angles_t = frequency[:, None] * places.astype(F32)[None, :]
    cos_t = jnp.cos(angles_t)
    sin_t = jnp.sin(angles_t)
    cos = cos_t.T
    sin = sin_t.T
    cosine = jnp.concatenate([cos] * 4, axis=1)
    sine = jnp.concatenate([-sin, sin, -sin, sin], axis=1)

    early = project(
        place, tokens, w_qkv, norm_gains, norm_biases, cosine, sine, 0, (), pack_len
    )
    far_cot = swap_narrow(tie(pick(cotangent, 1 - n), early[0]))
    normed, mixed = project(
        place, far_tok, w_qkv, norm_gains, norm_biases, cosine, sine, 2, early, pack_len
    )
    att, stats = attend(info, mixed)
    near_out, far_out, branch, normed2, active, back2, hidden_back, sums3 = feed(
        place, tokens, far_tok, cotangent, far_cot, att, w_out, w_up, w_down,
        norm_gains, norm_biases,
    )
    half_wide = width // 2
    down = Reduction(
        place,
        [(far_away(active), lambda x, c, b, h: (0, 4 * x + 2 * c + b),
          back2, lambda x, c, b, h: (0, 0), width)],
        2 * TILE, width, 1, 1.5,
    )
    up = Reduction(
        place,
        [(normed2, lambda x, c, b, h: (0, x),
          far_away(hidden_back), lambda x, c, b, h: (0, 2 * c + b), width)],
        2 * TILE, width, 1, 1.5,
    )
    last = down.far([])
    last = up.far([last])
    last = down.first([last])
    last = up.first([last])
    middle_back, branch_back, att_back, sums12 = return_pass(
        place, tokens, far_tok, cotangent, far_cot, branch, hidden_back, w_out, w_up,
        norm_gains, norm_biases, [last],
    )

    def back(half, deps):
        return attend_back(info, mixed, att, att_back, stats, cos_t, sin_t, half, deps)

    last = down.second([sums12])
    left_back = back(0, [last])
    by_rows = lambda x, c, b, h: (0, 2 * x + c)
    by_parts = lambda x, c, b, h: (0, 0, b)
    left = Reduction(
        place,
        [(normed, by_rows, far_away(left_back), by_parts, TILE),
         (far_away(att), by_rows, branch_back, lambda x, c, b, h: (0, b), half_wide)],
        TILE, 5 * TILE, 1, 1.2,
    )
    last = up.second([far_away(left_back)])
    last = down.keep([last])
    last = left.far([last])
    last = up.keep([last])
    got_out = swap_narrow(tie(far_out, last))
    right_back = back(1, [last])
    last = left.first([far_away(right_back)])
    last = down.step(last)
    right = Reduction(
        place, [(normed, by_rows, far_away(right_back), by_parts, TILE)], TILE, 3 * TILE, 1, 0.8
    )
    last = right.far([last])
    last = up.step(last)
    last = left.second([last])
    last = right.first([last, got_out])
    extra = len(down.bits) - 2
    for _ in range(extra):
        last = down.step(last)
    last = down.step(last)
    down.open(last)
    near_grad, far_grad, sums0 = finish(
        place, tokens, far_tok, middle_back, left_back, right_back, w_qkv, norm_gains,
        [last, down.from_core],
    )
    last = right.second([sums0])
    last = left.keep([last])
    norm_term = jnp.concatenate(
        [sums0[0:1], sums12[0:1], sums12[2:3], sums3[0:1],
         sums0[1:2], sums12[1:2], sums12[3:4], sums3[1:2]], axis=0
    )
    hops = [2 ** bit for bit in range(lax.axis_size("wide").bit_length() - 1)]

    def norm_step(last):
        nonlocal norm_term, norm_got
        norm_term = norm_term + tie(norm_got, last)
        if hops:
            norm_got = swap_wide(norm_term, hops.pop(0))
        return norm_term

    last = right.keep([last])
    for _ in range(extra):
        last = up.step(last)
    last = up.step(last)
    up.open(last)
    norm_got = swap_narrow(tie(norm_term, last))
    for _ in range(extra):
        last = left.step(last)
        last = right.step(last)
    last = left.step(last)
    last = norm_step(last)
    last = right.step(last)
    last = down.spread(last)
    got_grad = swap_narrow(tie(far_grad, last))
    last = norm_step(last)
    grad_down = gather(
        place, down.pieces(), (ff // 2, width), half_wide, 0, 2,
        lambda c, b, h: (2 * c + b, h), [last],
    )
    last = norm_step(grad_down)
    out = lax.dynamic_update_slice(near_out, tie(got_out, last)[None], (1 - n, 0, 0))
    last = left.step(last)
    left.open(last)
    last = right.step(last)
    right.open(last)
    last = norm_step(last)
    last = up.spread(last)
    grad_up = gather(
        place, up.pieces(), (half_wide, ff), half_wide, 0, 2,
        lambda c, b, h: (0, 2 * (2 * c + b) + h), [last],
    )
    last = grad_up
    while hops:
        last = norm_step(last)
    last = norm_step(last)
    grad_tok = lax.dynamic_update_slice(near_grad, tie(got_grad, last)[None], (1 - n, 0, 0))
    last = left.spread(last)
    last = right.spread(last)
    grad_out_proj = gather(
        place, left.pieces(), (half_wide, width), TILE, 3, 2,
        lambda c, b, h: (c, 2 * b + h), [last],
    )
    grad_qkv = gather_mixed(
        place, left.pieces(), (half_wide, 3 * width), 0, [], [last]
    )
    grad_qkv = gather_mixed(
        place, right.pieces(), (half_wide, 3 * width), 1, [grad_qkv], []
    )
    norm_term = lax.dynamic_slice_in_dim(norm_term, n * half_wide, half_wide, 1)
    return (
        out,
        grad_tok,
        grad_qkv,
        grad_out_proj,
        grad_up,
        grad_down,
        norm_term[:4],
        norm_term[4:],
    )


def solution(mesh):
    rows = P("wide", "narrow", None)
    return jax.shard_map(
        local,
        mesh=mesh,
        in_specs=(rows, P("wide", None), P(), P(), P(), P(), P(), P(), rows),
        out_specs=(
            rows, rows,
            P("narrow", None), P("narrow", None), P("narrow", None), P("narrow", None),
            P(None, "narrow"), P(None, "narrow"),
        ),
        check_vma=False,
    )
```

```python
import functools
import math

import jax
import jax.numpy as jnp
from jax import lax
from jax.experimental import pallas as pl
from jax.experimental.pallas import tpu as pltpu
from jax.sharding import PartitionSpec as P

HEAD_DIM = 64
EPS = 1e-05
F32 = jnp.float32
BF16 = jnp.bfloat16
TILE = 256
GROUP = 256
FLOPS_PER_US = 1000000000
NN = (((1,), (0,)), ((), ()))
NT = (((1,), (1,)), ((), ()))
TN = (((0,), (0,)), ((), ()))


def dot(left, right, dims=NN):
    return lax.dot_general(left, right, dims, preferred_element_type=F32)


def call(kernel, grid, prefetch, inputs, outputs, deps, name, vmem, us, scratch=(), aliases=None):
    given = len(prefetch) + len(inputs)

    def body(*refs):
        kernel(*refs[:given], *refs[given + len(deps) :])

    in_specs = [spec for _, spec in inputs] + [pl.BlockSpec(memory_space=pl.ANY)] * len(deps)
    return pl.pallas_call(
        body,
        grid_spec=pltpu.PrefetchScalarGridSpec(
            num_scalar_prefetch=len(prefetch),
            grid=grid,
            in_specs=in_specs,
            out_specs=tuple(spec for _, spec in outputs),
            scratch_shapes=list(scratch),
        ),
        out_shape=tuple(shape for shape, _ in outputs),
        input_output_aliases=aliases or {},
        compiler_params=pltpu.CompilerParams(vmem_limit_bytes=vmem * 1024 * 1024),
        cost_estimate=pl.CostEstimate(
            flops=int(us * FLOPS_PER_US), transcendentals=0, bytes_accessed=1
        ),
        name=name,
    )(*prefetch, *[array for array, _ in inputs], *deps)


def shape(dims, dtype):
    return jax.ShapeDtypeStruct(dims, dtype)


def far_away(array):
    return pltpu.with_memory_space_constraint(array, pltpu.HBM)


def whole(dims):
    return pl.BlockSpec(dims, lambda *_: (0,) * len(dims), pipeline_mode=pl.Buffered(1))


def row_block(size):
    return pl.BlockSpec((TILE, size), lambda i, *_: (i, 0))


def own_rows(size):
    return pl.BlockSpec((1, TILE, size), lambda i, place, *_: (place[0], jnp.minimum(i, 1), 0))


def far_rows(size):
    return pl.BlockSpec((TILE, size), lambda i, *_: (jnp.maximum(i - 2, 0), 0))


def pick_rows(own, far):
    return jnp.where(pl.program_id(0) < 2, own[0].astype(F32), far[...].astype(F32))


def put_rows(near, far, rows):
    @pl.when(pl.program_id(0) < 2)
    def _():
        near[0] = rows

    @pl.when(pl.program_id(0) >= 2)
    def _():
        far[...] = rows


def tie(array, *deps):
    return lax.optimization_barrier((array,) + deps)[0]


def norm_parts(rows):
    centre = rows - jnp.mean(rows, axis=-1, keepdims=True)
    rstd = lax.rsqrt(jnp.mean(centre * centre, axis=-1, keepdims=True) + EPS)
    return centre * rstd, rstd


def norm_back(unit, rstd, gain, grad):
    scaled = grad * gain
    first = jnp.mean(scaled, axis=-1, keepdims=True)
    second = jnp.mean(scaled * unit, axis=-1, keepdims=True)
    return rstd * (scaled - first - unit * second)


def token_sum(rows):
    return jnp.sum(rows, axis=0, keepdims=True)


def project_kernel(place, tok, w, gains, biases, cosine, sine, normed_out, mixed_out):
    rows = tok[0] if len(tok.shape) == 3 else tok[...]
    unit, _ = norm_parts(rows.astype(F32))
    normed = (unit * gains[0:1, :] + biases[0:1, :]).astype(BF16)
    normed_out[...] = normed
    width = normed.shape[1]
    lanes = lax.broadcasted_iota(jnp.int32, (TILE, 128), 1)
    first_half = lanes % HEAD_DIM < HEAD_DIM // 2
    scale = 1.0 / math.sqrt(HEAD_DIM)
    cos = cosine[...]
    sin = sine[...]
    for start in range(0, 3 * width, 256):
        part = dot(normed, w[:, start : start + 256])
        if start >= 2 * width:
            mixed_out[:, start : start + 256] = part.astype(BF16)
            continue
        for sub in range(0, 256, 128):
            u = part[:, sub : sub + 128]
            turned = jnp.where(first_half, pltpu.roll(u, 96, 1), pltpu.roll(u, 32, 1))
            out = u * cos + turned * sin
            out = out.astype(BF16)
            if start < width:
                out = out * jnp.asarray(scale, BF16)
            mixed_out[:, start + sub : start + sub + 128] = out


def project(place, tok, w_qkv, gains, biases, cosine, sine, first_block, earlier, pack_len):
    width, wide = w_qkv.shape
    steps = tok.shape[-2] // TILE
    at = lambda size: pl.BlockSpec((TILE, size), lambda i, *_: (i + first_block, 0))
    own = tok.ndim == 3
    return call(
        project_kernel,
        (steps,),
        [place],
        [
            (tok, own_rows(width) if own else row_block(width)),
            (far_away(w_qkv), whole(w_qkv.shape)),
            (gains, whole(gains.shape)),
            (biases, whole(biases.shape)),
            (cosine, at(128)),
            (sine, at(128)),
        ],
        [
            (pltpu.HBM((pack_len, width), BF16), at(width)),
            (pltpu.HBM((pack_len, wide), BF16), at(wide)),
        ],
        [far_away(array) for array in earlier],
        "project",
        24,
        8,
        aliases={7: 0, 8: 1} if earlier else None,
    )


def diagonal_mask(scores):
    size = scores.shape[1]
    first = scores.shape[0] - size
    keys = lax.broadcasted_iota(jnp.int32, (size, size), 0)
    asks = lax.broadcasted_iota(jnp.int32, (size, size), 1)
    tail = jnp.where(keys <= asks, scores[first:], -1e30)
    if first == 0:
        return tail
    return jnp.concatenate([scores[:first], tail], axis=0)


def attend_kernel(info, q, k, v, out, stats, key_heads, q_t, v_t, out_t):
    heads = GROUP // HEAD_DIM
    blocks = q.shape[0] // TILE
    for i in range(blocks):
        rows = slice(i * TILE, (i + 1) * TILE)
        at = pl.multiple_of(info[i] * TILE, TILE)
        q_t[:, pl.ds(at, TILE)] = q[rows, :].T
        v_t[:, pl.ds(at, TILE)] = v[rows, :].T
        for h in range(heads):
            key_heads[h, pl.ds(at, TILE), :] = k[rows, h * HEAD_DIM : (h + 1) * HEAD_DIM]

    def one_head(h, first_key):
        head_rows = pl.ds(pl.multiple_of(h * HEAD_DIM, HEAD_DIM), HEAD_DIM)
        for block in range(blocks):
            cols = slice(block * TILE, (block + 1) * TILE)
            keys = slice(first_key(block), (block + 1) * TILE)
            scores = diagonal_mask(dot(key_heads[h, keys, :], q_t[head_rows, cols]))
            peak = jnp.max(scores, axis=0, keepdims=True)
            weights = jnp.exp(scores - peak)
            total = jnp.sum(weights, axis=0, keepdims=True)
            mixed = dot(v_t[head_rows, keys], weights.astype(BF16))
            out_t[head_rows, cols] = mixed * (1.0 / total)
            stats[0, pl.ds(h, 1), cols] = peak + jnp.log(total)

    many = info[blocks] != 0

    @pl.when(jnp.logical_not(many))
    def _():
        @pl.loop(0, heads)
        def _(h):
            one_head(h, lambda block: 0)

    @pl.when(many)
    def _():
        @pl.loop(0, heads)
        def _(h):
            one_head(h, lambda block: block * TILE)

    for i in range(blocks):
        at = pl.multiple_of(info[i] * TILE, TILE)
        out[i * TILE : (i + 1) * TILE, :] = out_t[:, pl.ds(at, TILE)].T.astype(BF16)


def attend(info, mixed):
    rows, wide = mixed.shape
    width = wide // 3
    groups = width // GROUP
    heads = GROUP // HEAD_DIM
    part = lambda shift: pl.BlockSpec((rows, GROUP), lambda g, s: (0, g + shift * groups))
    return call(
        attend_kernel,
        (groups,),
        [info],
        [(far_away(mixed), part(0)), (far_away(mixed), part(1)), (far_away(mixed), part(2))],
        [
            (pltpu.HBM((rows, width), BF16), part(0)),
            (
                shape((groups, heads, rows), F32),
                pl.BlockSpec((1, heads, rows), lambda g, s: (g, 0, 0)),
            ),
        ],
        [],
        "attend",
        24,
        36,
        scratch=[
            pltpu.VMEM((heads, rows, HEAD_DIM), BF16),
            pltpu.VMEM((GROUP, rows), BF16),
            pltpu.VMEM((GROUP, rows), BF16),
            pltpu.VMEM((GROUP, rows), F32),
        ],
    )


def feed_kernel(place, own_tok, far_tok, own_cot, far_cot, att, w_out, w_up, w_down, gains, biases,
                near_out, far_out, branch_out, normed2_out, active_out, back2_out, hidden_back_out, sums,
                slope):
    chunk = 512
    residual = pick_rows(own_tok, far_tok)
    branch = dot(att[...], w_out[...])
    branch_out[...] = branch
    unit1, _ = norm_parts(branch)
    middle = residual + unit1 * gains[1:2, :] + biases[1:2, :]
    unit2, _ = norm_parts(middle)
    normed2 = (unit2 * gains[2:3, :] + biases[2:3, :]).astype(BF16)
    normed2_out[...] = normed2
    ff = w_up.shape[1]
    root = math.sqrt(2.0 / math.pi)
    branch2 = jnp.zeros_like(branch)
    ahead = dot(normed2, w_up[:, :chunk])
    for start in range(0, ff, chunk):
        cols = slice(start, start + chunk)
        z = ahead
        if start + chunk < ff:
            ahead = dot(normed2, w_up[:, start + chunk : start + 2 * chunk])
        square = z * z
        bend = jnp.tanh(z * (root + (root * 0.044715) * square))
        half = 0.5 + 0.5 * bend
        active = (z * half).astype(BF16)
        active_out[:, cols] = active
        inner = (0.5 * root) + (1.5 * root * 0.044715) * square
        slope[:, cols] = half + z * (1.0 - bend * bend) * inner
        branch2 = branch2 + dot(active, w_down[cols, :])
    unit3, rstd3 = norm_parts(branch2)
    put_rows(near_out, far_out, (middle + unit3 * gains[3:4, :] + biases[3:4, :]).astype(BF16))
    upstream = pick_rows(own_cot, far_cot)
    back2 = norm_back(unit3, rstd3, gains[3:4, :], upstream).astype(BF16)
    back2_out[...] = back2

    @pl.when(pl.program_id(0) == 0)
    def _():
        sums[...] = jnp.zeros_like(sums)

    sums[0:1, :] += token_sum(upstream * unit3)
    sums[1:2, :] += token_sum(upstream)
    for start in range(0, ff, chunk):
        cols = slice(start, start + chunk)
        grad_active = dot(back2, w_down[cols, :], NT)
        hidden_back_out[:, cols] = (grad_active * slope[:, cols]).astype(BF16)


def feed(place, tokens, far_tok, cotangent, far_cot, att, w_out, w_up, w_down, gains, biases):
    rows, width = att.shape
    ff = w_up.shape[1]
    return call(
        feed_kernel,
        (rows // TILE,),
        [place],
        [
            (far_away(tokens), own_rows(width)), (far_tok, far_rows(width)),
            (far_away(cotangent), own_rows(width)), (far_cot, far_rows(width)),
            (far_away(att), row_block(width)),
            (w_out, whole(w_out.shape)), (w_up, whole(w_up.shape)), (w_down, whole(w_down.shape)),
            (gains, whole(gains.shape)), (biases, whole(biases.shape)),
        ],
        [
            (pltpu.HBM((2, rows // 2, width), BF16), own_rows(width)),
            (shape((rows // 2, width), BF16), far_rows(width)),
            (pltpu.HBM((rows, width), F32), row_block(width)),
            (shape((rows, width), BF16), row_block(width)),
            (pltpu.HBM((rows, ff), BF16), row_block(ff)),
            (shape((rows, width), BF16), row_block(width)),
            (pltpu.HBM((rows, ff), BF16), row_block(ff)),
            (shape((8, width), F32), whole((8, width))),
        ],
        [],
        "feed",
        52,
        49,
        scratch=[pltpu.VMEM((TILE, ff), F32)],
    )


def return_kernel(place, own_tok, far_tok, own_cot, far_cot, branch, hidden_back, w_out, w_up, gains, biases,
                  middle_back_out, branch_back_out, att_back_out, sums):
    unit1, rstd1 = norm_parts(branch[...])
    middle = pick_rows(own_tok, far_tok) + unit1 * gains[1:2, :] + biases[1:2, :]
    unit2, rstd2 = norm_parts(middle)
    grad2 = dot(hidden_back[...], w_up[...], NT)
    middle_back = pick_rows(own_cot, far_cot) + norm_back(unit2, rstd2, gains[2:3, :], grad2)
    middle_back_out[...] = middle_back
    branch_back = norm_back(unit1, rstd1, gains[1:2, :], middle_back).astype(BF16)
    branch_back_out[...] = branch_back
    att_back_out[...] = dot(branch_back, w_out[...], NT).astype(BF16)

    @pl.when(pl.program_id(0) == 0)
    def _():
        sums[...] = jnp.zeros_like(sums)

    sums[0:1, :] += token_sum(middle_back * unit1)
    sums[1:2, :] += token_sum(middle_back)
    sums[2:3, :] += token_sum(grad2 * unit2)
    sums[3:4, :] += token_sum(grad2)


def return_pass(place, tokens, far_tok, cotangent, far_cot, branch, hidden_back, w_out, w_up,
                gains, biases, deps):
    rows, width = branch.shape
    ff = w_up.shape[1]
    return call(
        return_kernel,
        (rows // TILE,),
        [place],
        [
            (far_away(tokens), own_rows(width)), (far_tok, far_rows(width)),
            (far_away(cotangent), own_rows(width)), (far_cot, far_rows(width)),
            (far_away(branch), row_block(width)), (far_away(hidden_back), row_block(ff)),
            (far_away(w_out), whole(w_out.shape)), (far_away(w_up), whole(w_up.shape)),
            (gains, whole(gains.shape)), (biases, whole(biases.shape)),
        ],
        [
            (pltpu.HBM((rows, width), F32), row_block(width)),
            (shape((rows, width), BF16), row_block(width)),
            (shape((rows, width), BF16), row_block(width)),
            (shape((8, width), F32), whole((8, width))),
        ],
        deps,
        "return_pass",
        32,
        24,
    )


def attend_back_kernel(info, q, k, v, att, grad, stats, cos_t, sin_t, back,
                       q_heads, k_heads, v_heads, g_heads, q_t, k_t, g_t, inner, q_acc, k_acc, v_acc):
    heads = GROUP // HEAD_DIM
    half = HEAD_DIM // 2
    blocks = q.shape[0] // TILE
    rows_all = blocks * TILE
    for i in range(blocks):
        rows = slice(i * TILE, (i + 1) * TILE)
        at = pl.multiple_of(info[i] * TILE, TILE)
        spot = pl.ds(at, TILE)
        q_t[:, spot] = q[rows, :].T
        k_t[:, spot] = k[rows, :].T
        grad_t = grad[rows, :].T
        g_t[:, spot] = grad_t
        product = att[rows, :].T.astype(F32) * grad_t.astype(F32)
        for h in range(heads):
            lanes = slice(h * HEAD_DIM, (h + 1) * HEAD_DIM)
            q_heads[h, spot, :] = q[rows, lanes]
            k_heads[h, spot, :] = k[rows, lanes]
            v_heads[h, spot, :] = v[rows, lanes]
            g_heads[h, spot, :] = grad[rows, lanes]
            inner[pl.ds(h, 1), spot] = jnp.sum(product[lanes, :], axis=0, keepdims=True)

    def one_head(h, last_ask):
        head_rows = pl.ds(pl.multiple_of(h * HEAD_DIM, HEAD_DIM), HEAD_DIM)
        for block in range(blocks):
            keys = slice(block * TILE, (block + 1) * TILE)
            cols = slice(block * TILE, last_ask(block))
            scores = dot(k_heads[h, keys, :], q_t[head_rows, cols])
            low = scores[:, :TILE]
            keys_at = lax.broadcasted_iota(jnp.int32, (TILE, TILE), 0)
            asks_at = lax.broadcasted_iota(jnp.int32, (TILE, TILE), 1)
            low = jnp.where(keys_at <= asks_at, low, -1e30)
            if scores.shape[1] > TILE:
                scores = jnp.concatenate([low, scores[:, TILE:]], axis=1)
            else:
                scores = low
            weights = jnp.exp(scores - stats[0, pl.ds(h, 1), cols])
            weight_back = dot(v_heads[h, keys, :], g_t[head_rows, cols])
            score_back = (weights * (weight_back - inner[pl.ds(h, 1), cols])).astype(BF16)
            v_acc[h, keys, :] = dot(weights.astype(BF16), g_heads[h, cols, :])
            k_acc[h, keys, :] = dot(score_back, q_heads[h, cols, :])
            change = dot(k_t[head_rows, keys], score_back)
            if block == 0:
                q_acc[head_rows, cols] = change
            elif last_ask(0) < rows_all:
                q_acc[head_rows, cols] = change
            else:
                q_acc[head_rows, cols] += change

    many = info[blocks] != 0

    @pl.when(jnp.logical_not(many))
    def _():
        @pl.loop(0, heads)
        def _(h):
            one_head(h, lambda block: rows_all)

    @pl.when(many)
    def _():
        @pl.loop(0, heads)
        def _(h):
            one_head(h, lambda block: (block + 1) * TILE)

    scale = 1.0 / math.sqrt(HEAD_DIM)
    for i in range(blocks):
        rows = slice(i * TILE, (i + 1) * TILE)
        spot = pl.ds(pl.multiple_of(info[i] * TILE, TILE), TILE)
        cos = cos_t[:, rows]
        sin = sin_t[:, rows]

        def turn_back(parts, factor):
            turned = []
            for part in parts:
                first, second = part[:half], part[half:]
                turned.append(first * cos + second * sin)
                turned.append(second * cos - first * sin)
            return (jnp.concatenate(turned, axis=0) * factor).T.astype(BF16)

        back[0, rows, :] = turn_back(
            [q_acc[h * HEAD_DIM : (h + 1) * HEAD_DIM, spot] for h in range(heads)], scale
        )
        back[1, rows, :] = turn_back([k_acc[h, spot, :].T for h in range(heads)], 1.0)
        back[2, rows, :] = jnp.concatenate(
            [v_acc[h, spot, :] for h in range(heads)], axis=1
        ).astype(BF16)


def attend_back(info, mixed, att, grad, stats, cos_t, sin_t, half, deps):
    rows, wide = mixed.shape
    width = wide // 3
    groups = width // GROUP
    heads = GROUP // HEAD_DIM
    first = half * (groups // 2)
    spec = lambda shift: pl.BlockSpec((rows, GROUP), lambda i, s: (0, i + first + shift * groups))
    per_head = pltpu.VMEM((heads, rows, HEAD_DIM), BF16)
    turned = pltpu.VMEM((GROUP, rows), BF16)
    angles = pl.BlockSpec((HEAD_DIM // 2, rows), lambda i, s: (0, 0))
    return call(
        attend_back_kernel,
        (groups // 2,),
        [info],
        [
            (far_away(mixed), spec(0)), (far_away(mixed), spec(1)), (far_away(mixed), spec(2)),
            (far_away(att), spec(0)), (far_away(grad), spec(0)),
            (stats, pl.BlockSpec((1, heads, rows), lambda i, s: (i + first, 0, 0))),
            (cos_t, angles), (sin_t, angles),
        ],
        [
            (
                pltpu.HBM((3, rows, 2 * GROUP), BF16),
                pl.BlockSpec((3, rows, GROUP), lambda i, s: (0, 0, i)),
            ),
        ],
        deps,
        "attend_back",
        32,
        24,
        scratch=[
            per_head, per_head, per_head, per_head,
            turned, turned, turned,
            pltpu.VMEM((8, rows), F32),
            pltpu.VMEM((GROUP, rows), F32),
            pltpu.VMEM((heads, rows, HEAD_DIM), F32),
            pltpu.VMEM((heads, rows, HEAD_DIM), F32),
        ],
    )[0]


def finish_kernel(place, own_tok, far_tok, middle_back, left_back, right_back, w_qkv, gains,
                  near_out, far_out, sums):
    half = left_back.shape[2]
    unit, rstd = norm_parts(pick_rows(own_tok, far_tok))
    grad = None
    for part in range(3):
        for side, back in enumerate((left_back, right_back)):
            start = (2 * part + side) * half
            term = dot(back[part], w_qkv[:, start : start + half], NT)
            grad = term if grad is None else grad + term
    back = middle_back[...] + norm_back(unit, rstd, gains[0:1, :], grad)
    put_rows(near_out, far_out, back.astype(BF16))

    @pl.when(pl.program_id(0) == 0)
    def _():
        sums[...] = jnp.zeros_like(sums)

    sums[0:1, :] += token_sum(grad * unit)
    sums[1:2, :] += token_sum(grad)


def finish(place, tokens, far_tok, middle_back, left_back, right_back, w_qkv, gains, deps):
    rows, width = middle_back.shape
    parts = pl.BlockSpec((3, TILE, width // 2), lambda i, *_: (0, i, 0))
    return call(
        finish_kernel,
        (rows // TILE,),
        [place],
        [
            (far_away(tokens), own_rows(width)), (far_tok, far_rows(width)),
            (far_away(middle_back), row_block(width)), (far_away(left_back), parts), (far_away(right_back), parts),
            (far_away(w_qkv), whole(w_qkv.shape)), (gains, whole(gains.shape)),
        ],
        [
            (pltpu.HBM((2, rows // 2, width), BF16), own_rows(width)),
            (shape((rows // 2, width), BF16), far_rows(width)),
            (shape((8, width), F32), whole((8, width))),
        ],
        deps,
        "finish",
        24,
        8,
    )


def weight_grad_kernel(source_count, out_count, place, *refs):
    outs = refs[-out_count:]
    addends = refs[2 * source_count : -out_count]
    share = pl.num_programs(0) // out_count
    start = 0
    for number in range(source_count):
        left, right = refs[2 * number], refs[2 * number + 1]
        rights = [right] if len(right.shape) == 2 else [right.at[p] for p in range(3)]
        turned = left[...].T
        for piece in rights:
            cols = slice(start, start + piece.shape[1])
            start = cols.stop
            total = dot(turned, piece[...])
            for addend in addends:
                total = total + addend[:, cols].astype(F32)
            total = total.astype(BF16)
            if out_count == 1:
                outs[0][:, cols] = total
                continue
            for turn, out in enumerate(outs):

                @pl.when(pl.program_id(0) // share == turn)
                def _(out=out, cols=cols, total=total):
                    out[:, cols] = total


def swap_wide(rows, bit):
    size = lax.axis_size("wide")
    return lax.ppermute(rows, "wide", [(i, i ^ bit) for i in range(size)])


def swap_narrow(rows):
    return lax.ppermute(rows, "narrow", [(0, 1), (1, 0)])


def swap_crossed(rows, first):
    pairs = []
    for i in range(lax.axis_size("wide")):
        for n in range(2):
            along_x = (i % 2 == 0) == first
            peer = (i, 1 - n) if along_x else (i ^ 2, n)
            pairs.append((2 * i + n, 2 * peer[0] + peer[1]))
    return lax.ppermute(rows, ("wide", "narrow"), pairs)


def swap_two(rows, even_bit, odd_bit):
    size = lax.axis_size("wide")
    return lax.ppermute(
        rows, "wide", [(i, i ^ (even_bit if i % 2 == 0 else odd_bit)) for i in range(size)]
    )


def pair_sum(mine, theirs):
    return (mine.astype(F32) + theirs.astype(F32)).astype(BF16)


def choose(which, bit):
    return jnp.where(which == 1, bit, 1 - bit)


class Reduction:
    def __init__(self, place, sources, rows, cols, halves, us):
        self.place, self.sources = place, sources
        self.rows, self.cols, self.halves, self.us = rows, cols, halves, us
        self.bits = []
        bit = 4
        while bit < lax.axis_size("wide"):
            self.bits.append(bit)
            bit *= 2

    def blocks(self, steps, core_of, pair_of, addends, deps, outs=1):
        tokens = self.sources[0][0].shape[0]

        def at(place_of):
            def index(i, h, place):
                core = core_of(place)
                first, second = pair_of(i, place)
                x = jnp.where(core == 0, first, second)
                b = jnp.where(core == 0, second, first)
                return place_of(x, core, b, h)

            return index

        inputs = []
        for left, left_of, right, right_of, width in self.sources:
            inputs.append((left, pl.BlockSpec((tokens, self.rows), at(left_of))))
            dims = (tokens, width) if right.ndim == 2 else (3, tokens, width)
            inputs.append((right, pl.BlockSpec(dims, at(right_of))))
        block = (self.rows, self.cols // self.halves)
        share = steps // outs
        for array, row in addends:
            inputs.append((array, pl.BlockSpec(block, lambda i, h, place, row=row: (row(i), h))))
        return call(
            functools.partial(weight_grad_kernel, len(self.sources), outs),
            (steps, self.halves),
            [self.place],
            inputs,
            [
                (
                    shape((share * self.rows, self.cols), BF16),
                    pl.BlockSpec(
                        block, lambda i, h, place, at=turn * share: (jnp.clip(i - at, 0, share - 1), h)
                    ),
                )
                for turn in range(outs)
            ],
            deps,
            "weight_grad",
            24,
            0.15 + 0.1 * self.us * steps,
        )

    def far(self, deps):
        pair_of = lambda i, place: (choose(i // 2, place[4]), choose(i % 2, place[3]))
        sent = self.blocks(4, lambda place: 1 - place[1], pair_of, [], deps, outs=2)
        self.core = [swap_wide(part, 1) for part in sent]
        return sent[0]

    def first(self, deps):
        pair_of = lambda i, place: (1 - place[3], choose(i, place[4]))
        sent = self.blocks(
            2, lambda place: place[1], pair_of, [(self.core[0], lambda i: i)], deps + self.core[1:]
        )[0]
        self.near = swap_crossed(sent, True)
        return sent

    def second(self, deps):
        pair_of = lambda i, place: (place[3], 1 - place[4])
        addends = [(self.core[1], lambda i: 0), (self.near, lambda i: 0)]
        sent = self.blocks(1, lambda place: place[1], pair_of, addends, deps)[0]
        self.side = swap_crossed(sent, False)
        return sent

    def keep(self, deps):
        pair_of = lambda i, place: (place[3], place[4])
        addends = [(self.core[1], lambda i: 1), (self.near, lambda i: 1), (self.side, lambda i: 0)]
        self.total = self.blocks(1, lambda place: place[1], pair_of, addends, deps)[0]
        self.hop = 0
        self.send()
        return self.total

    def send(self):
        self.got = swap_two(self.total, self.bits[self.hop], self.bits[-1 - self.hop])
        self.hop += 1

    def step(self, dep):
        self.total = pair_sum(self.total, tie(self.got, dep))
        if self.hop < len(self.bits):
            self.send()
        else:
            self.from_core = swap_wide(self.total, 1)
        return self.total

    def open(self, dep):
        self.from_y = swap_wide(tie(self.total, dep), 2)

    def spread(self, dep):
        self.from_y = tie(self.from_y, dep)
        self.from_both = swap_wide(self.from_y, 1)
        return self.from_y

    def pieces(self):
        return [self.total, self.from_y, self.from_core, self.from_both]


def gather_kernel(place, *refs):
    out = refs[-1]
    for number, piece in enumerate(refs[:4]):

        @pl.when(pl.program_id(0) == number)
        def _(piece=piece):
            out[...] = piece[...].astype(F32)


def piece_owner(number, place):
    c = jnp.where(number < 2, place[1], 1 - place[1])
    b = jnp.where(number % 2 == 0, place[2], 1 - place[2])
    return c, b


def gather(place, pieces, dims, cols, first, parts, block_at, deps):
    rows = pieces[0].shape[0]

    def part_of(number):
        def index(i, h, place):
            turn = jnp.where(i == number, h, jnp.where(i < number, 0, parts - 1))
            return (0, first + turn)

        return pl.BlockSpec((rows, cols), index)

    return call(
        gather_kernel,
        (4, parts),
        [place],
        [(piece, part_of(number)) for number, piece in enumerate(pieces)],
        [
            (
                shape(dims, F32),
                pl.BlockSpec(
                    (rows, cols), lambda i, h, place: block_at(*piece_owner(i, place), h)
                ),
            )
        ],
        deps,
        "gather",
        20,
        6,
    )[0]


def gather_mixed_kernel(place, *refs):
    out = refs[-1]
    quarter = refs[0].shape[1]
    mine = pl.program_id(0) == place[1]
    for core in range(2):

        @pl.when(mine == (core == 0))
        def _(core=core):
            for other in range(2):
                b = place[2] if other == 0 else 1 - place[2]
                at = pl.multiple_of(b * quarter, quarter)
                out[:, pl.ds(at, quarter)] = refs[2 * core + other][...].astype(F32)


def gather_mixed(place, pieces, dims, first, half, earlier, deps):
    piece = pl.BlockSpec((TILE, TILE), lambda i, p, place: (0, first + p))
    return call(
        gather_mixed_kernel,
        (2, 3),
        [place],
        [(array, piece) for array in pieces],
        [
            (
                shape(dims, F32),
                pl.BlockSpec((TILE, 2 * TILE), lambda i, p, place: (i, 2 * p + half)),
            )
        ],
        earlier + deps,
        "gather_mixed",
        16,
        4,
        aliases={5: 0} if earlier else None,
    )[0]


def local(tokens, doc_ids, w_qkv, w_out, w_up, w_down, norm_gains, norm_biases, cotangent):
    narrow_size = lax.axis_size("narrow")
    packs, tok_rows, width = tokens.shape
    assert narrow_size == 2 and packs == 2 and tok_rows == 2 * TILE
    pack_len = tok_rows * narrow_size
    ff = w_up.shape[1]
    n = lax.axis_index("narrow")
    w = lax.axis_index("wide")
    core = w % 2
    side = (w // 2) % 2
    place = jnp.stack(
        [n, core, side, jnp.where(core == 0, n, side), jnp.where(core == 0, side, n)]
    ).astype(jnp.int32)
    pick = lambda array, index: lax.dynamic_index_in_dim(array, index, 0, keepdims=False)

    far_tok = swap_narrow(pick(tokens, 1 - n))
    doc_row = pick(doc_ids, n)
    many = (doc_row[pack_len - 1] != 0).astype(jnp.int32)
    block_at = jnp.stack([n, 3 - n, 1 - n, 2 + n]).astype(jnp.int32)
    info = jnp.concatenate([block_at, many[None]])

    halves = HEAD_DIM // 2
    frequency = jnp.exp(
        -math.log(10000.0) * jnp.arange(halves, dtype=F32) * 2.0 / HEAD_DIM
    )
    places = (block_at[:, None] * TILE + jnp.arange(TILE, dtype=jnp.int32)[None, :]).reshape(-1)
    angles_t = frequency[:, None] * places.astype(F32)[None, :]
    cos_t = jnp.cos(angles_t)
    sin_t = jnp.sin(angles_t)
    cos = cos_t.T
    sin = sin_t.T
    cosine = jnp.concatenate([cos] * 4, axis=1)
    sine = jnp.concatenate([-sin, sin, -sin, sin], axis=1)

    early = project(
        place, tokens, w_qkv, norm_gains, norm_biases, cosine, sine, 0, (), pack_len
    )
    far_cot = swap_narrow(tie(pick(cotangent, 1 - n), early[0]))
    normed, mixed = project(
        place, far_tok, w_qkv, norm_gains, norm_biases, cosine, sine, 2, early, pack_len
    )
    att, stats = attend(info, mixed)
    near_out, far_out, branch, normed2, active, back2, hidden_back, sums3 = feed(
        place, tokens, far_tok, cotangent, far_cot, att, w_out, w_up, w_down,
        norm_gains, norm_biases,
    )
    half_wide = width // 2
    down = Reduction(
        place,
        [(far_away(active), lambda x, c, b, h: (0, 4 * x + 2 * c + b),
          back2, lambda x, c, b, h: (0, 0), width)],
        2 * TILE, width, 1, 1.5,
    )
    up = Reduction(
        place,
        [(normed2, lambda x, c, b, h: (0, x),
          far_away(hidden_back), lambda x, c, b, h: (0, 2 * c + b), width)],
        2 * TILE, width, 1, 1.5,
    )
    last = down.far([])
    last = up.far([last])
    last = down.first([last])
    last = up.first([last])
    middle_back, branch_back, att_back, sums12 = return_pass(
        place, tokens, far_tok, cotangent, far_cot, branch, hidden_back, w_out, w_up,
        norm_gains, norm_biases, [last],
    )

    def back(half, deps):
        return attend_back(info, mixed, att, att_back, stats, cos_t, sin_t, half, deps)

    last = down.second([sums12])
    left_back = back(0, [last])
    by_rows = lambda x, c, b, h: (0, 2 * x + c)
    by_parts = lambda x, c, b, h: (0, 0, b)
    left = Reduction(
        place,
        [(far_away(att), by_rows, branch_back, lambda x, c, b, h: (0, b), half_wide),
         (normed, by_rows, far_away(left_back), by_parts, TILE)],
        TILE, 5 * TILE, 1, 1.2,
    )
    last = up.second([far_away(left_back)])
    last = down.keep([last])
    last = left.far([last])
    last = up.keep([last])
    got_out = swap_narrow(tie(far_out, last))
    right_back = back(1, [last])
    last = left.first([far_away(right_back), got_out])
    last = down.step(last)
    right = Reduction(
        place, [(normed, by_rows, far_away(right_back), by_parts, TILE)], TILE, 3 * TILE, 1, 0.8
    )
    last = right.far([last])
    last = up.step(last)
    near_grad, far_grad, sums0 = finish(
        place, tokens, far_tok, middle_back, left_back, right_back, w_qkv, norm_gains, [last]
    )
    last = left.second([sums0])
    last = right.first([last])
    extra = len(down.bits) - 2
    for _ in range(extra):
        last = down.step(last)
    last = down.step(last)
    down.open(last)
    last = left.keep([last, down.from_core])
    last = right.second([last])
    norm_term = jnp.concatenate(
        [sums0[0:1], sums12[0:1], sums12[2:3], sums3[0:1],
         sums0[1:2], sums12[1:2], sums12[3:4], sums3[1:2]], axis=0
    )
    hops = [2 ** bit for bit in range(lax.axis_size("wide").bit_length() - 1)]

    def norm_step(last):
        nonlocal norm_term, norm_got
        norm_term = norm_term + tie(norm_got, last)
        if hops:
            norm_got = swap_wide(norm_term, hops.pop(0))
        return norm_term

    norm_got = swap_narrow(tie(norm_term, last))
    for _ in range(extra):
        last = up.step(last)
    last = up.step(last)
    last = norm_step(last)
    last = right.keep([last])
    up.open(last)
    last = norm_step(last)
    for _ in range(extra):
        last = left.step(last)
        last = right.step(last)
    last = left.step(last)
    last = right.step(last)
    got_grad = swap_narrow(tie(far_grad, last))
    last = down.spread(last)
    grad_down = gather(
        place, down.pieces(), (ff // 2, width), half_wide, 0, 2,
        lambda c, b, h: (2 * c + b, h), [last],
    )
    last = norm_step(grad_down)
    out = lax.dynamic_update_slice(near_out, tie(got_out, last)[None], (1 - n, 0, 0))
    last = left.step(last)
    left.open(last)
    last = right.step(last)
    right.open(last)
    last = norm_step(last)
    last = up.spread(last)
    grad_up = gather(
        place, up.pieces(), (half_wide, ff), half_wide, 0, 2,
        lambda c, b, h: (0, 2 * (2 * c + b) + h), [last],
    )
    last = grad_up
    while hops:
        last = norm_step(last)
    last = norm_step(last)
    grad_tok = lax.dynamic_update_slice(near_grad, tie(got_grad, last)[None], (1 - n, 0, 0))
    last = left.spread(last)
    grad_out_proj = gather(
        place, left.pieces(), (half_wide, width), half_wide, 0, 1,
        lambda c, b, h: (c, b), [last],
    )
    grad_qkv = gather_mixed(
        place, left.pieces(), (half_wide, 3 * width), 2, 0, [], [last]
    )
    right.spread(grad_qkv)
    grad_qkv = gather_mixed(
        place, right.pieces(), (half_wide, 3 * width), 0, 1, [grad_qkv], []
    )
    norm_term = lax.dynamic_slice_in_dim(norm_term, n * half_wide, half_wide, 1)
    return (
        out,
        grad_tok,
        grad_qkv,
        grad_out_proj,
        grad_up,
        grad_down,
        norm_term[:4],
        norm_term[4:],
    )


def solution(mesh):
    rows = P("wide", "narrow", None)
    return jax.shard_map(
        local,
        mesh=mesh,
        in_specs=(rows, P("wide", None), P(), P(), P(), P(), P(), P(), rows),
        out_specs=(
            rows, rows,
            P("narrow", None), P("narrow", None), P("narrow", None), P("narrow", None),
            P(None, "narrow"), P(None, "narrow"),
        ),
        check_vma=False,
    )
```

```python
import functools
import math

import jax
import jax.numpy as jnp
from jax import lax
from jax.experimental import pallas as pl
from jax.experimental.pallas import tpu as pltpu
from jax.sharding import PartitionSpec as P

HEAD_DIM = 64
EPS = 1e-05
F32 = jnp.float32
BF16 = jnp.bfloat16
TILE = 256
GROUP = 256
FLOPS_PER_US = 1000000000
NN = (((1,), (0,)), ((), ()))
NT = (((1,), (1,)), ((), ()))
TN = (((0,), (0,)), ((), ()))


def dot(left, right, dims=NN):
    return lax.dot_general(left, right, dims, preferred_element_type=F32)


def call(kernel, grid, prefetch, inputs, outputs, deps, name, vmem, us, scratch=(), aliases=None):
    given = len(prefetch) + len(inputs)

    def body(*refs):
        kernel(*refs[:given], *refs[given + len(deps) :])

    in_specs = [spec for _, spec in inputs] + [pl.BlockSpec(memory_space=pl.ANY)] * len(deps)
    return pl.pallas_call(
        body,
        grid_spec=pltpu.PrefetchScalarGridSpec(
            num_scalar_prefetch=len(prefetch),
            grid=grid,
            in_specs=in_specs,
            out_specs=tuple(spec for _, spec in outputs),
            scratch_shapes=list(scratch),
        ),
        out_shape=tuple(shape for shape, _ in outputs),
        input_output_aliases=aliases or {},
        compiler_params=pltpu.CompilerParams(vmem_limit_bytes=vmem * 1024 * 1024),
        cost_estimate=pl.CostEstimate(
            flops=int(us * FLOPS_PER_US), transcendentals=0, bytes_accessed=1
        ),
        name=name,
    )(*prefetch, *[array for array, _ in inputs], *deps)


def shape(dims, dtype):
    return jax.ShapeDtypeStruct(dims, dtype)


def far_away(array):
    return pltpu.with_memory_space_constraint(array, pltpu.HBM)


def whole(dims):
    return pl.BlockSpec(dims, lambda *_: (0,) * len(dims), pipeline_mode=pl.Buffered(1))


def row_block(size):
    return pl.BlockSpec((TILE, size), lambda i, *_: (i, 0))


def own_rows(size):
    return pl.BlockSpec((1, TILE, size), lambda i, place, *_: (place[0], jnp.minimum(i, 1), 0))


def far_rows(size):
    return pl.BlockSpec((TILE, size), lambda i, *_: (jnp.maximum(i - 2, 0), 0))


def pick_rows(own, far):
    return jnp.where(pl.program_id(0) < 2, own[0].astype(F32), far[...].astype(F32))


def put_rows(near, far, rows):
    @pl.when(pl.program_id(0) < 2)
    def _():
        near[0] = rows

    @pl.when(pl.program_id(0) >= 2)
    def _():
        far[...] = rows


def tie(array, *deps):
    return lax.optimization_barrier((array,) + deps)[0]


def norm_parts(rows):
    centre = rows - jnp.mean(rows, axis=-1, keepdims=True)
    rstd = lax.rsqrt(jnp.mean(centre * centre, axis=-1, keepdims=True) + EPS)
    return centre * rstd, rstd


def norm_back(unit, rstd, gain, grad):
    scaled = grad * gain
    first = jnp.mean(scaled, axis=-1, keepdims=True)
    second = jnp.mean(scaled * unit, axis=-1, keepdims=True)
    return rstd * (scaled - first - unit * second)


def token_sum(rows):
    return jnp.sum(rows, axis=0, keepdims=True)


def project_kernel(place, tok, w, gains, biases, cosine, sine, normed_out, mixed_out):
    rows = tok[0] if len(tok.shape) == 3 else tok[...]
    unit, _ = norm_parts(rows.astype(F32))
    normed = (unit * gains[0:1, :] + biases[0:1, :]).astype(BF16)
    normed_out[...] = normed
    width = normed.shape[1]
    lanes = lax.broadcasted_iota(jnp.int32, (TILE, 128), 1)
    first_half = lanes % HEAD_DIM < HEAD_DIM // 2
    scale = 1.0 / math.sqrt(HEAD_DIM)
    cos = cosine[...]
    sin = sine[...]
    for start in range(0, 3 * width, 256):
        part = dot(normed, w[:, start : start + 256])
        if start >= 2 * width:
            mixed_out[:, start : start + 256] = part.astype(BF16)
            continue
        for sub in range(0, 256, 128):
            u = part[:, sub : sub + 128]
            turned = jnp.where(first_half, pltpu.roll(u, 96, 1), pltpu.roll(u, 32, 1))
            out = u * cos + turned * sin
            out = out.astype(BF16)
            if start < width:
                out = out * jnp.asarray(scale, BF16)
            mixed_out[:, start + sub : start + sub + 128] = out


def project(place, tok, w_qkv, gains, biases, cosine, sine, first_block, earlier, pack_len):
    width, wide = w_qkv.shape
    steps = tok.shape[-2] // TILE
    at = lambda size: pl.BlockSpec((TILE, size), lambda i, *_: (i + first_block, 0))
    own = tok.ndim == 3
    return call(
        project_kernel,
        (steps,),
        [place],
        [
            (tok, own_rows(width) if own else row_block(width)),
            (far_away(w_qkv), whole(w_qkv.shape)),
            (gains, whole(gains.shape)),
            (biases, whole(biases.shape)),
            (cosine, at(128)),
            (sine, at(128)),
        ],
        [
            (pltpu.HBM((pack_len, width), BF16), at(width)),
            (pltpu.HBM((pack_len, wide), BF16), at(wide)),
        ],
        [far_away(array) for array in earlier],
        "project",
        24,
        8,
        aliases={7: 0, 8: 1} if earlier else None,
    )


def diagonal_mask(scores):
    size = scores.shape[1]
    first = scores.shape[0] - size
    keys = lax.broadcasted_iota(jnp.int32, (size, size), 0)
    asks = lax.broadcasted_iota(jnp.int32, (size, size), 1)
    tail = jnp.where(keys <= asks, scores[first:], -1e30)
    if first == 0:
        return tail
    return jnp.concatenate([scores[:first], tail], axis=0)


def attend_kernel(info, q, k, v, out, stats, key_heads, q_t, v_t, out_t):
    heads = GROUP // HEAD_DIM
    blocks = q.shape[0] // TILE
    for i in range(blocks):
        rows = slice(i * TILE, (i + 1) * TILE)
        at = pl.multiple_of(info[i] * TILE, TILE)
        q_t[:, pl.ds(at, TILE)] = q[rows, :].T
        v_t[:, pl.ds(at, TILE)] = v[rows, :].T
        for h in range(heads):
            key_heads[h, pl.ds(at, TILE), :] = k[rows, h * HEAD_DIM : (h + 1) * HEAD_DIM]

    def one_head(h, first_key):
        head_rows = pl.ds(pl.multiple_of(h * HEAD_DIM, HEAD_DIM), HEAD_DIM)
        for block in range(blocks):
            cols = slice(block * TILE, (block + 1) * TILE)
            keys = slice(first_key(block), (block + 1) * TILE)
            scores = diagonal_mask(dot(key_heads[h, keys, :], q_t[head_rows, cols]))
            peak = jnp.max(scores, axis=0, keepdims=True)
            weights = jnp.exp(scores - peak)
            total = jnp.sum(weights, axis=0, keepdims=True)
            mixed = dot(v_t[head_rows, keys], weights.astype(BF16))
            out_t[head_rows, cols] = mixed * (1.0 / total)
            stats[0, pl.ds(h, 1), cols] = peak + jnp.log(total)

    many = info[blocks] != 0

    @pl.when(jnp.logical_not(many))
    def _():
        @pl.loop(0, heads, unroll=2)
        def _(h):
            one_head(h, lambda block: 0)

    @pl.when(many)
    def _():
        @pl.loop(0, heads, unroll=2)
        def _(h):
            one_head(h, lambda block: block * TILE)

    for i in range(blocks):
        at = pl.multiple_of(info[i] * TILE, TILE)
        out[i * TILE : (i + 1) * TILE, :] = out_t[:, pl.ds(at, TILE)].T.astype(BF16)


def attend(info, mixed):
    rows, wide = mixed.shape
    width = wide // 3
    groups = width // GROUP
    heads = GROUP // HEAD_DIM
    part = lambda shift: pl.BlockSpec((rows, GROUP), lambda g, s: (0, g + shift * groups))
    return call(
        attend_kernel,
        (groups,),
        [info],
        [(far_away(mixed), part(0)), (far_away(mixed), part(1)), (far_away(mixed), part(2))],
        [
            (pltpu.HBM((rows, width), BF16), part(0)),
            (
                shape((groups, heads, rows), F32),
                pl.BlockSpec((1, heads, rows), lambda g, s: (g, 0, 0)),
            ),
        ],
        [],
        "attend",
        24,
        36,
        scratch=[
            pltpu.VMEM((heads, rows, HEAD_DIM), BF16),
            pltpu.VMEM((GROUP, rows), BF16),
            pltpu.VMEM((GROUP, rows), BF16),
            pltpu.VMEM((GROUP, rows), F32),
        ],
    )


def feed_kernel(place, own_tok, far_tok, own_cot, far_cot, att, w_out, w_up, w_down, gains, biases,
                near_out, far_out, branch_out, normed2_out, active_out, back2_out, hidden_back_out, sums,
                slope):
    chunk = 512
    residual = pick_rows(own_tok, far_tok)
    branch = dot(att[...], w_out[...])
    branch_out[...] = branch
    unit1, _ = norm_parts(branch)
    middle = residual + unit1 * gains[1:2, :] + biases[1:2, :]
    unit2, _ = norm_parts(middle)
    normed2 = (unit2 * gains[2:3, :] + biases[2:3, :]).astype(BF16)
    normed2_out[...] = normed2
    ff = w_up.shape[1]
    root = math.sqrt(2.0 / math.pi)
    branch2 = jnp.zeros_like(branch)
    ahead = dot(normed2, w_up[:, :chunk])
    for start in range(0, ff, chunk):
        cols = slice(start, start + chunk)
        z = ahead
        if start + chunk < ff:
            ahead = dot(normed2, w_up[:, start + chunk : start + 2 * chunk])
        square = z * z
        bend = jnp.tanh(z * (root + (root * 0.044715) * square))
        half = 0.5 + 0.5 * bend
        active = (z * half).astype(BF16)
        active_out[:, cols] = active
        inner = (0.5 * root) + (1.5 * root * 0.044715) * square
        slope[:, cols] = half + z * (1.0 - bend * bend) * inner
        branch2 = branch2 + dot(active, w_down[cols, :])
    unit3, rstd3 = norm_parts(branch2)
    put_rows(near_out, far_out, (middle + unit3 * gains[3:4, :] + biases[3:4, :]).astype(BF16))
    upstream = pick_rows(own_cot, far_cot)
    back2 = norm_back(unit3, rstd3, gains[3:4, :], upstream).astype(BF16)
    back2_out[...] = back2

    @pl.when(pl.program_id(0) == 0)
    def _():
        sums[...] = jnp.zeros_like(sums)

    sums[0:1, :] += token_sum(upstream * unit3)
    sums[1:2, :] += token_sum(upstream)
    for start in range(0, ff, chunk):
        cols = slice(start, start + chunk)
        grad_active = dot(back2, w_down[cols, :], NT)
        hidden_back_out[:, cols] = (grad_active * slope[:, cols]).astype(BF16)


def feed(place, tokens, far_tok, cotangent, far_cot, att, w_out, w_up, w_down, gains, biases):
    rows, width = att.shape
    ff = w_up.shape[1]
    return call(
        feed_kernel,
        (rows // TILE,),
        [place],
        [
            (far_away(tokens), own_rows(width)), (far_tok, far_rows(width)),
            (far_away(cotangent), own_rows(width)), (far_cot, far_rows(width)),
            (far_away(att), row_block(width)),
            (w_out, whole(w_out.shape)), (w_up, whole(w_up.shape)), (w_down, whole(w_down.shape)),
            (gains, whole(gains.shape)), (biases, whole(biases.shape)),
        ],
        [
            (pltpu.HBM((2, rows // 2, width), BF16), own_rows(width)),
            (shape((rows // 2, width), BF16), far_rows(width)),
            (pltpu.HBM((rows, width), F32), row_block(width)),
            (shape((rows, width), BF16), row_block(width)),
            (pltpu.HBM((rows, ff), BF16), row_block(ff)),
            (shape((rows, width), BF16), row_block(width)),
            (pltpu.HBM((rows, ff), BF16), row_block(ff)),
            (shape((8, width), F32), whole((8, width))),
        ],
        [],
        "feed",
        52,
        49,
        scratch=[pltpu.VMEM((TILE, ff), F32)],
    )


def return_kernel(place, own_tok, far_tok, own_cot, far_cot, branch, hidden_back, w_out, w_up, gains, biases,
                  middle_back_out, branch_back_out, att_back_out, sums):
    unit1, rstd1 = norm_parts(branch[...])
    middle = pick_rows(own_tok, far_tok) + unit1 * gains[1:2, :] + biases[1:2, :]
    unit2, rstd2 = norm_parts(middle)
    grad2 = dot(hidden_back[...], w_up[...], NT)
    middle_back = pick_rows(own_cot, far_cot) + norm_back(unit2, rstd2, gains[2:3, :], grad2)
    middle_back_out[...] = middle_back
    branch_back = norm_back(unit1, rstd1, gains[1:2, :], middle_back).astype(BF16)
    branch_back_out[...] = branch_back
    att_back_out[...] = dot(branch_back, w_out[...], NT).astype(BF16)

    @pl.when(pl.program_id(0) == 0)
    def _():
        sums[...] = jnp.zeros_like(sums)

    sums[0:1, :] += token_sum(middle_back * unit1)
    sums[1:2, :] += token_sum(middle_back)
    sums[2:3, :] += token_sum(grad2 * unit2)
    sums[3:4, :] += token_sum(grad2)


def return_pass(place, tokens, far_tok, cotangent, far_cot, branch, hidden_back, w_out, w_up,
                gains, biases, deps):
    rows, width = branch.shape
    ff = w_up.shape[1]
    return call(
        return_kernel,
        (rows // TILE,),
        [place],
        [
            (far_away(tokens), own_rows(width)), (far_tok, far_rows(width)),
            (far_away(cotangent), own_rows(width)), (far_cot, far_rows(width)),
            (far_away(branch), row_block(width)), (far_away(hidden_back), row_block(ff)),
            (far_away(w_out), whole(w_out.shape)), (far_away(w_up), whole(w_up.shape)),
            (gains, whole(gains.shape)), (biases, whole(biases.shape)),
        ],
        [
            (pltpu.HBM((rows, width), F32), row_block(width)),
            (shape((rows, width), BF16), row_block(width)),
            (shape((rows, width), BF16), row_block(width)),
            (shape((8, width), F32), whole((8, width))),
        ],
        deps,
        "return_pass",
        32,
        24,
    )


def attend_back_kernel(info, q, k, v, att, grad, stats, cos_t, sin_t, back,
                       q_heads, k_heads, v_heads, g_heads, q_t, k_t, g_t, inner, q_acc, k_acc, v_acc):
    heads = GROUP // HEAD_DIM
    half = HEAD_DIM // 2
    blocks = q.shape[0] // TILE
    rows_all = blocks * TILE
    for i in range(blocks):
        rows = slice(i * TILE, (i + 1) * TILE)
        at = pl.multiple_of(info[i] * TILE, TILE)
        spot = pl.ds(at, TILE)
        q_t[:, spot] = q[rows, :].T
        k_t[:, spot] = k[rows, :].T
        grad_t = grad[rows, :].T
        g_t[:, spot] = grad_t
        product = att[rows, :].T.astype(F32) * grad_t.astype(F32)
        for h in range(heads):
            lanes = slice(h * HEAD_DIM, (h + 1) * HEAD_DIM)
            q_heads[h, spot, :] = q[rows, lanes]
            k_heads[h, spot, :] = k[rows, lanes]
            v_heads[h, spot, :] = v[rows, lanes]
            g_heads[h, spot, :] = grad[rows, lanes]
            inner[pl.ds(h, 1), spot] = jnp.sum(product[lanes, :], axis=0, keepdims=True)

    def one_head(h, last_ask):
        head_rows = pl.ds(pl.multiple_of(h * HEAD_DIM, HEAD_DIM), HEAD_DIM)
        for block in range(blocks):
            keys = slice(block * TILE, (block + 1) * TILE)
            cols = slice(block * TILE, last_ask(block))
            scores = dot(k_heads[h, keys, :], q_t[head_rows, cols])
            low = scores[:, :TILE]
            keys_at = lax.broadcasted_iota(jnp.int32, (TILE, TILE), 0)
            asks_at = lax.broadcasted_iota(jnp.int32, (TILE, TILE), 1)
            low = jnp.where(keys_at <= asks_at, low, -1e30)
            if scores.shape[1] > TILE:
                scores = jnp.concatenate([low, scores[:, TILE:]], axis=1)
            else:
                scores = low
            weights = jnp.exp(scores - stats[0, pl.ds(h, 1), cols])
            weight_back = dot(v_heads[h, keys, :], g_t[head_rows, cols])
            score_back = (weights * (weight_back - inner[pl.ds(h, 1), cols])).astype(BF16)
            v_acc[h, keys, :] = dot(weights.astype(BF16), g_heads[h, cols, :])
            k_acc[h, keys, :] = dot(score_back, q_heads[h, cols, :])
            change = dot(k_t[head_rows, keys], score_back)
            if block == 0:
                q_acc[head_rows, cols] = change
            elif last_ask(0) < rows_all:
                q_acc[head_rows, cols] = change
            else:
                q_acc[head_rows, cols] += change

    many = info[blocks] != 0

    @pl.when(jnp.logical_not(many))
    def _():
        @pl.loop(0, heads, unroll=2)
        def _(h):
            one_head(h, lambda block: rows_all)

    @pl.when(many)
    def _():
        @pl.loop(0, heads, unroll=2)
        def _(h):
            one_head(h, lambda block: (block + 1) * TILE)

    scale = 1.0 / math.sqrt(HEAD_DIM)
    for i in range(blocks):
        rows = slice(i * TILE, (i + 1) * TILE)
        spot = pl.ds(pl.multiple_of(info[i] * TILE, TILE), TILE)
        cos = cos_t[:, rows]
        sin = sin_t[:, rows]

        def turn_back(parts, factor):
            turned = []
            for part in parts:
                first, second = part[:half], part[half:]
                turned.append(first * cos + second * sin)
                turned.append(second * cos - first * sin)
            return (jnp.concatenate(turned, axis=0) * factor).T.astype(BF16)

        back[0, rows, :] = turn_back(
            [q_acc[h * HEAD_DIM : (h + 1) * HEAD_DIM, spot] for h in range(heads)], scale
        )
        back[1, rows, :] = turn_back([k_acc[h, spot, :].T for h in range(heads)], 1.0)
        back[2, rows, :] = jnp.concatenate(
            [v_acc[h, spot, :] for h in range(heads)], axis=1
        ).astype(BF16)


def attend_back(info, mixed, att, grad, stats, cos_t, sin_t, half, deps):
    rows, wide = mixed.shape
    width = wide // 3
    groups = width // GROUP
    heads = GROUP // HEAD_DIM
    first = half * (groups // 2)
    spec = lambda shift: pl.BlockSpec((rows, GROUP), lambda i, s: (0, i + first + shift * groups))
    per_head = pltpu.VMEM((heads, rows, HEAD_DIM), BF16)
    turned = pltpu.VMEM((GROUP, rows), BF16)
    angles = pl.BlockSpec((HEAD_DIM // 2, rows), lambda i, s: (0, 0))
    return call(
        attend_back_kernel,
        (groups // 2,),
        [info],
        [
            (far_away(mixed), spec(0)), (far_away(mixed), spec(1)), (far_away(mixed), spec(2)),
            (far_away(att), spec(0)), (far_away(grad), spec(0)),
            (stats, pl.BlockSpec((1, heads, rows), lambda i, s: (i + first, 0, 0))),
            (cos_t, angles), (sin_t, angles),
        ],
        [
            (
                pltpu.HBM((3, rows, 2 * GROUP), BF16),
                pl.BlockSpec((3, rows, GROUP), lambda i, s: (0, 0, i)),
            ),
        ],
        deps,
        "attend_back",
        32,
        24,
        scratch=[
            per_head, per_head, per_head, per_head,
            turned, turned, turned,
            pltpu.VMEM((8, rows), F32),
            pltpu.VMEM((GROUP, rows), F32),
            pltpu.VMEM((heads, rows, HEAD_DIM), F32),
            pltpu.VMEM((heads, rows, HEAD_DIM), F32),
        ],
    )[0]


def finish_kernel(place, own_tok, far_tok, middle_back, left_back, right_back, w_qkv, gains,
                  near_out, far_out, sums):
    half = left_back.shape[2]
    unit, rstd = norm_parts(pick_rows(own_tok, far_tok))
    grad = None
    for part in range(3):
        for side, back in enumerate((left_back, right_back)):
            start = (2 * part + side) * half
            term = dot(back[part], w_qkv[:, start : start + half], NT)
            grad = term if grad is None else grad + term
    back = middle_back[...] + norm_back(unit, rstd, gains[0:1, :], grad)
    put_rows(near_out, far_out, back.astype(BF16))

    @pl.when(pl.program_id(0) == 0)
    def _():
        sums[...] = jnp.zeros_like(sums)

    sums[0:1, :] += token_sum(grad * unit)
    sums[1:2, :] += token_sum(grad)


def finish(place, tokens, far_tok, middle_back, left_back, right_back, w_qkv, gains, deps):
    rows, width = middle_back.shape
    parts = pl.BlockSpec((3, TILE, width // 2), lambda i, *_: (0, i, 0))
    return call(
        finish_kernel,
        (rows // TILE,),
        [place],
        [
            (far_away(tokens), own_rows(width)), (far_tok, far_rows(width)),
            (far_away(middle_back), row_block(width)), (far_away(left_back), parts), (far_away(right_back), parts),
            (far_away(w_qkv), whole(w_qkv.shape)), (gains, whole(gains.shape)),
        ],
        [
            (pltpu.HBM((2, rows // 2, width), BF16), own_rows(width)),
            (shape((rows // 2, width), BF16), far_rows(width)),
            (shape((8, width), F32), whole((8, width))),
        ],
        deps,
        "finish",
        24,
        8,
    )


def weight_grad_kernel(source_count, out_count, place, *refs):
    outs = refs[-out_count:]
    addends = refs[2 * source_count : -out_count]
    share = pl.num_programs(0) // out_count
    start = 0
    for number in range(source_count):
        left, right = refs[2 * number], refs[2 * number + 1]
        rights = [right] if len(right.shape) == 2 else [right.at[p] for p in range(3)]
        turned = left[...].T
        for piece in rights:
            cols = slice(start, start + piece.shape[1])
            start = cols.stop
            total = dot(turned, piece[...])
            for addend in addends:
                total = total + addend[:, cols].astype(F32)
            total = total.astype(BF16)
            if out_count == 1:
                outs[0][:, cols] = total
                continue
            for turn, out in enumerate(outs):

                @pl.when(pl.program_id(0) // share == turn)
                def _(out=out, cols=cols, total=total):
                    out[:, cols] = total


def swap_wide(rows, bit):
    size = lax.axis_size("wide")
    return lax.ppermute(rows, "wide", [(i, i ^ bit) for i in range(size)])


def swap_narrow(rows):
    return lax.ppermute(rows, "narrow", [(0, 1), (1, 0)])


def swap_crossed(rows, first):
    pairs = []
    for i in range(lax.axis_size("wide")):
        for n in range(2):
            along_x = (i % 2 == 0) == first
            peer = (i, 1 - n) if along_x else (i ^ 2, n)
            pairs.append((2 * i + n, 2 * peer[0] + peer[1]))
    return lax.ppermute(rows, ("wide", "narrow"), pairs)


def swap_two(rows, even_bit, odd_bit):
    size = lax.axis_size("wide")
    return lax.ppermute(
        rows, "wide", [(i, i ^ (even_bit if i % 2 == 0 else odd_bit)) for i in range(size)]
    )


def pair_sum(mine, theirs):
    return (mine.astype(F32) + theirs.astype(F32)).astype(BF16)


def choose(which, bit):
    return jnp.where(which == 1, bit, 1 - bit)


class Reduction:
    def __init__(self, place, sources, rows, cols, halves, us):
        self.place, self.sources = place, sources
        self.rows, self.cols, self.halves, self.us = rows, cols, halves, us
        self.bits = []
        bit = 4
        while bit < lax.axis_size("wide"):
            self.bits.append(bit)
            bit *= 2

    def blocks(self, steps, core_of, pair_of, addends, deps, outs=1):
        tokens = self.sources[0][0].shape[0]

        def at(place_of):
            def index(i, h, place):
                core = core_of(place)
                first, second = pair_of(i, place)
                x = jnp.where(core == 0, first, second)
                b = jnp.where(core == 0, second, first)
                return place_of(x, core, b, h)

            return index

        inputs = []
        for left, left_of, right, right_of, width in self.sources:
            inputs.append((left, pl.BlockSpec((tokens, self.rows), at(left_of))))
            dims = (tokens, width) if right.ndim == 2 else (3, tokens, width)
            inputs.append((right, pl.BlockSpec(dims, at(right_of))))
        block = (self.rows, self.cols // self.halves)
        share = steps // outs
        for array, row in addends:
            inputs.append((array, pl.BlockSpec(block, lambda i, h, place, row=row: (row(i), h))))
        return call(
            functools.partial(weight_grad_kernel, len(self.sources), outs),
            (steps, self.halves),
            [self.place],
            inputs,
            [
                (
                    shape((share * self.rows, self.cols), BF16),
                    pl.BlockSpec(
                        block, lambda i, h, place, at=turn * share: (jnp.clip(i - at, 0, share - 1), h)
                    ),
                )
                for turn in range(outs)
            ],
            deps,
            "weight_grad",
            24,
            0.15 + 0.1 * self.us * steps,
        )

    def far(self, deps):
        pair_of = lambda i, place: (choose(i // 2, place[4]), choose(i % 2, place[3]))
        sent = self.blocks(4, lambda place: 1 - place[1], pair_of, [], deps, outs=2)
        self.core = [swap_wide(part, 1) for part in sent]
        return sent[0]

    def first(self, deps):
        pair_of = lambda i, place: (1 - place[3], choose(i, place[4]))
        sent = self.blocks(
            2, lambda place: place[1], pair_of, [(self.core[0], lambda i: i)], deps + self.core[1:]
        )[0]
        self.near = swap_crossed(sent, True)
        return sent

    def second(self, deps):
        pair_of = lambda i, place: (place[3], 1 - place[4])
        addends = [(self.core[1], lambda i: 0), (self.near, lambda i: 0)]
        sent = self.blocks(1, lambda place: place[1], pair_of, addends, deps)[0]
        self.side = swap_crossed(sent, False)
        return sent

    def keep(self, deps):
        pair_of = lambda i, place: (place[3], place[4])
        addends = [(self.core[1], lambda i: 1), (self.near, lambda i: 1), (self.side, lambda i: 0)]
        self.total = self.blocks(1, lambda place: place[1], pair_of, addends, deps)[0]
        self.hop = 0
        self.send()
        return self.total

    def send(self):
        self.got = swap_two(self.total, self.bits[self.hop], self.bits[-1 - self.hop])
        self.hop += 1

    def step(self, dep):
        self.total = pair_sum(self.total, tie(self.got, dep))
        if self.hop < len(self.bits):
            self.send()
        else:
            self.from_core = swap_wide(self.total, 1)
        return self.total

    def open(self, dep):
        self.from_y = swap_wide(tie(self.total, dep), 2)

    def spread(self, dep):
        self.from_y = tie(self.from_y, dep)
        self.from_both = swap_wide(self.from_y, 1)
        return self.from_y

    def pieces(self):
        return [self.total, self.from_y, self.from_core, self.from_both]


def gather_kernel(place, *refs):
    out = refs[-1]
    for number, piece in enumerate(refs[:4]):

        @pl.when(pl.program_id(0) == number)
        def _(piece=piece):
            out[...] = piece[...].astype(F32)


def piece_owner(number, place):
    c = jnp.where(number < 2, place[1], 1 - place[1])
    b = jnp.where(number % 2 == 0, place[2], 1 - place[2])
    return c, b


def gather(place, pieces, dims, cols, first, parts, block_at, deps):
    rows = pieces[0].shape[0]

    def part_of(number):
        def index(i, h, place):
            turn = jnp.where(i == number, h, jnp.where(i < number, 0, parts - 1))
            return (0, first + turn)

        return pl.BlockSpec((rows, cols), index)

    return call(
        gather_kernel,
        (4, parts),
        [place],
        [(piece, part_of(number)) for number, piece in enumerate(pieces)],
        [
            (
                shape(dims, F32),
                pl.BlockSpec(
                    (rows, cols), lambda i, h, place: block_at(*piece_owner(i, place), h)
                ),
            )
        ],
        deps,
        "gather",
        20,
        6,
    )[0]


def gather_mixed_kernel(place, *refs):
    out = refs[-1]
    quarter = refs[0].shape[1]
    mine = pl.program_id(0) == place[1]
    for core in range(2):

        @pl.when(mine == (core == 0))
        def _(core=core):
            for other in range(2):
                b = place[2] if other == 0 else 1 - place[2]
                at = pl.multiple_of(b * quarter, quarter)
                out[:, pl.ds(at, quarter)] = refs[2 * core + other][...].astype(F32)


def gather_mixed(place, pieces, dims, first, half, earlier, deps):
    piece = pl.BlockSpec((TILE, TILE), lambda i, p, place: (0, first + p))
    return call(
        gather_mixed_kernel,
        (2, 3),
        [place],
        [(array, piece) for array in pieces],
        [
            (
                shape(dims, F32),
                pl.BlockSpec((TILE, 2 * TILE), lambda i, p, place: (i, 2 * p + half)),
            )
        ],
        earlier + deps,
        "gather_mixed",
        16,
        4,
        aliases={5: 0} if earlier else None,
    )[0]


def local(tokens, doc_ids, w_qkv, w_out, w_up, w_down, norm_gains, norm_biases, cotangent):
    narrow_size = lax.axis_size("narrow")
    packs, tok_rows, width = tokens.shape
    assert narrow_size == 2 and packs == 2 and tok_rows == 2 * TILE
    pack_len = tok_rows * narrow_size
    ff = w_up.shape[1]
    n = lax.axis_index("narrow")
    w = lax.axis_index("wide")
    core = w % 2
    side = (w // 2) % 2
    place = jnp.stack(
        [n, core, side, jnp.where(core == 0, n, side), jnp.where(core == 0, side, n)]
    ).astype(jnp.int32)
    pick = lambda array, index: lax.dynamic_index_in_dim(array, index, 0, keepdims=False)

    far_tok = swap_narrow(pick(tokens, 1 - n))
    doc_row = pick(doc_ids, n)
    many = (doc_row[pack_len - 1] != 0).astype(jnp.int32)
    block_at = jnp.stack([n, 3 - n, 1 - n, 2 + n]).astype(jnp.int32)
    info = jnp.concatenate([block_at, many[None]])

    halves = HEAD_DIM // 2
    frequency = jnp.exp(
        -math.log(10000.0) * jnp.arange(halves, dtype=F32) * 2.0 / HEAD_DIM
    )
    places = (block_at[:, None] * TILE + jnp.arange(TILE, dtype=jnp.int32)[None, :]).reshape(-1)
    angles_t = frequency[:, None] * places.astype(F32)[None, :]
    cos_t = jnp.cos(angles_t)
    sin_t = jnp.sin(angles_t)
    cos = cos_t.T
    sin = sin_t.T
    cosine = jnp.concatenate([cos] * 4, axis=1)
    sine = jnp.concatenate([-sin, sin, -sin, sin], axis=1)

    early = project(
        place, tokens, w_qkv, norm_gains, norm_biases, cosine, sine, 0, (), pack_len
    )
    far_cot = swap_narrow(tie(pick(cotangent, 1 - n), early[0]))
    normed, mixed = project(
        place, far_tok, w_qkv, norm_gains, norm_biases, cosine, sine, 2, early, pack_len
    )
    att, stats = attend(info, mixed)
    near_out, far_out, branch, normed2, active, back2, hidden_back, sums3 = feed(
        place, tokens, far_tok, cotangent, far_cot, att, w_out, w_up, w_down,
        norm_gains, norm_biases,
    )
    half_wide = width // 2
    down = Reduction(
        place,
        [(far_away(active), lambda x, c, b, h: (0, 4 * x + 2 * c + b),
          back2, lambda x, c, b, h: (0, 0), width)],
        2 * TILE, width, 1, 1.5,
    )
    up = Reduction(
        place,
        [(normed2, lambda x, c, b, h: (0, x),
          far_away(hidden_back), lambda x, c, b, h: (0, 2 * c + b), width)],
        2 * TILE, width, 1, 1.5,
    )
    last = down.far([])
    last = up.far([last])
    last = down.first([last])
    last = up.first([last])
    middle_back, branch_back, att_back, sums12 = return_pass(
        place, tokens, far_tok, cotangent, far_cot, branch, hidden_back, w_out, w_up,
        norm_gains, norm_biases, [last],
    )

    def back(half, deps):
        return attend_back(info, mixed, att, att_back, stats, cos_t, sin_t, half, deps)

    last = down.second([sums12])
    left_back = back(0, [last])
    by_rows = lambda x, c, b, h: (0, 2 * x + c)
    by_parts = lambda x, c, b, h: (0, 0, b)
    left = Reduction(
        place,
        [(far_away(att), by_rows, branch_back, lambda x, c, b, h: (0, b), half_wide),
         (normed, by_rows, far_away(left_back), by_parts, TILE)],
        TILE, 5 * TILE, 1, 1.2,
    )
    last = up.second([far_away(left_back)])
    last = down.keep([last])
    last = left.far([last])
    last = up.keep([last])
    got_out = swap_narrow(tie(far_out, last))
    right_back = back(1, [last])
    last = left.first([far_away(right_back), got_out])
    last = down.step(last)
    right = Reduction(
        place, [(normed, by_rows, far_away(right_back), by_parts, TILE)], TILE, 3 * TILE, 1, 0.8
    )
    last = right.far([last])
    last = up.step(last)
    near_grad, far_grad, sums0 = finish(
        place, tokens, far_tok, middle_back, left_back, right_back, w_qkv, norm_gains, [last]
    )
    last = left.second([sums0])
    last = right.first([last])
    extra = len(down.bits) - 2
    for _ in range(extra):
        last = down.step(last)
    last = down.step(last)
    down.open(last)
    last = left.keep([last])
    last = right.second([last])
    norm_term = jnp.concatenate(
        [sums0[0:1], sums12[0:1], sums12[2:3], sums3[0:1],
         sums0[1:2], sums12[1:2], sums12[3:4], sums3[1:2]], axis=0
    )
    hops = [2 ** bit for bit in range(lax.axis_size("wide").bit_length() - 1)]

    def norm_step(last):
        nonlocal norm_term, norm_got
        norm_term = norm_term + tie(norm_got, last)
        if hops:
            norm_got = swap_wide(norm_term, hops.pop(0))
        return norm_term

    norm_got = swap_narrow(tie(norm_term, last))
    for _ in range(extra):
        last = up.step(last)
    last = up.step(last)
    last = norm_step(last)
    last = right.keep([last])
    up.open(last)
    last = norm_step(last)
    for _ in range(extra):
        last = left.step(last)
        last = right.step(last)
    last = left.step(last)
    last = right.step(last)
    got_grad = swap_narrow(tie(far_grad, last))
    last = down.spread(last)
    grad_down = gather(
        place, down.pieces(), (ff // 2, width), half_wide, 0, 2,
        lambda c, b, h: (2 * c + b, h), [last],
    )
    last = norm_step(grad_down)
    out = lax.dynamic_update_slice(near_out, tie(got_out, last)[None], (1 - n, 0, 0))
    last = left.step(last)
    left.open(last)
    last = right.step(last)
    right.open(last)
    last = norm_step(last)
    last = up.spread(last)
    grad_up = gather(
        place, up.pieces(), (half_wide, ff), half_wide, 0, 2,
        lambda c, b, h: (0, 2 * (2 * c + b) + h), [last],
    )
    last = grad_up
    while hops:
        last = norm_step(last)
    last = norm_step(last)
    grad_tok = lax.dynamic_update_slice(near_grad, tie(got_grad, last)[None], (1 - n, 0, 0))
    last = left.spread(last)
    grad_out_proj = gather(
        place, left.pieces(), (half_wide, width), half_wide, 0, 1,
        lambda c, b, h: (c, b), [last],
    )
    grad_qkv = gather_mixed(
        place, left.pieces(), (half_wide, 3 * width), 2, 0, [], [last]
    )
    right.spread(grad_qkv)
    grad_qkv = gather_mixed(
        place, right.pieces(), (half_wide, 3 * width), 0, 1, [grad_qkv], []
    )
    norm_term = lax.dynamic_slice_in_dim(norm_term, n * half_wide, half_wide, 1)
    return (
        out,
        grad_tok,
        grad_qkv,
        grad_out_proj,
        grad_up,
        grad_down,
        norm_term[:4],
        norm_term[4:],
    )


def solution(mesh):
    rows = P("wide", "narrow", None)
    return jax.shard_map(
        local,
        mesh=mesh,
        in_specs=(rows, P("wide", None), P(), P(), P(), P(), P(), P(), rows),
        out_specs=(
            rows, rows,
            P("narrow", None), P("narrow", None), P("narrow", None), P("narrow", None),
            P(None, "narrow"), P(None, "narrow"),
        ),
        check_vma=False,
    )
```

```python
import functools
import math

import jax
import jax.numpy as jnp
from jax import lax
from jax.experimental import pallas as pl
from jax.experimental.pallas import tpu as pltpu
from jax.sharding import PartitionSpec as P

HEAD_DIM = 64
EPS = 1e-05
F32 = jnp.float32
BF16 = jnp.bfloat16
TILE = 256
GROUP = 256
FLOPS_PER_US = 1000000000
NN = (((1,), (0,)), ((), ()))
NT = (((1,), (1,)), ((), ()))
TN = (((0,), (0,)), ((), ()))


def dot(left, right, dims=NN):
    return lax.dot_general(left, right, dims, preferred_element_type=F32)


def call(kernel, grid, prefetch, inputs, outputs, deps, name, vmem, us, scratch=(), aliases=None):
    given = len(prefetch) + len(inputs)

    def body(*refs):
        kernel(*refs[:given], *refs[given + len(deps) :])

    in_specs = [spec for _, spec in inputs] + [pl.BlockSpec(memory_space=pl.ANY)] * len(deps)
    return pl.pallas_call(
        body,
        grid_spec=pltpu.PrefetchScalarGridSpec(
            num_scalar_prefetch=len(prefetch),
            grid=grid,
            in_specs=in_specs,
            out_specs=tuple(spec for _, spec in outputs),
            scratch_shapes=list(scratch),
        ),
        out_shape=tuple(shape for shape, _ in outputs),
        input_output_aliases=aliases or {},
        compiler_params=pltpu.CompilerParams(vmem_limit_bytes=vmem * 1024 * 1024),
        cost_estimate=pl.CostEstimate(
            flops=int(us * FLOPS_PER_US), transcendentals=0, bytes_accessed=1
        ),
        name=name,
    )(*prefetch, *[array for array, _ in inputs], *deps)


def shape(dims, dtype):
    return jax.ShapeDtypeStruct(dims, dtype)


def far_away(array):
    return pltpu.with_memory_space_constraint(array, pltpu.HBM)


def whole(dims):
    return pl.BlockSpec(dims, lambda *_: (0,) * len(dims), pipeline_mode=pl.Buffered(1))


def row_block(size):
    return pl.BlockSpec((TILE, size), lambda i, *_: (i, 0))


def own_rows(size):
    return pl.BlockSpec((1, TILE, size), lambda i, place, *_: (place[0], jnp.minimum(i, 1), 0))


def far_rows(size):
    return pl.BlockSpec((TILE, size), lambda i, *_: (jnp.maximum(i - 2, 0), 0))


def pick_rows(own, far):
    return jnp.where(pl.program_id(0) < 2, own[0].astype(F32), far[...].astype(F32))


def put_rows(near, far, rows):
    @pl.when(pl.program_id(0) < 2)
    def _():
        near[0] = rows

    @pl.when(pl.program_id(0) >= 2)
    def _():
        far[...] = rows


def tie(array, *deps):
    return lax.optimization_barrier((array,) + deps)[0]


def norm_parts(rows):
    centre = rows - jnp.mean(rows, axis=-1, keepdims=True)
    rstd = lax.rsqrt(jnp.mean(centre * centre, axis=-1, keepdims=True) + EPS)
    return centre * rstd, rstd


def norm_back(unit, rstd, gain, grad):
    scaled = grad * gain
    first = jnp.mean(scaled, axis=-1, keepdims=True)
    second = jnp.mean(scaled * unit, axis=-1, keepdims=True)
    return rstd * (scaled - first - unit * second)


def token_sum(rows):
    return jnp.sum(rows, axis=0, keepdims=True)


def project_kernel(place, tok, w, gains, biases, cosine, sine, normed_out, mixed_out):
    rows = tok[0] if len(tok.shape) == 3 else tok[...]
    unit, _ = norm_parts(rows.astype(F32))
    normed = (unit * gains[0:1, :] + biases[0:1, :]).astype(BF16)
    normed_out[...] = normed
    width = normed.shape[1]
    lanes = lax.broadcasted_iota(jnp.int32, (TILE, 128), 1)
    first_half = lanes % HEAD_DIM < HEAD_DIM // 2
    scale = 1.0 / math.sqrt(HEAD_DIM)
    cos = cosine[...]
    sin = sine[...]
    for start in range(0, 3 * width, 256):
        part = dot(normed, w[:, start : start + 256])
        if start >= 2 * width:
            mixed_out[:, start : start + 256] = part.astype(BF16)
            continue
        for sub in range(0, 256, 128):
            u = part[:, sub : sub + 128]
            turned = jnp.where(first_half, pltpu.roll(u, 96, 1), pltpu.roll(u, 32, 1))
            out = u * cos + turned * sin
            out = out.astype(BF16)
            if start < width:
                out = out * jnp.asarray(scale, BF16)
            mixed_out[:, start + sub : start + sub + 128] = out


def project(place, tok, w_qkv, gains, biases, cosine, sine, first_block, earlier, pack_len):
    width, wide = w_qkv.shape
    steps = tok.shape[-2] // TILE
    at = lambda size: pl.BlockSpec((TILE, size), lambda i, *_: (i + first_block, 0))
    own = tok.ndim == 3
    return call(
        project_kernel,
        (steps,),
        [place],
        [
            (tok, own_rows(width) if own else row_block(width)),
            (far_away(w_qkv), whole(w_qkv.shape)),
            (gains, whole(gains.shape)),
            (biases, whole(biases.shape)),
            (cosine, at(128)),
            (sine, at(128)),
        ],
        [
            (pltpu.HBM((pack_len, width), BF16), at(width)),
            (pltpu.HBM((pack_len, wide), BF16), at(wide)),
        ],
        [far_away(array) for array in earlier],
        "project",
        24,
        8,
        aliases={7: 0, 8: 1} if earlier else None,
    )


def diagonal_mask(scores):
    size = scores.shape[1]
    first = scores.shape[0] - size
    keys = lax.broadcasted_iota(jnp.int32, (size, size), 0)
    asks = lax.broadcasted_iota(jnp.int32, (size, size), 1)
    tail = jnp.where(keys <= asks, scores[first:], -1e30)
    if first == 0:
        return tail
    return jnp.concatenate([scores[:first], tail], axis=0)


def attend_kernel(info, q, k, v, out, stats, key_heads, q_t, v_t, out_t):
    heads = GROUP // HEAD_DIM
    blocks = q.shape[0] // TILE
    for i in range(blocks):
        rows = slice(i * TILE, (i + 1) * TILE)
        at = pl.multiple_of(info[i] * TILE, TILE)
        q_t[:, pl.ds(at, TILE)] = q[rows, :].T
        v_t[:, pl.ds(at, TILE)] = v[rows, :].T
        for h in range(heads):
            key_heads[h, pl.ds(at, TILE), :] = k[rows, h * HEAD_DIM : (h + 1) * HEAD_DIM]

    def one_head(h, first_key):
        head_rows = pl.ds(pl.multiple_of(h * HEAD_DIM, HEAD_DIM), HEAD_DIM)
        for block in range(blocks):
            cols = slice(block * TILE, (block + 1) * TILE)
            keys = slice(first_key(block), (block + 1) * TILE)
            scores = diagonal_mask(dot(key_heads[h, keys, :], q_t[head_rows, cols]))
            peak = jnp.max(scores, axis=0, keepdims=True)
            weights = jnp.exp(scores - peak)
            total = jnp.sum(weights, axis=0, keepdims=True)
            mixed = dot(v_t[head_rows, keys], weights.astype(BF16))
            out_t[head_rows, cols] = mixed * (1.0 / total)
            stats[0, pl.ds(h, 1), cols] = peak + jnp.log(total)

    many = info[blocks] != 0

    @pl.when(jnp.logical_not(many))
    def _():
        @pl.loop(0, heads, unroll=2)
        def _(h):
            one_head(h, lambda block: 0)

    @pl.when(many)
    def _():
        @pl.loop(0, heads, unroll=2)
        def _(h):
            one_head(h, lambda block: block * TILE)

    for i in range(blocks):
        at = pl.multiple_of(info[i] * TILE, TILE)
        out[i * TILE : (i + 1) * TILE, :] = out_t[:, pl.ds(at, TILE)].T.astype(BF16)


def attend(info, mixed):
    rows, wide = mixed.shape
    width = wide // 3
    groups = width // GROUP
    heads = GROUP // HEAD_DIM
    part = lambda shift: pl.BlockSpec((rows, GROUP), lambda g, s: (0, g + shift * groups))
    return call(
        attend_kernel,
        (groups,),
        [info],
        [(far_away(mixed), part(0)), (far_away(mixed), part(1)), (far_away(mixed), part(2))],
        [
            (pltpu.HBM((rows, width), BF16), part(0)),
            (
                shape((groups, heads, rows), F32),
                pl.BlockSpec((1, heads, rows), lambda g, s: (g, 0, 0)),
            ),
        ],
        [],
        "attend",
        24,
        36,
        scratch=[
            pltpu.VMEM((heads, rows, HEAD_DIM), BF16),
            pltpu.VMEM((GROUP, rows), BF16),
            pltpu.VMEM((GROUP, rows), BF16),
            pltpu.VMEM((GROUP, rows), F32),
        ],
    )


def feed_kernel(place, own_tok, far_tok, own_cot, far_cot, att, w_out, w_up, w_down, gains, biases,
                near_out, far_out, branch_out, normed2_out, active_out, back2_out, hidden_back_out, sums,
                slope):
    chunk = 512
    residual = pick_rows(own_tok, far_tok)
    branch = dot(att[...], w_out[...])
    branch_out[...] = branch
    unit1, _ = norm_parts(branch)
    middle = residual + unit1 * gains[1:2, :] + biases[1:2, :]
    unit2, _ = norm_parts(middle)
    normed2 = (unit2 * gains[2:3, :] + biases[2:3, :]).astype(BF16)
    normed2_out[...] = normed2
    ff = w_up.shape[1]
    root = math.sqrt(2.0 / math.pi)
    branch2 = jnp.zeros_like(branch)
    ahead = dot(normed2, w_up[:, :chunk])
    for start in range(0, ff, chunk):
        cols = slice(start, start + chunk)
        z = ahead
        if start + chunk < ff:
            ahead = dot(normed2, w_up[:, start + chunk : start + 2 * chunk])
        square = z * z
        bend = jnp.tanh(z * (root + (root * 0.044715) * square))
        half = 0.5 + 0.5 * bend
        active = (z * half).astype(BF16)
        active_out[:, cols] = active
        inner = (0.5 * root) + (1.5 * root * 0.044715) * square
        slope[:, cols] = half + z * (1.0 - bend * bend) * inner
        branch2 = branch2 + dot(active, w_down[cols, :])
    unit3, rstd3 = norm_parts(branch2)
    put_rows(near_out, far_out, (middle + unit3 * gains[3:4, :] + biases[3:4, :]).astype(BF16))
    upstream = pick_rows(own_cot, far_cot)
    back2 = norm_back(unit3, rstd3, gains[3:4, :], upstream).astype(BF16)
    back2_out[...] = back2

    @pl.when(pl.program_id(0) == 0)
    def _():
        sums[...] = jnp.zeros_like(sums)

    sums[0:1, :] += token_sum(upstream * unit3)
    sums[1:2, :] += token_sum(upstream)
    for start in range(0, ff, chunk):
        cols = slice(start, start + chunk)
        grad_active = dot(back2, w_down[cols, :], NT)
        hidden_back_out[:, cols] = (grad_active * slope[:, cols]).astype(BF16)


def feed(place, tokens, far_tok, cotangent, far_cot, att, w_out, w_up, w_down, gains, biases):
    rows, width = att.shape
    ff = w_up.shape[1]
    return call(
        feed_kernel,
        (rows // TILE,),
        [place],
        [
            (far_away(tokens), own_rows(width)), (far_tok, far_rows(width)),
            (far_away(cotangent), own_rows(width)), (far_cot, far_rows(width)),
            (far_away(att), row_block(width)),
            (w_out, whole(w_out.shape)), (w_up, whole(w_up.shape)), (w_down, whole(w_down.shape)),
            (gains, whole(gains.shape)), (biases, whole(biases.shape)),
        ],
        [
            (pltpu.HBM((2, rows // 2, width), BF16), own_rows(width)),
            (shape((rows // 2, width), BF16), far_rows(width)),
            (pltpu.HBM((rows, width), F32), row_block(width)),
            (shape((rows, width), BF16), row_block(width)),
            (pltpu.HBM((rows, ff), BF16), row_block(ff)),
            (shape((rows, width), BF16), row_block(width)),
            (pltpu.HBM((rows, ff), BF16), row_block(ff)),
            (shape((8, width), F32), whole((8, width))),
        ],
        [],
        "feed",
        52,
        49,
        scratch=[pltpu.VMEM((TILE, ff), F32)],
    )


def return_kernel(place, own_tok, far_tok, own_cot, far_cot, branch, hidden_back, w_out, w_up, gains, biases,
                  middle_back_out, branch_back_out, att_back_out, sums):
    unit1, rstd1 = norm_parts(branch[...])
    middle = pick_rows(own_tok, far_tok) + unit1 * gains[1:2, :] + biases[1:2, :]
    unit2, rstd2 = norm_parts(middle)
    grad2 = dot(hidden_back[...], w_up[...], NT)
    middle_back = pick_rows(own_cot, far_cot) + norm_back(unit2, rstd2, gains[2:3, :], grad2)
    middle_back_out[...] = middle_back
    branch_back = norm_back(unit1, rstd1, gains[1:2, :], middle_back).astype(BF16)
    branch_back_out[...] = branch_back
    att_back_out[...] = dot(branch_back, w_out[...], NT).astype(BF16)

    @pl.when(pl.program_id(0) == 0)
    def _():
        sums[...] = jnp.zeros_like(sums)

    sums[0:1, :] += token_sum(middle_back * unit1)
    sums[1:2, :] += token_sum(middle_back)
    sums[2:3, :] += token_sum(grad2 * unit2)
    sums[3:4, :] += token_sum(grad2)


def return_pass(place, tokens, far_tok, cotangent, far_cot, branch, hidden_back, w_out, w_up,
                gains, biases, deps):
    rows, width = branch.shape
    ff = w_up.shape[1]
    return call(
        return_kernel,
        (rows // TILE,),
        [place],
        [
            (far_away(tokens), own_rows(width)), (far_tok, far_rows(width)),
            (far_away(cotangent), own_rows(width)), (far_cot, far_rows(width)),
            (far_away(branch), row_block(width)), (far_away(hidden_back), row_block(ff)),
            (far_away(w_out), whole(w_out.shape)), (far_away(w_up), whole(w_up.shape)),
            (gains, whole(gains.shape)), (biases, whole(biases.shape)),
        ],
        [
            (pltpu.HBM((rows, width), F32), row_block(width)),
            (shape((rows, width), BF16), row_block(width)),
            (shape((rows, width), BF16), row_block(width)),
            (shape((8, width), F32), whole((8, width))),
        ],
        deps,
        "return_pass",
        32,
        24,
    )


def attend_back_kernel(info, q, k, v, att, grad, stats, cos_t, sin_t, back,
                       q_heads, k_heads, v_heads, g_heads, q_t, k_t, g_t, inner, q_acc, k_acc, v_acc):
    heads = GROUP // HEAD_DIM
    half = HEAD_DIM // 2
    blocks = q.shape[0] // TILE
    rows_all = blocks * TILE
    for i in range(blocks):
        rows = slice(i * TILE, (i + 1) * TILE)
        at = pl.multiple_of(info[i] * TILE, TILE)
        spot = pl.ds(at, TILE)
        q_t[:, spot] = q[rows, :].T
        k_t[:, spot] = k[rows, :].T
        grad_t = grad[rows, :].T
        g_t[:, spot] = grad_t
        product = att[rows, :].T.astype(F32) * grad_t.astype(F32)
        for h in range(heads):
            lanes = slice(h * HEAD_DIM, (h + 1) * HEAD_DIM)
            q_heads[h, spot, :] = q[rows, lanes]
            k_heads[h, spot, :] = k[rows, lanes]
            v_heads[h, spot, :] = v[rows, lanes]
            g_heads[h, spot, :] = grad[rows, lanes]
            inner[pl.ds(h, 1), spot] = jnp.sum(product[lanes, :], axis=0, keepdims=True)

    def one_head(h, last_ask):
        head_rows = pl.ds(pl.multiple_of(h * HEAD_DIM, HEAD_DIM), HEAD_DIM)
        for block in range(blocks):
            keys = slice(block * TILE, (block + 1) * TILE)
            cols = slice(block * TILE, last_ask(block))
            scores = dot(k_heads[h, keys, :], q_t[head_rows, cols])
            low = scores[:, :TILE]
            keys_at = lax.broadcasted_iota(jnp.int32, (TILE, TILE), 0)
            asks_at = lax.broadcasted_iota(jnp.int32, (TILE, TILE), 1)
            low = jnp.where(keys_at <= asks_at, low, -1e30)
            if scores.shape[1] > TILE:
                scores = jnp.concatenate([low, scores[:, TILE:]], axis=1)
            else:
                scores = low
            weights = jnp.exp(scores - stats[0, pl.ds(h, 1), cols])
            weight_back = dot(v_heads[h, keys, :], g_t[head_rows, cols])
            score_back = (weights * (weight_back - inner[pl.ds(h, 1), cols])).astype(BF16)
            v_acc[h, keys, :] = dot(weights.astype(BF16), g_heads[h, cols, :])
            k_acc[h, keys, :] = dot(score_back, q_heads[h, cols, :])
            change = dot(k_t[head_rows, keys], score_back)
            if block == 0:
                q_acc[head_rows, cols] = change
            elif last_ask(0) < rows_all:
                q_acc[head_rows, cols] = change
            else:
                q_acc[head_rows, cols] += change

    many = info[blocks] != 0

    @pl.when(jnp.logical_not(many))
    def _():
        @pl.loop(0, heads, unroll=2)
        def _(h):
            one_head(h, lambda block: rows_all)

    @pl.when(many)
    def _():
        @pl.loop(0, heads, unroll=2)
        def _(h):
            one_head(h, lambda block: (block + 1) * TILE)

    scale = 1.0 / math.sqrt(HEAD_DIM)
    for i in range(blocks):
        rows = slice(i * TILE, (i + 1) * TILE)
        spot = pl.ds(pl.multiple_of(info[i] * TILE, TILE), TILE)
        cos = cos_t[:, rows]
        sin = sin_t[:, rows]

        def turn_back(parts, factor):
            turned = []
            for part in parts:
                first, second = part[:half], part[half:]
                turned.append(first * cos + second * sin)
                turned.append(second * cos - first * sin)
            return (jnp.concatenate(turned, axis=0) * factor).T.astype(BF16)

        back[0, rows, :] = turn_back(
            [q_acc[h * HEAD_DIM : (h + 1) * HEAD_DIM, spot] for h in range(heads)], scale
        )
        back[1, rows, :] = turn_back([k_acc[h, spot, :].T for h in range(heads)], 1.0)
        back[2, rows, :] = jnp.concatenate(
            [v_acc[h, spot, :] for h in range(heads)], axis=1
        ).astype(BF16)


def attend_back(info, mixed, att, grad, stats, cos_t, sin_t, half, deps):
    rows, wide = mixed.shape
    width = wide // 3
    groups = width // GROUP
    heads = GROUP // HEAD_DIM
    first = half * (groups // 2)
    spec = lambda shift: pl.BlockSpec((rows, GROUP), lambda i, s: (0, i + first + shift * groups))
    per_head = pltpu.VMEM((heads, rows, HEAD_DIM), BF16)
    turned = pltpu.VMEM((GROUP, rows), BF16)
    angles = pl.BlockSpec((HEAD_DIM // 2, rows), lambda i, s: (0, 0))
    return call(
        attend_back_kernel,
        (groups // 2,),
        [info],
        [
            (far_away(mixed), spec(0)), (far_away(mixed), spec(1)), (far_away(mixed), spec(2)),
            (far_away(att), spec(0)), (far_away(grad), spec(0)),
            (stats, pl.BlockSpec((1, heads, rows), lambda i, s: (i + first, 0, 0))),
            (cos_t, angles), (sin_t, angles),
        ],
        [
            (
                pltpu.HBM((3, rows, 2 * GROUP), BF16),
                pl.BlockSpec((3, rows, GROUP), lambda i, s: (0, 0, i)),
            ),
        ],
        deps,
        "attend_back",
        32,
        24,
        scratch=[
            per_head, per_head, per_head, per_head,
            turned, turned, turned,
            pltpu.VMEM((8, rows), F32),
            pltpu.VMEM((GROUP, rows), F32),
            pltpu.VMEM((heads, rows, HEAD_DIM), F32),
            pltpu.VMEM((heads, rows, HEAD_DIM), F32),
        ],
    )[0]


def finish_kernel(place, own_tok, far_tok, middle_back, left_back, right_back, w_qkv, gains,
                  near_out, far_out, sums):
    half = left_back.shape[2]
    unit, rstd = norm_parts(pick_rows(own_tok, far_tok))
    grad = None
    for part in range(3):
        for side, back in enumerate((left_back, right_back)):
            start = (2 * part + side) * half
            term = dot(back[part], w_qkv[:, start : start + half], NT)
            grad = term if grad is None else grad + term
    back = middle_back[...] + norm_back(unit, rstd, gains[0:1, :], grad)
    put_rows(near_out, far_out, back.astype(BF16))

    @pl.when(pl.program_id(0) == 0)
    def _():
        sums[...] = jnp.zeros_like(sums)

    sums[0:1, :] += token_sum(grad * unit)
    sums[1:2, :] += token_sum(grad)


def finish(place, tokens, far_tok, middle_back, left_back, right_back, w_qkv, gains, deps):
    rows, width = middle_back.shape
    parts = pl.BlockSpec((3, TILE, width // 2), lambda i, *_: (0, i, 0))
    return call(
        finish_kernel,
        (rows // TILE,),
        [place],
        [
            (far_away(tokens), own_rows(width)), (far_tok, far_rows(width)),
            (far_away(middle_back), row_block(width)), (far_away(left_back), parts), (far_away(right_back), parts),
            (far_away(w_qkv), whole(w_qkv.shape)), (gains, whole(gains.shape)),
        ],
        [
            (pltpu.HBM((2, rows // 2, width), BF16), own_rows(width)),
            (shape((rows // 2, width), BF16), far_rows(width)),
            (shape((8, width), F32), whole((8, width))),
        ],
        deps,
        "finish",
        24,
        8,
    )


def weight_grad_kernel(source_count, out_count, place, *refs):
    outs = refs[-out_count:]
    addends = refs[2 * source_count : -out_count]
    share = pl.num_programs(0) // out_count
    start = 0
    for number in range(source_count):
        left, right = refs[2 * number], refs[2 * number + 1]
        rights = [right] if len(right.shape) == 2 else [right.at[p] for p in range(3)]
        turned = left[...].T
        for piece in rights:
            cols = slice(start, start + piece.shape[1])
            start = cols.stop
            total = dot(turned, piece[...])
            for addend in addends:
                total = total + addend[:, cols].astype(F32)
            total = total.astype(BF16)
            if out_count == 1:
                outs[0][:, cols] = total
                continue
            for turn, out in enumerate(outs):

                @pl.when(pl.program_id(0) // share == turn)
                def _(out=out, cols=cols, total=total):
                    out[:, cols] = total


def swap_wide(rows, bit):
    size = lax.axis_size("wide")
    return lax.ppermute(rows, "wide", [(i, i ^ bit) for i in range(size)])


def swap_narrow(rows):
    return lax.ppermute(rows, "narrow", [(0, 1), (1, 0)])


def swap_crossed(rows, first):
    pairs = []
    for i in range(lax.axis_size("wide")):
        for n in range(2):
            along_x = (i % 2 == 0) == first
            peer = (i, 1 - n) if along_x else (i ^ 2, n)
            pairs.append((2 * i + n, 2 * peer[0] + peer[1]))
    return lax.ppermute(rows, ("wide", "narrow"), pairs)


def swap_two(rows, even_bit, odd_bit):
    size = lax.axis_size("wide")
    return lax.ppermute(
        rows, "wide", [(i, i ^ (even_bit if i % 2 == 0 else odd_bit)) for i in range(size)]
    )


def pair_sum(mine, theirs):
    return (mine.astype(F32) + theirs.astype(F32)).astype(BF16)


def choose(which, bit):
    return jnp.where(which == 1, bit, 1 - bit)


class Reduction:
    def __init__(self, place, sources, rows, cols, halves, us):
        self.place, self.sources = place, sources
        self.rows, self.cols, self.halves, self.us = rows, cols, halves, us
        self.bits = []
        bit = 4
        while bit < lax.axis_size("wide"):
            self.bits.append(bit)
            bit *= 2

    def blocks(self, steps, core_of, pair_of, addends, deps, outs=1):
        tokens = self.sources[0][0].shape[0]

        def at(place_of):
            def index(i, h, place):
                core = core_of(place)
                first, second = pair_of(i, place)
                x = jnp.where(core == 0, first, second)
                b = jnp.where(core == 0, second, first)
                return place_of(x, core, b, h)

            return index

        inputs = []
        for left, left_of, right, right_of, width in self.sources:
            inputs.append((left, pl.BlockSpec((tokens, self.rows), at(left_of))))
            dims = (tokens, width) if right.ndim == 2 else (3, tokens, width)
            inputs.append((right, pl.BlockSpec(dims, at(right_of))))
        block = (self.rows, self.cols // self.halves)
        share = steps // outs
        for array, row in addends:
            inputs.append((array, pl.BlockSpec(block, lambda i, h, place, row=row: (row(i), h))))
        return call(
            functools.partial(weight_grad_kernel, len(self.sources), outs),
            (steps, self.halves),
            [self.place],
            inputs,
            [
                (
                    shape((share * self.rows, self.cols), BF16),
                    pl.BlockSpec(
                        block, lambda i, h, place, at=turn * share: (jnp.clip(i - at, 0, share - 1), h)
                    ),
                )
                for turn in range(outs)
            ],
            deps,
            "weight_grad",
            24,
            0.15 + 0.1 * self.us * steps,
        )

    def far(self, deps):
        pair_of = lambda i, place: (choose(i // 2, place[4]), choose(i % 2, place[3]))
        sent = self.blocks(4, lambda place: 1 - place[1], pair_of, [], deps, outs=2)
        self.core = [swap_wide(part, 1) for part in sent]
        return sent[0]

    def first(self, deps):
        pair_of = lambda i, place: (1 - place[3], choose(i, place[4]))
        sent = self.blocks(
            2, lambda place: place[1], pair_of, [(self.core[0], lambda i: i)], deps + self.core[1:]
        )[0]
        self.near = swap_crossed(sent, True)
        return sent

    def second(self, deps):
        pair_of = lambda i, place: (place[3], 1 - place[4])
        addends = [(self.core[1], lambda i: 0), (self.near, lambda i: 0)]
        sent = self.blocks(1, lambda place: place[1], pair_of, addends, deps)[0]
        self.side = swap_crossed(sent, False)
        return sent

    def keep(self, deps):
        pair_of = lambda i, place: (place[3], place[4])
        addends = [(self.core[1], lambda i: 1), (self.near, lambda i: 1), (self.side, lambda i: 0)]
        self.total = self.blocks(1, lambda place: place[1], pair_of, addends, deps)[0]
        self.hop = 0
        self.send()
        return self.total

    def send(self):
        self.got = swap_two(self.total, self.bits[self.hop], self.bits[-1 - self.hop])
        self.hop += 1

    def step(self, dep):
        self.total = pair_sum(self.total, tie(self.got, dep))
        if self.hop < len(self.bits):
            self.send()
        else:
            self.from_core = swap_wide(self.total, 1)
        return self.total

    def open(self, dep):
        self.from_y = swap_wide(tie(self.total, dep), 2)

    def spread(self, dep):
        self.from_y = tie(self.from_y, dep)
        self.from_both = swap_wide(self.from_y, 1)
        return self.from_y

    def pieces(self):
        return [self.total, self.from_y, self.from_core, self.from_both]


def gather_kernel(place, *refs):
    out = refs[-1]
    for number, piece in enumerate(refs[:4]):

        @pl.when(pl.program_id(0) == number)
        def _(piece=piece):
            out[...] = piece[...].astype(F32)


def piece_owner(number, place):
    c = jnp.where(number < 2, place[1], 1 - place[1])
    b = jnp.where(number % 2 == 0, place[2], 1 - place[2])
    return c, b


def gather(place, pieces, dims, cols, first, parts, block_at, deps):
    rows = pieces[0].shape[0]

    def part_of(number):
        def index(i, h, place):
            turn = jnp.where(i == number, h, jnp.where(i < number, 0, parts - 1))
            return (0, first + turn)

        return pl.BlockSpec((rows, cols), index)

    return call(
        gather_kernel,
        (4, parts),
        [place],
        [(piece, part_of(number)) for number, piece in enumerate(pieces)],
        [
            (
                shape(dims, F32),
                pl.BlockSpec(
                    (rows, cols), lambda i, h, place: block_at(*piece_owner(i, place), h)
                ),
            )
        ],
        deps,
        "gather",
        20,
        6,
    )[0]


def gather_mixed_kernel(place, *refs):
    out = refs[-1]
    quarter = refs[0].shape[1]
    mine = pl.program_id(0) == place[1]
    for core in range(2):

        @pl.when(mine == (core == 0))
        def _(core=core):
            for other in range(2):
                b = place[2] if other == 0 else 1 - place[2]
                at = pl.multiple_of(b * quarter, quarter)
                out[:, pl.ds(at, quarter)] = refs[2 * core + other][...].astype(F32)


def gather_mixed(place, pieces, dims, first, half, earlier, deps):
    piece = pl.BlockSpec((TILE, TILE), lambda i, p, place: (0, first + p))
    return call(
        gather_mixed_kernel,
        (2, 3),
        [place],
        [(array, piece) for array in pieces],
        [
            (
                shape(dims, F32),
                pl.BlockSpec((TILE, 2 * TILE), lambda i, p, place: (i, 2 * p + half)),
            )
        ],
        earlier + deps,
        "gather_mixed",
        16,
        4,
        aliases={5: 0} if earlier else None,
    )[0]


def local(tokens, doc_ids, w_qkv, w_out, w_up, w_down, norm_gains, norm_biases, cotangent):
    narrow_size = lax.axis_size("narrow")
    packs, tok_rows, width = tokens.shape
    assert narrow_size == 2 and packs == 2 and tok_rows == 2 * TILE
    pack_len = tok_rows * narrow_size
    ff = w_up.shape[1]
    n = lax.axis_index("narrow")
    w = lax.axis_index("wide")
    core = w % 2
    side = (w // 2) % 2
    place = jnp.stack(
        [n, core, side, jnp.where(core == 0, n, side), jnp.where(core == 0, side, n)]
    ).astype(jnp.int32)
    pick = lambda array, index: lax.dynamic_index_in_dim(array, index, 0, keepdims=False)

    far_tok = swap_narrow(pick(tokens, 1 - n))
    doc_row = pick(doc_ids, n)
    many = (doc_row[pack_len - 1] != 0).astype(jnp.int32)
    block_at = jnp.stack([n, 3 - n, 1 - n, 2 + n]).astype(jnp.int32)
    info = jnp.concatenate([block_at, many[None]])

    halves = HEAD_DIM // 2
    frequency = jnp.exp(
        -math.log(10000.0) * jnp.arange(halves, dtype=F32) * 2.0 / HEAD_DIM
    )
    places = (block_at[:, None] * TILE + jnp.arange(TILE, dtype=jnp.int32)[None, :]).reshape(-1)
    angles_t = frequency[:, None] * places.astype(F32)[None, :]
    cos_t = jnp.cos(angles_t)
    sin_t = jnp.sin(angles_t)
    cos = cos_t.T
    sin = sin_t.T
    cosine = jnp.concatenate([cos] * 4, axis=1)
    sine = jnp.concatenate([-sin, sin, -sin, sin], axis=1)

    early = project(
        place, tokens, w_qkv, norm_gains, norm_biases, cosine, sine, 0, (), pack_len
    )
    far_cot = swap_narrow(tie(pick(cotangent, 1 - n), early[0]))
    normed, mixed = project(
        place, far_tok, w_qkv, norm_gains, norm_biases, cosine, sine, 2, early, pack_len
    )
    att, stats = attend(info, mixed)
    near_out, far_out, branch, normed2, active, back2, hidden_back, sums3 = feed(
        place, tokens, far_tok, cotangent, far_cot, att, w_out, w_up, w_down,
        norm_gains, norm_biases,
    )
    half_wide = width // 2
    down = Reduction(
        place,
        [(far_away(active), lambda x, c, b, h: (0, 4 * x + 2 * c + b),
          back2, lambda x, c, b, h: (0, 0), width)],
        2 * TILE, width, 1, 1.5,
    )
    up = Reduction(
        place,
        [(normed2, lambda x, c, b, h: (0, x),
          far_away(hidden_back), lambda x, c, b, h: (0, 2 * c + b), width)],
        2 * TILE, width, 1, 1.5,
    )
    last = down.far([])
    last = up.far([last])
    last = down.first([last])
    last = up.first([last])
    middle_back, branch_back, att_back, sums12 = return_pass(
        place, tokens, far_tok, cotangent, far_cot, branch, hidden_back, w_out, w_up,
        norm_gains, norm_biases, [last],
    )

    def back(half, deps):
        return attend_back(info, mixed, att, att_back, stats, cos_t, sin_t, half, deps)

    last = down.second([sums12])
    left_back = back(0, [last])
    by_rows = lambda x, c, b, h: (0, 2 * x + c)
    by_parts = lambda x, c, b, h: (0, 0, b)
    left = Reduction(
        place,
        [(far_away(att), by_rows, branch_back, lambda x, c, b, h: (0, b), half_wide),
         (normed, by_rows, far_away(left_back), by_parts, TILE)],
        TILE, 5 * TILE, 1, 1.2,
    )
    last = up.second([far_away(left_back)])
    last = down.keep([last])
    last = left.far([last])
    last = up.keep([last])
    got_out = swap_narrow(tie(far_out, last))
    right_back = back(1, [last])
    last = left.first([far_away(right_back), got_out])
    last = down.step(last)
    right = Reduction(
        place, [(normed, by_rows, far_away(right_back), by_parts, TILE)], TILE, 3 * TILE, 1, 0.8
    )
    last = right.far([last])
    last = up.step(last)
    near_grad, far_grad, sums0 = finish(
        place, tokens, far_tok, middle_back, left_back, right_back, w_qkv, norm_gains, [last]
    )
    last = left.second([sums0])
    last = right.first([last])
    extra = len(down.bits) - 2
    for _ in range(extra):
        last = down.step(last)
    last = down.step(last)
    down.open(last)
    last = left.keep([last])
    last = right.second([last])
    norm_term = jnp.concatenate(
        [sums0[0:1], sums12[0:1], sums12[2:3], sums3[0:1],
         sums0[1:2], sums12[1:2], sums12[3:4], sums3[1:2]], axis=0
    )
    hops = [2 ** bit for bit in range(lax.axis_size("wide").bit_length() - 1)]

    def norm_step(last):
        nonlocal norm_term, norm_got
        norm_term = norm_term + tie(norm_got, last)
        if hops:
            norm_got = swap_wide(norm_term, hops.pop(0))
        return norm_term

    norm_got = swap_narrow(tie(norm_term, last))
    for _ in range(extra):
        last = up.step(last)
    last = up.step(last)
    last = norm_step(last)
    last = right.keep([last])
    got_grad = swap_narrow(tie(far_grad, last))
    up.open(last)
    last = norm_step(last)
    for _ in range(extra):
        last = left.step(last)
        last = right.step(last)
    last = left.step(last)
    last = right.step(last)
    last = down.spread(last)
    grad_down = gather(
        place, down.pieces(), (ff // 2, width), half_wide, 0, 2,
        lambda c, b, h: (2 * c + b, h), [last],
    )
    grad_tok = lax.dynamic_update_slice(near_grad, tie(got_grad, grad_down)[None], (1 - n, 0, 0))
    last = norm_step(grad_down)
    out = lax.dynamic_update_slice(near_out, tie(got_out, last)[None], (1 - n, 0, 0))
    last = left.step(last)
    left.open(last)
    last = right.step(last)
    right.open(last)
    last = norm_step(last)
    last = up.spread(last)
    grad_up = gather(
        place, up.pieces(), (half_wide, ff), half_wide, 0, 2,
        lambda c, b, h: (0, 2 * (2 * c + b) + h), [last],
    )
    last = grad_up
    while hops:
        last = norm_step(last)
    last = norm_step(last)
    last = left.spread(last)
    grad_out_proj = gather(
        place, left.pieces(), (half_wide, width), half_wide, 0, 1,
        lambda c, b, h: (c, b), [last],
    )
    grad_qkv = gather_mixed(
        place, left.pieces(), (half_wide, 3 * width), 2, 0, [], [last]
    )
    right.spread(grad_qkv)
    grad_qkv = gather_mixed(
        place, right.pieces(), (half_wide, 3 * width), 0, 1, [grad_qkv], []
    )
    norm_term = lax.dynamic_slice_in_dim(norm_term, n * half_wide, half_wide, 1)
    return (
        out,
        grad_tok,
        grad_qkv,
        grad_out_proj,
        grad_up,
        grad_down,
        norm_term[:4],
        norm_term[4:],
    )


def solution(mesh):
    rows = P("wide", "narrow", None)
    return jax.shard_map(
        local,
        mesh=mesh,
        in_specs=(rows, P("wide", None), P(), P(), P(), P(), P(), P(), rows),
        out_specs=(
            rows, rows,
            P("narrow", None), P("narrow", None), P("narrow", None), P("narrow", None),
            P(None, "narrow"), P(None, "narrow"),
        ),
        check_vma=False,
    )
```
